128 devices in a mesh: req: 16 (over y, x), seq: 4 (over z), hid: 2 (over core).
Axes of the slice: x: 4, y: 4, z: 4, core: 2. Of those that a mesh axis runs over, the one named last changes fastest.
Arguments:
- tokens: bfloat16 [65536, 2048], P(('req', 'seq')), may hold values from -6 to 6
- attention_gain: bfloat16 [2048], replicated, may hold values from 0.099609375 to 1.8984375
- project_weight: bfloat16 [2048, 2048], P(None, 'hid'), may hold values from -0.125 to 0.125
- conv_weight: bfloat16 [4, 2048], P(None, 'hid'), may hold values from -3 to 3
- decay_down: bfloat16 [2048, 16], replicated, may hold values from -0.125 to 0.125
- decay_up: bfloat16 [16, 512], P(None, 'hid'), may hold values from -1.5 to 1.5
- decay_bias: float32 [512], P('hid'), may hold values from -2 to 10
- output_gate: bfloat16 [2048, 1024], P(None, 'hid'), may hold values from -0.125 to 0.125
- head_gain: bfloat16 [512], replicated, may hold values from 0.099609375 to 1.8984375
- output_weight: bfloat16 [1024, 2048], P('hid'), may hold values from -0.1875 to 0.1875
- mixer_gain: bfloat16 [2048], replicated, may hold values from 0.099609375 to 1.8984375
- gate_weight: bfloat16 [2048, 2816], P('req', 'hid'), may hold values from -0.125 to 0.125
- up_weight: bfloat16 [2048, 2816], P('req', 'hid'), may hold values from -0.125 to 0.125
- down_weight: bfloat16 [2816, 2048], P('hid', 'req'), may hold values from -0.109375 to 0.109375
- prompt_pages: int32 [16, 16], P('req'), may hold values from 0 to 64, as said below
- prompt_start: int32 [16, 16], P('req'), may hold values from 0 to 63, as said below
Outputs:
- hidden_out: bfloat16 [65536, 2048], P(('req', 'seq', 'hid'))
- page_states: bfloat16 [1024, 2, 256, 512], P(('req', 'seq'), 'hid')
- conv_edges: bfloat16 [1024, 3, 2048], P(('req', 'seq'), None, 'hid')
The draws below stay inside these ranges and needn't reach their ends.
Inputs may be any that keep to these rules, and one draw needn't show every extreme that they name: `prompt_pages`: row r lists the page counts of the prompts of group r; 0 marks an unused slot; in every draw some group holds one prompt of all its 64 pages. `prompt_start`: the slots of a row that are used cover pages in increasing order without intersection and end by page 64; pages between prompts belong to none; an unused slot starts at page 64 - 1, and every draw has one.
All inputs are finite; a program needn't handle non-finite values.
Results may differ from the reference program's by a relative error of at most 0.014.
Values may be sent and summed in bfloat16 or wider, within the bound.
A program may use at most 192 MiB of HBM per device.

```python
import jax
import jax.numpy as jnp
from jax import lax

D = 2048
HEADS = 2
HK = 256
HV = 512
RANK = 16
FF = 2816
KCONV = 4
PAGE = 64
GROUP = 4096
TOKENS = 65536
PAGES_G = 64
PAGES = 1024
REQ_G = 16
CONVW = 1024
N_REQ = 16
N_HID = 2


def draw_decay_bias(key, part):
    pick_key, slow_key, fast_key = jax.random.split(key, 3)
    channel_count = HEADS * HK
    slow_share = 0.5
    slow_mask = jax.random.uniform(pick_key, (channel_count,)) < slow_share
    slow_rate = jax.random.uniform(slow_key, (channel_count,), minval=0.1, maxval=1.5) / GROUP
    fast_rate = 1.0 / jax.random.uniform(fast_key, (channel_count,), minval=10.0, maxval=60.0)
    step_rate = jnp.where(slow_mask, slow_rate, fast_rate)
    retained = jnp.exp(-16.0 * step_rate)
    return (jnp.log(retained) - jnp.log1p(-retained)).astype(jnp.float32)


def prompt_layout(key):
    folded = jax.random.fold_in(key, 11)
    order_key, length_key, gap_key = jax.random.split(folded, 3)
    group_count = TOKENS // GROUP
    ranking = jax.random.permutation(order_key, group_count)
    long_rows = (ranking < 2)[:, None]
    lengths = jax.random.randint(length_key, (group_count, REQ_G), 1, 4)
    gap_pages = jax.random.randint(gap_key, (group_count, REQ_G), 0, 2)
    starts = jnp.cumsum(lengths + gap_pages, axis=1) - lengths
    slot_index = jnp.arange(REQ_G)[None, :]
    long_lengths = jnp.where(slot_index == 0, PAGES_G, 0)
    long_starts = jnp.where(slot_index == 0, 0, PAGES_G - 1)
    page_counts = jnp.where(long_rows, long_lengths, lengths).astype(jnp.int32)
    begins = jnp.where(long_rows, long_starts, starts).astype(jnp.int32)
    return (page_counts, begins)


def draw_prompt_pages(key, part):
    return prompt_layout(key)[0]


def draw_prompt_start(key, part):
    return prompt_layout(key)[1]


def block_levels(own_key, shape, cuts, smallest, top_value):
    factor_of, own = 1.0, jax.random.fold_in(own_key, 6)
    for dim, shards_of in cuts:
        draws = jnp.exp(jax.random.uniform(jax.random.fold_in(own, dim), (shards_of,), jnp.float32, smallest / len(cuts), top_value / len(cuts)))
        factor_of = factor_of * jnp.repeat(draws, shape[dim] // shards_of).reshape([-1 if axis == dim else 1 for axis in range(len(shape))])
    return factor_of


def noise(key, shape, deviation, reach, shards=(), kind=jnp.bfloat16):
    factor_of = block_levels(key, shape, shards, -0.22, 0.18) if shards else 1.0
    values = jax.random.normal(key, shape, jnp.float32) * deviation * factor_of
    return jnp.minimum(jnp.maximum(values, -reach), reach).astype(kind)


def setup_inputs(seed: int = 0) -> dict:
    seeds = jax.random.split(jax.random.key(seed), 17)
    tokens = noise(seeds[0], (TOKENS, D), 1.0, 6.0, ((0, 64),))
    attention_gain = jnp.clip(1.0 + 0.18 * jax.random.normal(seeds[1], (D,), jnp.float32), 0.099609375, 1.8984375).astype(jnp.bfloat16)
    project_weight = noise(seeds[2], (D, HEADS * CONVW), D ** -0.5, 0.125, ((1, 2),))
    conv_weight = noise(seeds[3], (KCONV, HEADS * CONVW), KCONV ** -0.5, 3.0, ((1, 2),))
    decay_down = noise(seeds[4], (D, RANK), D ** -0.5, 0.125)
    decay_up = noise(seeds[5], (RANK, HEADS * HK), RANK ** -0.5, 1.5, ((1, 2),))
    decay_bias = draw_decay_bias(jax.random.fold_in(seeds[16], 71), 0)
    output_gate = noise(seeds[7], (D, HEADS * HV), D ** -0.5, 0.125, ((1, 2),))
    head_gain = jnp.clip(1.0 + 0.18 * jax.random.normal(seeds[8], (HV,), jnp.float32), 0.099609375, 1.8984375).astype(jnp.bfloat16)
    output_weight = noise(seeds[9], (HEADS * HV, D), (HEADS * HV) ** -0.5, 0.1875, ((0, 2),))
    mixer_gain = jnp.clip(1.0 + 0.18 * jax.random.normal(seeds[10], (D,), jnp.float32), 0.099609375, 1.8984375).astype(jnp.bfloat16)
    gate_weight = noise(seeds[11], (D, FF), D ** -0.5, 0.125, ((0, 16), (1, 2)))
    up_weight = noise(seeds[12], (D, FF), D ** -0.5, 0.125, ((0, 16), (1, 2)))
    down_weight = noise(seeds[13], (FF, D), FF ** -0.5, 0.109375, ((0, 2), (1, 16)))
    prompt_pages = draw_prompt_pages(jax.random.fold_in(seeds[16], 71), 0)
    prompt_start = draw_prompt_start(jax.random.fold_in(seeds[16], 71), 0)
    return {"tokens": tokens, "attention_gain": attention_gain, "project_weight": project_weight, "conv_weight": conv_weight, "decay_down": decay_down, "decay_up": decay_up, "decay_bias": decay_bias, "output_gate": output_gate, "head_gain": head_gain, "output_weight": output_weight, "mixer_gain": mixer_gain, "gate_weight": gate_weight, "up_weight": up_weight, "down_weight": down_weight, "prompt_pages": prompt_pages, "prompt_start": prompt_start}


EPSILON = 1e-06
TOP_PRECISION = lax.Precision.HIGHEST

def rms_scaled(values, scale_gain):
    values = values.astype(jnp.float32)
    return values * lax.rsqrt(lax.optimization_barrier(jnp.mean(values * values, axis=-1, keepdims=True)) + EPSILON) * scale_gain.astype(jnp.float32)

def round_trip(values):
    return lax.optimization_barrier(values.astype(jnp.bfloat16)).astype(jnp.float32)

def page_segments(page_counts, starts, total_pages):
    position = jnp.arange(total_pages, dtype=jnp.int32)
    inside = (position[None, :] >= starts[:, None]) & (position[None, :] < starts[:, None] + page_counts[:, None])
    labels = jnp.arange(1, page_counts.shape[0] + 1, dtype=jnp.int32)
    segment = lax.optimization_barrier(jnp.sum(jnp.where(inside, labels[:, None], 0), axis=0)).astype(jnp.int32) - 1
    earlier = jnp.concatenate([jnp.full((1,), -1, jnp.int32), segment[:-1]])
    return ((segment == earlier) & (segment >= 0)).astype(jnp.float32)

def short_conv(by_page, before, carried, conv_taps):
    kept_rows = before.astype(jnp.float32) * carried[:, None, None]
    widened = jnp.concatenate([kept_rows, by_page.astype(jnp.float32)], axis=1)
    tap_count = conv_taps.shape[0]
    length = by_page.shape[1]
    result = jnp.zeros(by_page.shape, jnp.float32)
    for offset in range(tap_count):
        result = result + conv_taps[offset].astype(jnp.float32) * widened[:, tap_count - 1 - offset:tap_count - 1 - offset + length]
    return result

def split_features(mixed_rows, key_width):
    query_rows = jax.nn.silu(mixed_rows[..., :key_width])
    key_rows = jax.nn.silu(mixed_rows[..., key_width:2 * key_width]) * key_width ** (-0.5)
    value_matrix = mixed_rows[..., 2 * key_width:]
    return (query_rows.transpose(0, 2, 1, 3), key_rows.transpose(0, 2, 1, 3), value_matrix.transpose(0, 2, 1, 3))

def page_step(memory_state, inputs):
    query_rows, key_rows, value_matrix, decay_sum, carried = inputs
    memory_state = memory_state * carried
    length = query_rows.shape[1]
    raised_rows = query_rows * jnp.exp(decay_sum)
    lowered = key_rows * jnp.exp(-decay_sum)
    scores = jnp.einsum('hik,hjk->hij', raised_rows, lowered, precision=TOP_PRECISION)
    rows_index = jnp.arange(length)
    causal = rows_index[:, None] >= rows_index[None, :]
    scores = jnp.where(causal[None], scores, 0.0)
    layer_output = jnp.einsum('hij,hjv->hiv', scores, value_matrix, precision=TOP_PRECISION)
    layer_output = layer_output + jnp.einsum('eow,ews->eos', raised_rows, memory_state, precision=TOP_PRECISION)
    closing_sum = decay_sum[:, -1:, :]
    weighted_rows = key_rows * jnp.exp(closing_sum - decay_sum)
    memory_state = jnp.exp(closing_sum[:, 0, :])[:, :, None] * memory_state + jnp.einsum('lte,ltb->leb', weighted_rows, value_matrix, precision=TOP_PRECISION)
    return (memory_state, (layer_output, memory_state))

def reference(tokens, attention_gain, project_weight, conv_weight, decay_down, decay_up, decay_bias, output_gate, head_gain, output_weight, mixer_gain, gate_weight, up_weight, down_weight, prompt_pages, prompt_start):
    page_total = GROUP // PAGE
    rim_rows = KCONV - 1

    def one_group(packed):
        group_rows, page_counts, starts = packed
        normed = rms_scaled(group_rows, attention_gain).astype(jnp.bfloat16)
        projected = jnp.dot(normed, project_weight, preferred_element_type=jnp.float32).astype(jnp.bfloat16)
        by_page = projected.reshape(page_total, PAGE, HEADS * CONVW)
        before = jnp.concatenate([jnp.zeros((1, rim_rows, HEADS * CONVW), jnp.bfloat16), by_page[:-1, PAGE - rim_rows:]], axis=0)
        carried = page_segments(page_counts, starts, page_total)
        mixed_rows = short_conv(by_page, before, carried, conv_weight).reshape(page_total, PAGE, HEADS, CONVW)
        query_rows, key_rows, value_matrix = split_features(mixed_rows, HK)
        lowrank = jnp.dot(normed, decay_down, preferred_element_type=jnp.float32).astype(jnp.bfloat16)
        decay_log = jax.nn.log_sigmoid(jnp.dot(lowrank, decay_up, preferred_element_type=jnp.float32) + decay_bias) / 16.0
        decay_log = decay_log.reshape(page_total, PAGE, HEADS, HK).transpose(0, 2, 1, 3)
        decay_sum = jnp.cumsum(decay_log, axis=2)
        start_memory = jnp.zeros((HEADS, HK, HV), jnp.float32)
        final_memory, (outputs, memories) = lax.scan(page_step, start_memory, (query_rows, key_rows, value_matrix, decay_sum, carried))
        attended = outputs.transpose(0, 2, 1, 3).reshape(GROUP, HEADS, HV)
        normed_heads = rms_scaled(attended, head_gain)
        opening = jax.nn.silu(jnp.dot(normed, output_gate, preferred_element_type=jnp.float32)).reshape(GROUP, HEADS, HV)
        gated_rows = (normed_heads * opening).astype(jnp.bfloat16).reshape(GROUP, HEADS * HV)
        mixed_sum = jnp.zeros((GROUP, D), jnp.float32)
        for head_index in range(HEADS):
            lower = head_index * HV
            mixed_sum = mixed_sum + round_trip(jnp.dot(gated_rows[:, lower:lower + HV], output_weight[lower:lower + HV], preferred_element_type=jnp.float32))
        residual = (group_rows.astype(jnp.float32) + mixed_sum).astype(jnp.bfloat16)
        feed_in = rms_scaled(residual, mixer_gain).astype(jnp.bfloat16)
        gate_part = jnp.dot(feed_in, gate_weight, preferred_element_type=jnp.float32)
        up_part = jnp.dot(feed_in, up_weight, preferred_element_type=jnp.float32)
        hidden = (jax.nn.silu(gate_part) * up_part).astype(jnp.bfloat16)
        block_width = FF // N_HID
        feed_sum = jnp.zeros((GROUP, D), jnp.float32)
        for part_index in range(N_HID):
            lower = part_index * block_width
            feed_sum = feed_sum + round_trip(jnp.dot(hidden[:, lower:lower + block_width], down_weight[lower:lower + block_width], preferred_element_type=jnp.float32))
        result = (residual.astype(jnp.float32) + feed_sum).astype(jnp.bfloat16)
        return (result, memories.astype(jnp.bfloat16), by_page[:, PAGE - rim_rows:])
    results, memories, conv_edges = lax.map(one_group, (tokens.reshape(N_REQ, GROUP, D), prompt_pages, prompt_start))
    return (results.reshape(TOKENS, D), memories.reshape(PAGES, HEADS, HK, HV), conv_edges.reshape(PAGES, KCONV - 1, HEADS * CONVW))
```

```python
import jax
import jax.numpy as jnp
from jax import lax
from jax.sharding import PartitionSpec as P

HK = 256
HV = 512
KCONV = 4
PAGE = 64
CONVW = 1024


EPSILON = 1e-06
TOP_PRECISION = lax.Precision.HIGHEST


def shifted(value, axis, steps):
    count = lax.axis_size(axis)
    first, last = (max(0, -steps), min(count, count - steps))
    return lax.ppermute(value, axis, [(source, source + steps) for source in range(first, last)])


def prefix_2(array, axis, join, neutral):
    place = lax.axis_index(axis)
    gathered = jax.tree.map(
        lambda a, kind: lax.all_gather(a.astype(kind), axis), array, (jnp.bfloat16, jnp.bfloat16)
    )
    state = jax.tree.map(lambda a, e: jnp.zeros_like(a) + jnp.asarray(e, a.dtype), array, neutral)

    def one(lap, state):
        return join(
            state,
            jax.tree.map(
                lambda a, own: lax.dynamic_index_in_dim(a, lap, 0, False).astype(own.dtype),
                gathered,
                array,
            ),
        )

    return lax.fori_loop(0, place, one, state)


def rms_scaled(values, scale_gain):
    values = values.astype(jnp.float32)
    return (
        values
        * lax.rsqrt(jnp.mean(values * values, axis=-1, keepdims=True) + EPSILON)
        * scale_gain.astype(jnp.float32)
    )


def page_segments(page_counts, starts, total_pages):
    position = jnp.arange(total_pages, dtype=jnp.int32)
    inside = (position[None, :] >= starts[:, None]) & (
        position[None, :] < starts[:, None] + page_counts[:, None]
    )
    labels = jnp.arange(1, page_counts.shape[0] + 1, dtype=jnp.int32)
    segment = jnp.sum(jnp.where(inside, labels[:, None], 0), axis=0) - 1
    earlier = jnp.concatenate([jnp.full((1,), -1, jnp.int32), segment[:-1]])
    return ((segment == earlier) & (segment >= 0)).astype(jnp.float32)


def short_conv(by_page, before, carried, conv_taps):
    kept_rows = before.astype(jnp.float32) * carried[:, None, None]
    widened = jnp.concatenate([kept_rows, by_page.astype(jnp.float32)], axis=1)
    tap_count = conv_taps.shape[0]
    length = by_page.shape[1]
    result = jnp.zeros(by_page.shape, jnp.float32)
    for offset in range(tap_count):
        result = (
            result
            + conv_taps[offset].astype(jnp.float32)
            * widened[:, tap_count - 1 - offset : tap_count - 1 - offset + length]
        )
    return result


def split_features(mixed_rows, key_width):
    query_rows = jax.nn.silu(mixed_rows[..., :key_width])
    key_rows = jax.nn.silu(mixed_rows[..., key_width : 2 * key_width]) * key_width ** (-0.5)
    value_matrix = mixed_rows[..., 2 * key_width :]
    return (
        query_rows.transpose(0, 2, 1, 3),
        key_rows.transpose(0, 2, 1, 3),
        value_matrix.transpose(0, 2, 1, 3),
    )


def page_block(query_rows, key_rows, value_matrix, decay_sum, carried):
    length = query_rows.shape[2]
    page_count = query_rows.shape[0]
    raised_rows = query_rows * jnp.exp(decay_sum)
    lowered = key_rows * jnp.exp(-decay_sum)
    scores = jnp.einsum("phik,phjk->phij", raised_rows, lowered, precision=TOP_PRECISION)
    rows_index = jnp.arange(length)
    causal = rows_index[:, None] >= rows_index[None, :]
    scores = jnp.where(causal[None, None], scores, 0.0)
    layer_output = jnp.einsum("phij,phjv->phiv", scores, value_matrix, precision=TOP_PRECISION)
    closing_sum = decay_sum[:, :, -1, :]
    weighted_rows = key_rows * jnp.exp(closing_sum[:, :, None, :] - decay_sum)
    page_terms = jnp.einsum(
        "phte,phtb->pheb", weighted_rows, value_matrix, precision=TOP_PRECISION
    )
    through = jnp.cumsum(closing_sum, axis=0)
    resets = jnp.cumsum(1.0 - carried)
    pages = jnp.arange(page_count)
    valid = (pages[:, None] >= pages[None, :]) & (resets[:, None] == resets[None, :])
    spread = through[:, None] - through[None, :]
    spread = jnp.where(valid[:, :, None, None], spread, 0.0)
    weights = jnp.where(valid[:, :, None, None], jnp.exp(spread), 0.0)
    memories = jnp.einsum("pqhe,qheb->pheb", weights, page_terms, precision=TOP_PRECISION)
    previous = jnp.concatenate([jnp.zeros_like(memories[:1]), memories[:-1]], axis=0)
    previous = previous * carried[:, None, None, None]
    layer_output = layer_output + jnp.einsum(
        "phik,phkv->phiv", raised_rows, previous, precision=TOP_PRECISION
    )
    return memories[-1], layer_output, memories


def on_device(
    tokens,
    attention_gain,
    project_weight,
    conv_weight,
    decay_down,
    decay_up,
    decay_bias,
    output_gate,
    head_gain,
    output_weight,
    mixer_gain,
    gate_weight,
    up_weight,
    down_weight,
    prompt_pages,
    prompt_start,
):
    token_count = tokens.shape[0]
    page_count = token_count // PAGE
    local_heads = project_weight.shape[1] // CONVW
    rim_rows = KCONV - 1
    seq_index = lax.axis_index("seq")
    group_pages = page_count * lax.axis_size("seq")
    page_flags = page_segments(prompt_pages[0], prompt_start[0], group_pages)
    carried = lax.dynamic_slice_in_dim(page_flags, seq_index * page_count, page_count)
    normed = rms_scaled(tokens, attention_gain).astype(jnp.bfloat16)
    projected = jnp.dot(normed, project_weight, preferred_element_type=jnp.float32).astype(
        jnp.bfloat16
    )
    by_page = projected.reshape(page_count, PAGE, local_heads * CONVW)
    incoming = shifted(by_page[-1, PAGE - rim_rows :], "seq", 1)
    before = jnp.concatenate([incoming[None], by_page[:-1, PAGE - rim_rows :]], axis=0)
    mixed_rows = short_conv(by_page, before, carried, conv_weight).reshape(
        page_count, PAGE, local_heads, CONVW
    )
    query_rows, key_rows, value_matrix = split_features(mixed_rows, HK)
    lowrank = jnp.dot(normed, decay_down, preferred_element_type=jnp.float32).astype(jnp.bfloat16)
    decay_log = (
        jax.nn.log_sigmoid(
            jnp.dot(lowrank, decay_up, preferred_element_type=jnp.float32) + decay_bias
        )
        / 16.0
    )
    decay_log = decay_log.reshape(page_count, PAGE, local_heads, HK).transpose(0, 2, 1, 3)
    decay_sum = jnp.cumsum(decay_log, axis=2)
    local_memory, outputs, memories = page_block(
        query_rows, key_rows, value_matrix, decay_sum, carried
    )
    totals = decay_sum[:, :, -1, :]
    through = jnp.cumsum(totals, axis=0)
    alive_mask = jnp.cumprod(carried)
    block_decay = alive_mask[-1] * jnp.exp(through[-1])

    def compose(earlier, latter):
        return (earlier[0] * latter[0], latter[0][..., None] * earlier[1] + latter[1])

    prefix = prefix_2(
        (block_decay, local_memory),
        "seq",
        compose,
        (jnp.ones_like(block_decay), jnp.zeros_like(local_memory)),
    )
    incoming_state = prefix[1]
    before_sum = through - totals
    extent_factor = alive_mask[:, None, None, None] * jnp.exp(decay_sum + before_sum[:, :, None, :])
    outputs = outputs + jnp.einsum(
        "dlof,lfg->dlog", query_rows * extent_factor, incoming_state, precision=TOP_PRECISION
    )
    memories = (
        memories + (alive_mask[:, None, None] * jnp.exp(through))[..., None] * incoming_state[None]
    )
    attended = outputs.transpose(0, 2, 1, 3).reshape(token_count, local_heads, HV)
    normed_heads = rms_scaled(attended, head_gain)
    opening = jax.nn.silu(jnp.dot(normed, output_gate, preferred_element_type=jnp.float32)).reshape(
        token_count, local_heads, HV
    )
    gated_rows = (
        (normed_heads * opening).astype(jnp.bfloat16).reshape(token_count, local_heads * HV)
    )
    partial_value = jnp.dot(gated_rows, output_weight, preferred_element_type=jnp.float32)
    half_rows = token_count // lax.axis_size("hid")
    row_start = lax.axis_index("hid") * half_rows
    mixed_sum = lax.psum(partial_value.astype(jnp.bfloat16), "hid").astype(jnp.float32)
    residual = (tokens.astype(jnp.float32) + mixed_sum).astype(jnp.bfloat16)
    feed_in = rms_scaled(residual, mixer_gain).astype(jnp.bfloat16)
    own_residual = lax.dynamic_slice_in_dim(residual, row_start, half_rows, 0)

    def widen(weight_rows):
        return jnp.dot(feed_in, weight_rows, preferred_element_type=jnp.float32)

    gate_part = widen(lax.all_gather(gate_weight, "req", axis=0, tiled=True))
    up_part = widen(lax.all_gather(up_weight, "req", axis=0, tiled=True))
    hidden = (jax.nn.silu(gate_part) * up_part).astype(jnp.bfloat16)
    partials = jnp.dot(
        hidden,
        lax.all_gather(down_weight, "req", axis=1, tiled=True),
        preferred_element_type=jnp.float32,
    )
    feed_sum = lax.psum_scatter(
        partials.astype(jnp.bfloat16), "hid", scatter_dimension=0, tiled=True
    ).astype(jnp.float32)
    result = (own_residual.astype(jnp.float32) + feed_sum).astype(jnp.bfloat16)
    return (result, memories.astype(jnp.bfloat16), by_page[:, PAGE - rim_rows :])


def solution(mesh):
    return jax.shard_map(
        on_device,
        mesh=mesh,
        in_specs=(
            P(("req", "seq"), None),
            P(),
            P(None, "hid"),
            P(None, "hid"),
            P(),
            P(None, "hid"),
            P("hid"),
            P(None, "hid"),
            P(),
            P("hid", None),
            P(),
            P("req", "hid"),
            P("req", "hid"),
            P("hid", "req"),
            P("req", None),
            P("req", None),
        ),
        out_specs=(
            P(("req", "seq", "hid"), None),
            P(("req", "seq"), "hid", None, None),
            P(("req", "seq"), None, "hid"),
        ),
        check_vma=False,
    )
```

```python
import jax
import jax.numpy as jnp
from jax import lax
from jax.sharding import PartitionSpec as P

HK = 256
HV = 512
KCONV = 4
PAGE = 64
CONVW = 1024


EPSILON = 1e-06
TOP_PRECISION = lax.Precision.HIGHEST


def shifted(value, axis, steps):
    count = lax.axis_size(axis)
    first, last = (max(0, -steps), min(count, count - steps))
    return lax.ppermute(value, axis, [(source, source + steps) for source in range(first, last)])


def prefix_2(array, axis, join, neutral):
    place = lax.axis_index(axis)
    gathered = jax.tree.map(
        lambda a, kind: lax.all_gather(a.astype(kind), axis), array, (jnp.bfloat16, jnp.bfloat16)
    )
    state = jax.tree.map(lambda a, e: jnp.zeros_like(a) + jnp.asarray(e, a.dtype), array, neutral)

    def one(lap, state):
        return join(
            state,
            jax.tree.map(
                lambda a, own: lax.dynamic_index_in_dim(a, lap, 0, False).astype(own.dtype),
                gathered,
                array,
            ),
        )

    return lax.fori_loop(0, place, one, state)


def rms_scaled(values, scale_gain):
    values = values.astype(jnp.float32)
    return (
        values
        * lax.rsqrt(jnp.mean(values * values, axis=-1, keepdims=True) + EPSILON)
        * scale_gain.astype(jnp.float32)
    )


def page_segments(page_counts, starts, total_pages):
    position = jnp.arange(total_pages, dtype=jnp.int32)
    inside = (position[None, :] >= starts[:, None]) & (
        position[None, :] < starts[:, None] + page_counts[:, None]
    )
    labels = jnp.arange(1, page_counts.shape[0] + 1, dtype=jnp.int32)
    segment = jnp.sum(jnp.where(inside, labels[:, None], 0), axis=0) - 1
    earlier = jnp.concatenate([jnp.full((1,), -1, jnp.int32), segment[:-1]])
    return ((segment == earlier) & (segment >= 0)).astype(jnp.float32)


def short_conv(by_page, before, carried, conv_taps):
    kept_rows = before.astype(jnp.float32) * carried[:, None, None]
    widened = jnp.concatenate([kept_rows, by_page.astype(jnp.float32)], axis=1)
    tap_count = conv_taps.shape[0]
    length = by_page.shape[1]
    result = jnp.zeros(by_page.shape, jnp.float32)
    for offset in range(tap_count):
        result = (
            result
            + conv_taps[offset].astype(jnp.float32)
            * widened[:, tap_count - 1 - offset : tap_count - 1 - offset + length]
        )
    return result


def split_features(mixed_rows, key_width):
    query_rows = jax.nn.silu(mixed_rows[..., :key_width])
    key_rows = jax.nn.silu(mixed_rows[..., key_width : 2 * key_width]) * key_width ** (-0.5)
    value_matrix = mixed_rows[..., 2 * key_width :]
    return (
        query_rows.transpose(0, 2, 1, 3),
        key_rows.transpose(0, 2, 1, 3),
        value_matrix.transpose(0, 2, 1, 3),
    )


def page_block(query_rows, key_rows, value_matrix, decay_sum, carried):
    length = query_rows.shape[2]
    page_count = query_rows.shape[0]
    raised_rows = query_rows * jnp.exp(decay_sum)
    lowered = key_rows * jnp.exp(-decay_sum)
    scores = jnp.einsum("phik,phjk->phij", raised_rows, lowered, precision=TOP_PRECISION)
    rows_index = jnp.arange(length)
    causal = rows_index[:, None] >= rows_index[None, :]
    scores = jnp.where(causal[None, None], scores, 0.0)
    layer_output = jnp.einsum("phij,phjv->phiv", scores, value_matrix, precision=TOP_PRECISION)
    closing_sum = decay_sum[:, :, -1, :]
    weighted_rows = key_rows * jnp.exp(closing_sum[:, :, None, :] - decay_sum)
    page_terms = jnp.einsum(
        "phte,phtb->pheb", weighted_rows, value_matrix, precision=TOP_PRECISION
    )
    through = jnp.cumsum(closing_sum, axis=0)
    resets = jnp.cumsum(1.0 - carried)
    pages = jnp.arange(page_count)
    valid = (pages[:, None] >= pages[None, :]) & (resets[:, None] == resets[None, :])
    spread = through[:, None] - through[None, :]
    spread = jnp.where(valid[:, :, None, None], spread, 0.0)
    weights = jnp.where(valid[:, :, None, None], jnp.exp(spread), 0.0)
    memories = jnp.einsum("pqhe,qheb->pheb", weights, page_terms, precision=TOP_PRECISION)
    previous = jnp.concatenate([jnp.zeros_like(memories[:1]), memories[:-1]], axis=0)
    previous = previous * carried[:, None, None, None]
    layer_output = layer_output + jnp.einsum(
        "phik,phkv->phiv", raised_rows, previous, precision=TOP_PRECISION
    )
    return memories[-1], layer_output, memories


def on_device(
    tokens,
    attention_gain,
    project_weight,
    conv_weight,
    decay_down,
    decay_up,
    decay_bias,
    output_gate,
    head_gain,
    output_weight,
    mixer_gain,
    gate_weight,
    up_weight,
    down_weight,
    prompt_pages,
    prompt_start,
):
    token_count = tokens.shape[0]
    page_count = token_count // PAGE
    local_heads = project_weight.shape[1] // CONVW
    rim_rows = KCONV - 1
    seq_index = lax.axis_index("seq")
    group_pages = page_count * lax.axis_size("seq")
    page_flags = page_segments(prompt_pages[0], prompt_start[0], group_pages)
    carried = lax.dynamic_slice_in_dim(page_flags, seq_index * page_count, page_count)
    normed = rms_scaled(tokens, attention_gain).astype(jnp.bfloat16)
    projected = jnp.dot(normed, project_weight, preferred_element_type=jnp.float32).astype(
        jnp.bfloat16
    )
    by_page = projected.reshape(page_count, PAGE, local_heads * CONVW)
    incoming = shifted(by_page[-1, PAGE - rim_rows :], "seq", 1)
    before = jnp.concatenate([incoming[None], by_page[:-1, PAGE - rim_rows :]], axis=0)
    mixed_rows = short_conv(by_page, before, carried, conv_weight).reshape(
        page_count, PAGE, local_heads, CONVW
    )
    query_rows, key_rows, value_matrix = split_features(mixed_rows, HK)
    gate_rows = lax.all_gather(gate_weight, "req", axis=0, tiled=True)
    up_rows = lax.all_gather(up_weight, "req", axis=0, tiled=True)
    down_columns = lax.all_gather(down_weight, "req", axis=1, tiled=True)
    gate_rows, query_rows = lax.optimization_barrier((gate_rows, query_rows))
    lowrank = jnp.dot(normed, decay_down, preferred_element_type=jnp.float32).astype(jnp.bfloat16)
    decay_log = (
        jax.nn.log_sigmoid(
            jnp.dot(lowrank, decay_up, preferred_element_type=jnp.float32) + decay_bias
        )
        / 16.0
    )
    decay_log = decay_log.reshape(page_count, PAGE, local_heads, HK).transpose(0, 2, 1, 3)
    decay_sum = jnp.cumsum(decay_log, axis=2)
    local_memory, outputs, memories = page_block(
        query_rows, key_rows, value_matrix, decay_sum, carried
    )
    totals = decay_sum[:, :, -1, :]
    through = jnp.cumsum(totals, axis=0)
    alive_mask = jnp.cumprod(carried)
    block_decay = alive_mask[-1] * jnp.exp(through[-1])

    def compose(earlier, latter):
        return (earlier[0] * latter[0], latter[0][..., None] * earlier[1] + latter[1])

    prefix = prefix_2(
        (block_decay, local_memory),
        "seq",
        compose,
        (jnp.ones_like(block_decay), jnp.zeros_like(local_memory)),
    )
    incoming_state = prefix[1]
    before_sum = through - totals
    extent_factor = alive_mask[:, None, None, None] * jnp.exp(decay_sum + before_sum[:, :, None, :])
    outputs = outputs + jnp.einsum(
        "dlof,lfg->dlog", query_rows * extent_factor, incoming_state, precision=TOP_PRECISION
    )
    memories = (
        memories + (alive_mask[:, None, None] * jnp.exp(through))[..., None] * incoming_state[None]
    )
    up_rows, outputs = lax.optimization_barrier((up_rows, outputs))
    attended = outputs.transpose(0, 2, 1, 3).reshape(token_count, local_heads, HV)
    normed_heads = rms_scaled(attended, head_gain)
    opening = jax.nn.silu(jnp.dot(normed, output_gate, preferred_element_type=jnp.float32)).reshape(
        token_count, local_heads, HV
    )
    gated_rows = (
        (normed_heads * opening).astype(jnp.bfloat16).reshape(token_count, local_heads * HV)
    )
    down_columns, gated_rows = lax.optimization_barrier((down_columns, gated_rows))
    partial_value = jnp.dot(gated_rows, output_weight, preferred_element_type=jnp.float32)
    half_rows = token_count // lax.axis_size("hid")
    row_start = lax.axis_index("hid") * half_rows
    mixed_sum = lax.psum(partial_value.astype(jnp.bfloat16), "hid").astype(jnp.float32)
    residual = (tokens.astype(jnp.float32) + mixed_sum).astype(jnp.bfloat16)
    feed_in = rms_scaled(residual, mixer_gain).astype(jnp.bfloat16)
    own_residual = lax.dynamic_slice_in_dim(residual, row_start, half_rows, 0)

    def widen(weight_rows):
        return jnp.dot(feed_in, weight_rows, preferred_element_type=jnp.float32)

    gate_part = widen(gate_rows)
    up_part = widen(up_rows)
    hidden = (jax.nn.silu(gate_part) * up_part).astype(jnp.bfloat16)
    partials = jnp.dot(hidden, down_columns, preferred_element_type=jnp.float32)
    feed_sum = lax.psum_scatter(
        partials.astype(jnp.bfloat16), "hid", scatter_dimension=0, tiled=True
    ).astype(jnp.float32)
    result = (own_residual.astype(jnp.float32) + feed_sum).astype(jnp.bfloat16)
    return (result, memories.astype(jnp.bfloat16), by_page[:, PAGE - rim_rows :])


def solution(mesh):
    return jax.shard_map(
        on_device,
        mesh=mesh,
        in_specs=(
            P(("req", "seq"), None),
            P(),
            P(None, "hid"),
            P(None, "hid"),
            P(),
            P(None, "hid"),
            P("hid"),
            P(None, "hid"),
            P(),
            P("hid", None),
            P(),
            P("req", "hid"),
            P("req", "hid"),
            P("hid", "req"),
            P("req", None),
            P("req", None),
        ),
        out_specs=(
            P(("req", "seq", "hid"), None),
            P(("req", "seq"), "hid", None, None),
            P(("req", "seq"), None, "hid"),
        ),
        check_vma=False,
    )
```

```python
import functools

import jax
import jax.numpy as jnp
from jax import lax
from jax.sharding import PartitionSpec as P
from jax.experimental import pallas as pl
from jax.experimental.pallas import tpu as pltpu

HK = 256
HV = 512
KCONV = 4
PAGE = 64
CONVW = 1024


EPSILON = 1e-06
TOP_PRECISION = lax.Precision.HIGHEST


def shifted(value, axis, steps):
    count = lax.axis_size(axis)
    first, last = (max(0, -steps), min(count, count - steps))
    return lax.ppermute(value, axis, [(source, source + steps) for source in range(first, last)])


def prefix_2(array, axis, join, neutral):
    place = lax.axis_index(axis)
    gathered = jax.tree.map(
        lambda a, kind: lax.all_gather(a.astype(kind), axis), array, (jnp.bfloat16, jnp.bfloat16)
    )
    state = jax.tree.map(lambda a, e: jnp.zeros_like(a) + jnp.asarray(e, a.dtype), array, neutral)

    def one(lap, state):
        return join(
            state,
            jax.tree.map(
                lambda a, own: lax.dynamic_index_in_dim(a, lap, 0, False).astype(own.dtype),
                gathered,
                array,
            ),
        )

    return lax.fori_loop(0, place, one, state)


def partner_kernel(rows, src_ref, dst_ref, send_sem, recv_sem):
    partner = 1 - lax.axis_index("hid")
    barrier = pltpu.get_barrier_semaphore()
    pl.semaphore_signal(
        barrier, inc=1, device_id={"hid": partner}, device_id_type=pl.DeviceIdType.MESH
    )
    pl.semaphore_wait(barrier, 1)
    start = pl.multiple_of(partner * rows, rows) if rows < src_ref.shape[0] else 0
    copy = pltpu.make_async_remote_copy(
        src_ref=src_ref.at[pl.ds(start, rows)],
        dst_ref=dst_ref,
        send_sem=send_sem,
        recv_sem=recv_sem,
        device_id={"hid": partner},
        device_id_type=pl.DeviceIdType.MESH,
    )
    copy.start()
    copy.wait()


def from_partner(value, rows, kernel_id):
    return pl.pallas_call(
        functools.partial(partner_kernel, rows),
        out_shape=jax.ShapeDtypeStruct((rows,) + value.shape[1:], value.dtype),
        in_specs=[pl.BlockSpec(memory_space=pl.ANY)],
        out_specs=pl.BlockSpec(memory_space=pl.ANY),
        scratch_shapes=[pltpu.SemaphoreType.DMA, pltpu.SemaphoreType.DMA],
        compiler_params=pltpu.CompilerParams(collective_id=kernel_id, has_side_effects=True),
    )(value)


def rms_scaled(values, scale_gain):
    values = values.astype(jnp.float32)
    return (
        values
        * lax.rsqrt(jnp.mean(values * values, axis=-1, keepdims=True) + EPSILON)
        * scale_gain.astype(jnp.float32)
    )


def page_segments(page_counts, starts, total_pages):
    position = jnp.arange(total_pages, dtype=jnp.int32)
    inside = (position[None, :] >= starts[:, None]) & (
        position[None, :] < starts[:, None] + page_counts[:, None]
    )
    labels = jnp.arange(1, page_counts.shape[0] + 1, dtype=jnp.int32)
    segment = jnp.sum(jnp.where(inside, labels[:, None], 0), axis=0) - 1
    earlier = jnp.concatenate([jnp.full((1,), -1, jnp.int32), segment[:-1]])
    return ((segment == earlier) & (segment >= 0)).astype(jnp.float32)


def short_conv(by_page, before, carried, conv_taps):
    kept_rows = before.astype(jnp.float32) * carried[:, None, None]
    widened = jnp.concatenate([kept_rows, by_page.astype(jnp.float32)], axis=1)
    tap_count = conv_taps.shape[0]
    length = by_page.shape[1]
    result = jnp.zeros(by_page.shape, jnp.float32)
    for offset in range(tap_count):
        result = (
            result
            + conv_taps[offset].astype(jnp.float32)
            * widened[:, tap_count - 1 - offset : tap_count - 1 - offset + length]
        )
    return result


def split_features(mixed_rows, key_width):
    query_rows = jax.nn.silu(mixed_rows[..., :key_width])
    key_rows = jax.nn.silu(mixed_rows[..., key_width : 2 * key_width]) * key_width ** (-0.5)
    value_matrix = mixed_rows[..., 2 * key_width :]
    return (
        query_rows.transpose(0, 2, 1, 3),
        key_rows.transpose(0, 2, 1, 3),
        value_matrix.transpose(0, 2, 1, 3),
    )


def page_block(query_rows, key_rows, value_matrix, decay_sum, carried):
    length = query_rows.shape[2]
    page_count = query_rows.shape[0]
    raised_rows = query_rows * jnp.exp(decay_sum)
    lowered = key_rows * jnp.exp(-decay_sum)
    scores = jnp.einsum("phik,phjk->phij", raised_rows, lowered, precision=TOP_PRECISION)
    rows_index = jnp.arange(length)
    causal = rows_index[:, None] >= rows_index[None, :]
    scores = jnp.where(causal[None, None], scores, 0.0)
    layer_output = jnp.einsum("phij,phjv->phiv", scores, value_matrix, precision=TOP_PRECISION)
    closing_sum = decay_sum[:, :, -1, :]
    weighted_rows = key_rows * jnp.exp(closing_sum[:, :, None, :] - decay_sum)
    page_terms = jnp.einsum(
        "phte,phtb->pheb", weighted_rows, value_matrix, precision=TOP_PRECISION
    )
    through = jnp.cumsum(closing_sum, axis=0)
    resets = jnp.cumsum(1.0 - carried)
    pages = jnp.arange(page_count)
    valid = (pages[:, None] >= pages[None, :]) & (resets[:, None] == resets[None, :])
    spread = through[:, None] - through[None, :]
    spread = jnp.where(valid[:, :, None, None], spread, 0.0)
    weights = jnp.where(valid[:, :, None, None], jnp.exp(spread), 0.0)
    memories = jnp.einsum("pqhe,qheb->pheb", weights, page_terms, precision=TOP_PRECISION)
    previous = jnp.concatenate([jnp.zeros_like(memories[:1]), memories[:-1]], axis=0)
    previous = previous * carried[:, None, None, None]
    layer_output = layer_output + jnp.einsum(
        "phik,phkv->phiv", raised_rows, previous, precision=TOP_PRECISION
    )
    return memories[-1], layer_output, memories


def on_device(
    tokens,
    attention_gain,
    project_weight,
    conv_weight,
    decay_down,
    decay_up,
    decay_bias,
    output_gate,
    head_gain,
    output_weight,
    mixer_gain,
    gate_weight,
    up_weight,
    down_weight,
    prompt_pages,
    prompt_start,
):
    token_count = tokens.shape[0]
    page_count = token_count // PAGE
    local_heads = project_weight.shape[1] // CONVW
    rim_rows = KCONV - 1
    seq_index = lax.axis_index("seq")
    group_pages = page_count * lax.axis_size("seq")
    page_flags = page_segments(prompt_pages[0], prompt_start[0], group_pages)
    carried = lax.dynamic_slice_in_dim(page_flags, seq_index * page_count, page_count)
    normed = rms_scaled(tokens, attention_gain).astype(jnp.bfloat16)
    projected = jnp.dot(normed, project_weight, preferred_element_type=jnp.float32).astype(
        jnp.bfloat16
    )
    by_page = projected.reshape(page_count, PAGE, local_heads * CONVW)
    incoming = shifted(by_page[-1, PAGE - rim_rows :], "seq", 1)
    before = jnp.concatenate([incoming[None], by_page[:-1, PAGE - rim_rows :]], axis=0)
    mixed_rows = short_conv(by_page, before, carried, conv_weight).reshape(
        page_count, PAGE, local_heads, CONVW
    )
    query_rows, key_rows, value_matrix = split_features(mixed_rows, HK)
    lowrank = jnp.dot(normed, decay_down, preferred_element_type=jnp.float32).astype(jnp.bfloat16)
    decay_log = (
        jax.nn.log_sigmoid(
            jnp.dot(lowrank, decay_up, preferred_element_type=jnp.float32) + decay_bias
        )
        / 16.0
    )
    decay_log = decay_log.reshape(page_count, PAGE, local_heads, HK).transpose(0, 2, 1, 3)
    decay_sum = jnp.cumsum(decay_log, axis=2)
    local_memory, outputs, memories = page_block(
        query_rows, key_rows, value_matrix, decay_sum, carried
    )
    totals = decay_sum[:, :, -1, :]
    through = jnp.cumsum(totals, axis=0)
    alive_mask = jnp.cumprod(carried)
    block_decay = alive_mask[-1] * jnp.exp(through[-1])

    def compose(earlier, latter):
        return (earlier[0] * latter[0], latter[0][..., None] * earlier[1] + latter[1])

    prefix = prefix_2(
        (block_decay, local_memory),
        "seq",
        compose,
        (jnp.ones_like(block_decay), jnp.zeros_like(local_memory)),
    )
    incoming_state = prefix[1]
    before_sum = through - totals
    extent_factor = alive_mask[:, None, None, None] * jnp.exp(decay_sum + before_sum[:, :, None, :])
    outputs = outputs + jnp.einsum(
        "dlof,lfg->dlog", query_rows * extent_factor, incoming_state, precision=TOP_PRECISION
    )
    memories = (
        memories + (alive_mask[:, None, None] * jnp.exp(through))[..., None] * incoming_state[None]
    )
    attended = outputs.transpose(0, 2, 1, 3).reshape(token_count, local_heads, HV)
    normed_heads = rms_scaled(attended, head_gain)
    opening = jax.nn.silu(jnp.dot(normed, output_gate, preferred_element_type=jnp.float32)).reshape(
        token_count, local_heads, HV
    )
    gated_rows = (
        (normed_heads * opening).astype(jnp.bfloat16).reshape(token_count, local_heads * HV)
    )
    partial_value = jnp.dot(gated_rows, output_weight, preferred_element_type=jnp.float32)
    half_rows = token_count // lax.axis_size("hid")
    row_start = lax.axis_index("hid") * half_rows
    own_value = partial_value.astype(jnp.bfloat16)
    mixed_sum = own_value.astype(jnp.float32) + from_partner(own_value, token_count, 0).astype(
        jnp.float32
    )
    residual = (tokens.astype(jnp.float32) + mixed_sum).astype(jnp.bfloat16)
    feed_in = rms_scaled(residual, mixer_gain).astype(jnp.bfloat16)
    own_residual = lax.dynamic_slice_in_dim(residual, row_start, half_rows, 0)

    def widen(weight_rows):
        return jnp.dot(feed_in, weight_rows, preferred_element_type=jnp.float32)

    gate_part = widen(lax.all_gather(gate_weight, "req", axis=0, tiled=True))
    up_part = widen(lax.all_gather(up_weight, "req", axis=0, tiled=True))
    hidden = (jax.nn.silu(gate_part) * up_part).astype(jnp.bfloat16)
    partials = jnp.dot(
        hidden,
        lax.all_gather(down_weight, "req", axis=1, tiled=True),
        preferred_element_type=jnp.float32,
    )
    own_partials = partials.astype(jnp.bfloat16)
    feed_sum = lax.dynamic_slice_in_dim(own_partials, row_start, half_rows, 0).astype(
        jnp.float32
    ) + from_partner(own_partials, half_rows, 1).astype(jnp.float32)
    result = (own_residual.astype(jnp.float32) + feed_sum).astype(jnp.bfloat16)
    return (result, memories.astype(jnp.bfloat16), by_page[:, PAGE - rim_rows :])


def solution(mesh):
    return jax.shard_map(
        on_device,
        mesh=mesh,
        in_specs=(
            P(("req", "seq"), None),
            P(),
            P(None, "hid"),
            P(None, "hid"),
            P(),
            P(None, "hid"),
            P("hid"),
            P(None, "hid"),
            P(),
            P("hid", None),
            P(),
            P("req", "hid"),
            P("req", "hid"),
            P("hid", "req"),
            P("req", None),
            P("req", None),
        ),
        out_specs=(
            P(("req", "seq", "hid"), None),
            P(("req", "seq"), "hid", None, None),
            P(("req", "seq"), None, "hid"),
        ),
        check_vma=False,
    )
```

```python
import functools

import jax
import jax.numpy as jnp
from jax import lax
from jax.sharding import PartitionSpec as P
from jax.experimental import pallas as pl
from jax.experimental.pallas import tpu as pltpu

HK = 256
HV = 512
KCONV = 4
PAGE = 64
CONVW = 1024


EPSILON = 1e-06
TOP_PRECISION = lax.Precision.HIGHEST


def shifted(value, axis, steps):
    count = lax.axis_size(axis)
    first, last = (max(0, -steps), min(count, count - steps))
    return lax.ppermute(value, axis, [(source, source + steps) for source in range(first, last)])


def prefix_2(array, axis, join, neutral):
    place = lax.axis_index(axis)
    decay, memory = array
    width = memory.shape[-1]
    packed = jnp.concatenate(
        [memory.reshape(-1, width), jnp.pad(decay.reshape(1, -1), ((0, 0), (0, width - decay.size)))],
        axis=0,
    ).astype(jnp.bfloat16)
    received = spread_over_seq(packed)
    gathered = (
        received[:, -1, : decay.size].reshape((-1,) + decay.shape),
        received[:, :-1].reshape((-1,) + memory.shape),
    )
    state = jax.tree.map(lambda a, e: jnp.zeros_like(a) + jnp.asarray(e, a.dtype), array, neutral)

    def one(lap, state):
        return join(
            state,
            jax.tree.map(
                lambda a, own: lax.dynamic_index_in_dim(a, lap, 0, False).astype(own.dtype),
                gathered,
                array,
            ),
        )

    return lax.fori_loop(0, place, one, state)


def partner_kernel(rows, src_ref, dst_ref, send_sem, recv_sem):
    partner = 1 - lax.axis_index("hid")
    barrier = pltpu.get_barrier_semaphore()
    pl.semaphore_signal(
        barrier, inc=1, device_id={"hid": partner}, device_id_type=pl.DeviceIdType.MESH
    )
    pl.semaphore_wait(barrier, 1)
    start = pl.multiple_of(partner * rows, rows) if rows < src_ref.shape[0] else 0
    copy = pltpu.make_async_remote_copy(
        src_ref=src_ref.at[pl.ds(start, rows)],
        dst_ref=dst_ref,
        send_sem=send_sem,
        recv_sem=recv_sem,
        device_id={"hid": partner},
        device_id_type=pl.DeviceIdType.MESH,
    )
    copy.start()
    copy.wait()


def from_partner(value, rows, kernel_id):
    return pl.pallas_call(
        functools.partial(partner_kernel, rows),
        out_shape=jax.ShapeDtypeStruct((rows,) + value.shape[1:], value.dtype),
        in_specs=[pl.BlockSpec(memory_space=pl.ANY)],
        out_specs=pl.BlockSpec(memory_space=pl.ANY),
        scratch_shapes=[pltpu.SemaphoreType.DMA, pltpu.SemaphoreType.DMA],
        compiler_params=pltpu.CompilerParams(collective_id=kernel_id, has_side_effects=True),
    )(value)


def spread_kernel(src_ref, dst_ref, send_sem, recv_sem):
    count = lax.axis_size("seq")
    me = lax.axis_index("seq")
    barrier = pltpu.get_barrier_semaphore()
    for step in range(1, count):
        pl.semaphore_signal(
            barrier,
            inc=1,
            device_id={"seq": lax.rem(me + step, count)},
            device_id_type=pl.DeviceIdType.MESH,
        )
    pl.semaphore_wait(barrier, count - 1)
    copies = []
    for step in range(1, count):
        copy = pltpu.make_async_remote_copy(
            src_ref=src_ref,
            dst_ref=dst_ref.at[me],
            send_sem=send_sem.at[step - 1],
            recv_sem=recv_sem.at[me],
            device_id={"seq": lax.rem(me + step, count)},
            device_id_type=pl.DeviceIdType.MESH,
        )
        copy.start()
        copies.append(copy)
    for copy in copies:
        copy.wait_send()
    for step in range(1, count):
        source = lax.rem(me + count - step, count)
        pltpu.make_async_remote_copy(
            src_ref=src_ref,
            dst_ref=dst_ref.at[source],
            send_sem=send_sem.at[step - 1],
            recv_sem=recv_sem.at[source],
            device_id={"seq": source},
            device_id_type=pl.DeviceIdType.MESH,
        ).wait_recv()


def spread_over_seq(value):
    count = lax.axis_size("seq")
    return pl.pallas_call(
        spread_kernel,
        out_shape=jax.ShapeDtypeStruct((count,) + value.shape, value.dtype),
        in_specs=[pl.BlockSpec(memory_space=pl.ANY)],
        out_specs=pl.BlockSpec(memory_space=pl.ANY),
        scratch_shapes=[
            pltpu.SemaphoreType.DMA((count - 1,)),
            pltpu.SemaphoreType.DMA((count,)),
        ],
        compiler_params=pltpu.CompilerParams(collective_id=2, has_side_effects=True),
    )(value)


def rms_scaled(values, scale_gain):
    values = values.astype(jnp.float32)
    return (
        values
        * lax.rsqrt(jnp.mean(values * values, axis=-1, keepdims=True) + EPSILON)
        * scale_gain.astype(jnp.float32)
    )


def page_segments(page_counts, starts, total_pages):
    position = jnp.arange(total_pages, dtype=jnp.int32)
    inside = (position[None, :] >= starts[:, None]) & (
        position[None, :] < starts[:, None] + page_counts[:, None]
    )
    labels = jnp.arange(1, page_counts.shape[0] + 1, dtype=jnp.int32)
    segment = jnp.sum(jnp.where(inside, labels[:, None], 0), axis=0) - 1
    earlier = jnp.concatenate([jnp.full((1,), -1, jnp.int32), segment[:-1]])
    return ((segment == earlier) & (segment >= 0)).astype(jnp.float32)


def short_conv(by_page, before, carried, conv_taps):
    kept_rows = before.astype(jnp.float32) * carried[:, None, None]
    widened = jnp.concatenate([kept_rows, by_page.astype(jnp.float32)], axis=1)
    tap_count = conv_taps.shape[0]
    length = by_page.shape[1]
    result = jnp.zeros(by_page.shape, jnp.float32)
    for offset in range(tap_count):
        result = (
            result
            + conv_taps[offset].astype(jnp.float32)
            * widened[:, tap_count - 1 - offset : tap_count - 1 - offset + length]
        )
    return result


def split_features(mixed_rows, key_width):
    query_rows = jax.nn.silu(mixed_rows[..., :key_width])
    key_rows = jax.nn.silu(mixed_rows[..., key_width : 2 * key_width]) * key_width ** (-0.5)
    value_matrix = mixed_rows[..., 2 * key_width :]
    return (
        query_rows.transpose(0, 2, 1, 3),
        key_rows.transpose(0, 2, 1, 3),
        value_matrix.transpose(0, 2, 1, 3),
    )


def page_block(query_rows, key_rows, value_matrix, decay_sum, carried):
    length = query_rows.shape[2]
    page_count = query_rows.shape[0]
    raised_rows = query_rows * jnp.exp(decay_sum)
    lowered = key_rows * jnp.exp(-decay_sum)
    scores = jnp.einsum("phik,phjk->phij", raised_rows, lowered, precision=TOP_PRECISION)
    rows_index = jnp.arange(length)
    causal = rows_index[:, None] >= rows_index[None, :]
    scores = jnp.where(causal[None, None], scores, 0.0)
    layer_output = jnp.einsum("phij,phjv->phiv", scores, value_matrix, precision=TOP_PRECISION)
    closing_sum = decay_sum[:, :, -1, :]
    weighted_rows = key_rows * jnp.exp(closing_sum[:, :, None, :] - decay_sum)
    page_terms = jnp.einsum(
        "phte,phtb->pheb", weighted_rows, value_matrix, precision=TOP_PRECISION
    )
    through = jnp.cumsum(closing_sum, axis=0)
    resets = jnp.cumsum(1.0 - carried)
    pages = jnp.arange(page_count)
    valid = (pages[:, None] >= pages[None, :]) & (resets[:, None] == resets[None, :])
    spread = through[:, None] - through[None, :]
    spread = jnp.where(valid[:, :, None, None], spread, 0.0)
    weights = jnp.where(valid[:, :, None, None], jnp.exp(spread), 0.0)
    memories = jnp.einsum("pqhe,qheb->pheb", weights, page_terms, precision=TOP_PRECISION)
    previous = jnp.concatenate([jnp.zeros_like(memories[:1]), memories[:-1]], axis=0)
    previous = previous * carried[:, None, None, None]
    layer_output = layer_output + jnp.einsum(
        "phik,phkv->phiv", raised_rows, previous, precision=TOP_PRECISION
    )
    return memories[-1], layer_output, memories


def on_device(
    tokens,
    attention_gain,
    project_weight,
    conv_weight,
    decay_down,
    decay_up,
    decay_bias,
    output_gate,
    head_gain,
    output_weight,
    mixer_gain,
    gate_weight,
    up_weight,
    down_weight,
    prompt_pages,
    prompt_start,
):
    token_count = tokens.shape[0]
    page_count = token_count // PAGE
    local_heads = project_weight.shape[1] // CONVW
    rim_rows = KCONV - 1
    seq_index = lax.axis_index("seq")
    group_pages = page_count * lax.axis_size("seq")
    page_flags = page_segments(prompt_pages[0], prompt_start[0], group_pages)
    carried = lax.dynamic_slice_in_dim(page_flags, seq_index * page_count, page_count)
    normed = rms_scaled(tokens, attention_gain).astype(jnp.bfloat16)
    projected = jnp.dot(normed, project_weight, preferred_element_type=jnp.float32).astype(
        jnp.bfloat16
    )
    by_page = projected.reshape(page_count, PAGE, local_heads * CONVW)
    incoming = shifted(by_page[-1, PAGE - rim_rows :], "seq", 1)
    before = jnp.concatenate([incoming[None], by_page[:-1, PAGE - rim_rows :]], axis=0)
    mixed_rows = short_conv(by_page, before, carried, conv_weight).reshape(
        page_count, PAGE, local_heads, CONVW
    )
    query_rows, key_rows, value_matrix = split_features(mixed_rows, HK)
    lowrank = jnp.dot(normed, decay_down, preferred_element_type=jnp.float32).astype(jnp.bfloat16)
    decay_log = (
        jax.nn.log_sigmoid(
            jnp.dot(lowrank, decay_up, preferred_element_type=jnp.float32) + decay_bias
        )
        / 16.0
    )
    decay_log = decay_log.reshape(page_count, PAGE, local_heads, HK).transpose(0, 2, 1, 3)
    decay_sum = jnp.cumsum(decay_log, axis=2)
    local_memory, outputs, memories = page_block(
        query_rows, key_rows, value_matrix, decay_sum, carried
    )
    totals = decay_sum[:, :, -1, :]
    through = jnp.cumsum(totals, axis=0)
    alive_mask = jnp.cumprod(carried)
    block_decay = alive_mask[-1] * jnp.exp(through[-1])

    def compose(earlier, latter):
        return (earlier[0] * latter[0], latter[0][..., None] * earlier[1] + latter[1])

    prefix = prefix_2(
        (block_decay, local_memory),
        "seq",
        compose,
        (jnp.ones_like(block_decay), jnp.zeros_like(local_memory)),
    )
    incoming_state = prefix[1]
    before_sum = through - totals
    extent_factor = alive_mask[:, None, None, None] * jnp.exp(decay_sum + before_sum[:, :, None, :])
    outputs = outputs + jnp.einsum(
        "dlof,lfg->dlog", query_rows * extent_factor, incoming_state, precision=TOP_PRECISION
    )
    memories = (
        memories + (alive_mask[:, None, None] * jnp.exp(through))[..., None] * incoming_state[None]
    )
    attended = outputs.transpose(0, 2, 1, 3).reshape(token_count, local_heads, HV)
    normed_heads = rms_scaled(attended, head_gain)
    opening = jax.nn.silu(jnp.dot(normed, output_gate, preferred_element_type=jnp.float32)).reshape(
        token_count, local_heads, HV
    )
    gated_rows = (
        (normed_heads * opening).astype(jnp.bfloat16).reshape(token_count, local_heads * HV)
    )
    partial_value = jnp.dot(gated_rows, output_weight, preferred_element_type=jnp.float32)
    half_rows = token_count // lax.axis_size("hid")
    row_start = lax.axis_index("hid") * half_rows
    own_value = partial_value.astype(jnp.bfloat16)
    mixed_sum = own_value.astype(jnp.float32) + from_partner(own_value, token_count, 0).astype(
        jnp.float32
    )
    residual = (tokens.astype(jnp.float32) + mixed_sum).astype(jnp.bfloat16)
    feed_in = rms_scaled(residual, mixer_gain).astype(jnp.bfloat16)
    own_residual = lax.dynamic_slice_in_dim(residual, row_start, half_rows, 0)

    def widen(weight_rows):
        return jnp.dot(feed_in, weight_rows, preferred_element_type=jnp.float32)

    gate_part = widen(lax.all_gather(gate_weight, "req", axis=0, tiled=True))
    up_part = widen(lax.all_gather(up_weight, "req", axis=0, tiled=True))
    hidden = (jax.nn.silu(gate_part) * up_part).astype(jnp.bfloat16)
    partials = jnp.dot(
        hidden,
        lax.all_gather(down_weight, "req", axis=1, tiled=True),
        preferred_element_type=jnp.float32,
    )
    own_partials = partials.astype(jnp.bfloat16)
    feed_sum = lax.dynamic_slice_in_dim(own_partials, row_start, half_rows, 0).astype(
        jnp.float32
    ) + from_partner(own_partials, half_rows, 1).astype(jnp.float32)
    result = (own_residual.astype(jnp.float32) + feed_sum).astype(jnp.bfloat16)
    return (result, memories.astype(jnp.bfloat16), by_page[:, PAGE - rim_rows :])


def solution(mesh):
    return jax.shard_map(
        on_device,
        mesh=mesh,
        in_specs=(
            P(("req", "seq"), None),
            P(),
            P(None, "hid"),
            P(None, "hid"),
            P(),
            P(None, "hid"),
            P("hid"),
            P(None, "hid"),
            P(),
            P("hid", None),
            P(),
            P("req", "hid"),
            P("req", "hid"),
            P("hid", "req"),
            P("req", None),
            P("req", None),
        ),
        out_specs=(
            P(("req", "seq", "hid"), None),
            P(("req", "seq"), "hid", None, None),
            P(("req", "seq"), None, "hid"),
        ),
        check_vma=False,
    )
```

```python
import functools

import jax
import jax.numpy as jnp
from jax import lax
from jax.sharding import PartitionSpec as P
from jax.experimental import pallas as pl
from jax.experimental.pallas import tpu as pltpu

HK = 256
HV = 512
KCONV = 4
PAGE = 64
CONVW = 1024


EPSILON = 1e-06
TOP_PRECISION = lax.Precision.HIGHEST


def shifted(value, axis, steps):
    count = lax.axis_size(axis)
    first, last = (max(0, -steps), min(count, count - steps))
    return lax.ppermute(value, axis, [(source, source + steps) for source in range(first, last)])


def prefix_2(array, axis, join, neutral):
    place = lax.axis_index(axis)
    decay, memory = array
    width = memory.shape[-1]
    packed = jnp.concatenate(
        [memory.reshape(-1, width), jnp.pad(decay.reshape(1, -1), ((0, 0), (0, width - decay.size)))],
        axis=0,
    ).astype(jnp.bfloat16)
    received = spread_over_seq(packed)
    gathered = (
        received[:, -1, : decay.size].reshape((-1,) + decay.shape),
        received[:, :-1].reshape((-1,) + memory.shape),
    )
    state = jax.tree.map(lambda a, e: jnp.zeros_like(a) + jnp.asarray(e, a.dtype), array, neutral)

    def one(lap, state):
        return join(
            state,
            jax.tree.map(
                lambda a, own: lax.dynamic_index_in_dim(a, lap, 0, False).astype(own.dtype),
                gathered,
                array,
            ),
        )

    return lax.fori_loop(0, place, one, state)


def partner_kernel(rows, src_ref, dst_ref, send_sem, recv_sem):
    partner = 1 - lax.axis_index("hid")
    barrier = pltpu.get_barrier_semaphore()
    pl.semaphore_signal(
        barrier, inc=1, device_id={"hid": partner}, device_id_type=pl.DeviceIdType.MESH
    )
    pl.semaphore_wait(barrier, 1)
    start = pl.multiple_of(partner * rows, rows) if rows < src_ref.shape[0] else 0
    copy = pltpu.make_async_remote_copy(
        src_ref=src_ref.at[pl.ds(start, rows)],
        dst_ref=dst_ref,
        send_sem=send_sem,
        recv_sem=recv_sem,
        device_id={"hid": partner},
        device_id_type=pl.DeviceIdType.MESH,
    )
    copy.start()
    copy.wait()


def from_partner(value, rows, kernel_id):
    return pl.pallas_call(
        functools.partial(partner_kernel, rows),
        out_shape=jax.ShapeDtypeStruct((rows,) + value.shape[1:], value.dtype),
        in_specs=[pl.BlockSpec(memory_space=pl.ANY)],
        out_specs=pl.BlockSpec(memory_space=pl.ANY),
        scratch_shapes=[pltpu.SemaphoreType.DMA, pltpu.SemaphoreType.DMA],
        compiler_params=pltpu.CompilerParams(collective_id=kernel_id, has_side_effects=True),
    )(value)


def spread_kernel(src_ref, dst_ref, send_sem, recv_sem):
    count = lax.axis_size("seq")
    me = lax.axis_index("seq")
    barrier = pltpu.get_barrier_semaphore()
    for step in range(1, count):
        pl.semaphore_signal(
            barrier,
            inc=1,
            device_id={"seq": lax.rem(me + step, count)},
            device_id_type=pl.DeviceIdType.MESH,
        )
    pl.semaphore_wait(barrier, count - 1)
    copies = []
    for step in range(1, count):
        copy = pltpu.make_async_remote_copy(
            src_ref=src_ref,
            dst_ref=dst_ref.at[me],
            send_sem=send_sem.at[step - 1],
            recv_sem=recv_sem.at[me],
            device_id={"seq": lax.rem(me + step, count)},
            device_id_type=pl.DeviceIdType.MESH,
        )
        copy.start()
        copies.append(copy)
    for copy in copies:
        copy.wait_send()
    for step in range(1, count):
        source = lax.rem(me + count - step, count)
        pltpu.make_async_remote_copy(
            src_ref=src_ref,
            dst_ref=dst_ref.at[source],
            send_sem=send_sem.at[step - 1],
            recv_sem=recv_sem.at[source],
            device_id={"seq": source},
            device_id_type=pl.DeviceIdType.MESH,
        ).wait_recv()


def spread_over_seq(value):
    count = lax.axis_size("seq")
    return pl.pallas_call(
        spread_kernel,
        out_shape=jax.ShapeDtypeStruct((count,) + value.shape, value.dtype),
        in_specs=[pl.BlockSpec(memory_space=pl.ANY)],
        out_specs=pl.BlockSpec(memory_space=pl.ANY),
        scratch_shapes=[
            pltpu.SemaphoreType.DMA((count - 1,)),
            pltpu.SemaphoreType.DMA((count,)),
        ],
        compiler_params=pltpu.CompilerParams(collective_id=2, has_side_effects=True),
    )(value)


def rms_scaled(values, scale_gain):
    values = values.astype(jnp.float32)
    return (
        values
        * lax.rsqrt(jnp.mean(values * values, axis=-1, keepdims=True) + EPSILON)
        * scale_gain.astype(jnp.float32)
    )


def page_segments(page_counts, starts, total_pages):
    position = jnp.arange(total_pages, dtype=jnp.int32)
    inside = (position[None, :] >= starts[:, None]) & (
        position[None, :] < starts[:, None] + page_counts[:, None]
    )
    labels = jnp.arange(1, page_counts.shape[0] + 1, dtype=jnp.int32)
    segment = jnp.sum(jnp.where(inside, labels[:, None], 0), axis=0) - 1
    earlier = jnp.concatenate([jnp.full((1,), -1, jnp.int32), segment[:-1]])
    return ((segment == earlier) & (segment >= 0)).astype(jnp.float32)


def short_conv(by_page, before, carried, conv_taps):
    kept_rows = before.astype(jnp.float32) * carried[:, None, None]
    widened = jnp.concatenate([kept_rows, by_page.astype(jnp.float32)], axis=1)
    tap_count = conv_taps.shape[0]
    length = by_page.shape[1]
    result = jnp.zeros(by_page.shape, jnp.float32)
    for offset in range(tap_count):
        result = (
            result
            + conv_taps[offset].astype(jnp.float32)
            * widened[:, tap_count - 1 - offset : tap_count - 1 - offset + length]
        )
    return result


def split_features(mixed_rows, key_width):
    query_rows = jax.nn.silu(mixed_rows[..., :key_width])
    key_rows = jax.nn.silu(mixed_rows[..., key_width : 2 * key_width]) * key_width ** (-0.5)
    value_matrix = mixed_rows[..., 2 * key_width :]
    return (
        query_rows.transpose(0, 2, 1, 3),
        key_rows.transpose(0, 2, 1, 3),
        value_matrix.transpose(0, 2, 1, 3),
    )


def page_block(query_rows, key_rows, value_matrix, decay_sum, carried):
    length = query_rows.shape[2]
    page_count = query_rows.shape[0]
    raised_rows = query_rows * jnp.exp(decay_sum)
    lowered = key_rows * jnp.exp(-decay_sum)
    scores = jnp.einsum("phik,phjk->phij", raised_rows, lowered, precision=TOP_PRECISION)
    rows_index = jnp.arange(length)
    causal = rows_index[:, None] >= rows_index[None, :]
    scores = jnp.where(causal[None, None], scores, 0.0)
    layer_output = jnp.einsum("phij,phjv->phiv", scores, value_matrix, precision=TOP_PRECISION)
    closing_sum = decay_sum[:, :, -1, :]
    weighted_rows = key_rows * jnp.exp(closing_sum[:, :, None, :] - decay_sum)
    page_terms = jnp.einsum(
        "phte,phtb->pheb", weighted_rows, value_matrix, precision=TOP_PRECISION
    )
    through = jnp.cumsum(closing_sum, axis=0)
    resets = jnp.cumsum(1.0 - carried)
    pages = jnp.arange(page_count)
    valid = (pages[:, None] >= pages[None, :]) & (resets[:, None] == resets[None, :])
    spread = through[:, None] - through[None, :]
    spread = jnp.where(valid[:, :, None, None], spread, 0.0)
    weights = jnp.where(valid[:, :, None, None], jnp.exp(spread), 0.0)
    memories = jnp.einsum("pqhe,qheb->pheb", weights, page_terms, precision=TOP_PRECISION)
    previous = jnp.concatenate([jnp.zeros_like(memories[:1]), memories[:-1]], axis=0)
    previous = previous * carried[:, None, None, None]
    layer_output = layer_output + jnp.einsum(
        "phik,phkv->phiv", raised_rows, previous, precision=TOP_PRECISION
    )
    return memories[-1], layer_output, memories


def on_device(
    tokens,
    attention_gain,
    project_weight,
    conv_weight,
    decay_down,
    decay_up,
    decay_bias,
    output_gate,
    head_gain,
    output_weight,
    mixer_gain,
    gate_weight,
    up_weight,
    down_weight,
    prompt_pages,
    prompt_start,
):
    token_count = tokens.shape[0]
    page_count = token_count // PAGE
    local_heads = project_weight.shape[1] // CONVW
    rim_rows = KCONV - 1
    seq_index = lax.axis_index("seq")
    group_pages = page_count * lax.axis_size("seq")
    page_flags = page_segments(prompt_pages[0], prompt_start[0], group_pages)
    carried = lax.dynamic_slice_in_dim(page_flags, seq_index * page_count, page_count)
    normed = rms_scaled(tokens, attention_gain).astype(jnp.bfloat16)
    projected = jnp.dot(normed, project_weight, preferred_element_type=jnp.float32).astype(
        jnp.bfloat16
    )
    by_page = projected.reshape(page_count, PAGE, local_heads * CONVW)
    incoming = shifted(by_page[-1, PAGE - rim_rows :], "seq", 1)
    before = jnp.concatenate([incoming[None], by_page[:-1, PAGE - rim_rows :]], axis=0)
    mixed_rows = short_conv(by_page, before, carried, conv_weight).reshape(
        page_count, PAGE, local_heads, CONVW
    )
    query_rows, key_rows, value_matrix = split_features(mixed_rows, HK)
    lowrank = jnp.dot(normed, decay_down, preferred_element_type=jnp.float32).astype(jnp.bfloat16)
    decay_log = (
        jax.nn.log_sigmoid(
            jnp.dot(lowrank, decay_up, preferred_element_type=jnp.float32) + decay_bias
        )
        / 16.0
    )
    decay_log = decay_log.reshape(page_count, PAGE, local_heads, HK).transpose(0, 2, 1, 3)
    decay_sum = jnp.cumsum(decay_log, axis=2)
    local_memory, outputs, memories = page_block(
        query_rows, key_rows, value_matrix, decay_sum, carried
    )
    totals = decay_sum[:, :, -1, :]
    through = jnp.cumsum(totals, axis=0)
    alive_mask = jnp.cumprod(carried)
    block_decay = alive_mask[-1] * jnp.exp(through[-1])

    def compose(earlier, latter):
        return (earlier[0] * latter[0], latter[0][..., None] * earlier[1] + latter[1])

    prefix = prefix_2(
        (block_decay, local_memory),
        "seq",
        compose,
        (jnp.ones_like(block_decay), jnp.zeros_like(local_memory)),
    )
    incoming_state = prefix[1]
    before_sum = through - totals
    extent_factor = alive_mask[:, None, None, None] * jnp.exp(decay_sum + before_sum[:, :, None, :])
    outputs = outputs + jnp.einsum(
        "dlof,lfg->dlog", query_rows * extent_factor, incoming_state, precision=TOP_PRECISION
    )
    memories = (
        memories + (alive_mask[:, None, None] * jnp.exp(through))[..., None] * incoming_state[None]
    )
    attended = outputs.transpose(0, 2, 1, 3).reshape(token_count, local_heads, HV)
    normed_heads = rms_scaled(attended, head_gain)
    opening = jax.nn.silu(jnp.dot(normed, output_gate, preferred_element_type=jnp.float32)).reshape(
        token_count, local_heads, HV
    )
    gated_rows = (
        (normed_heads * opening).astype(jnp.bfloat16).reshape(token_count, local_heads * HV)
    )
    partial_value = jnp.dot(gated_rows, output_weight, preferred_element_type=jnp.float32)
    half_rows = token_count // lax.axis_size("hid")
    row_start = lax.axis_index("hid") * half_rows
    own_value = partial_value.astype(jnp.bfloat16)
    mixed_sum = own_value.astype(jnp.float32) + from_partner(own_value, token_count, 0).astype(
        jnp.float32
    )
    residual = (tokens.astype(jnp.float32) + mixed_sum).astype(jnp.bfloat16)
    feed_in = rms_scaled(residual, mixer_gain).astype(jnp.bfloat16)
    own_residual = lax.dynamic_slice_in_dim(residual, row_start, half_rows, 0)

    seq_count = lax.axis_size("seq")

    def gather_rows(weight_block):
        quarter = weight_block.shape[0] // seq_count
        own = lax.dynamic_slice_in_dim(weight_block, seq_index * quarter, quarter, 0)
        return lax.all_gather(own, ("req", "seq"), axis=0, tiled=True)

    def widen(weight_rows):
        return jnp.dot(feed_in, weight_rows, preferred_element_type=jnp.float32)

    gate_part = widen(gather_rows(gate_weight))
    up_part = widen(gather_rows(up_weight))
    hidden = (jax.nn.silu(gate_part) * up_part).astype(jnp.bfloat16)
    down_quarters = gather_rows(down_weight.reshape(seq_count, -1, down_weight.shape[1]))
    down_columns = down_quarters.reshape(
        lax.axis_size("req"), seq_count, -1, down_weight.shape[1]
    ).transpose(1, 2, 0, 3).reshape(down_weight.shape[0], -1)
    partials = jnp.dot(hidden, down_columns, preferred_element_type=jnp.float32)
    own_partials = partials.astype(jnp.bfloat16)
    feed_sum = lax.dynamic_slice_in_dim(own_partials, row_start, half_rows, 0).astype(
        jnp.float32
    ) + from_partner(own_partials, half_rows, 1).astype(jnp.float32)
    result = (own_residual.astype(jnp.float32) + feed_sum).astype(jnp.bfloat16)
    return (result, memories.astype(jnp.bfloat16), by_page[:, PAGE - rim_rows :])


def solution(mesh):
    return jax.shard_map(
        on_device,
        mesh=mesh,
        in_specs=(
            P(("req", "seq"), None),
            P(),
            P(None, "hid"),
            P(None, "hid"),
            P(),
            P(None, "hid"),
            P("hid"),
            P(None, "hid"),
            P(),
            P("hid", None),
            P(),
            P("req", "hid"),
            P("req", "hid"),
            P("hid", "req"),
            P("req", None),
            P("req", None),
        ),
        out_specs=(
            P(("req", "seq", "hid"), None),
            P(("req", "seq"), "hid", None, None),
            P(("req", "seq"), None, "hid"),
        ),
        check_vma=False,
    )
```

```python
import functools

import jax
import jax.numpy as jnp
from jax import lax
from jax.sharding import PartitionSpec as P
from jax.experimental import pallas as pl
from jax.experimental.pallas import tpu as pltpu

HK = 256
HV = 512
KCONV = 4
PAGE = 64
CONVW = 1024


EPSILON = 1e-06
TOP_PRECISION = lax.Precision.HIGHEST


def shifted(value, axis, steps):
    count = lax.axis_size(axis)
    first, last = (max(0, -steps), min(count, count - steps))
    return lax.ppermute(value, axis, [(source, source + steps) for source in range(first, last)])


def prefix_2(array, axis, join, neutral):
    place = lax.axis_index(axis)
    decay, memory = array
    width = memory.shape[-1]
    packed = jnp.concatenate(
        [memory.reshape(-1, width), jnp.pad(decay.reshape(1, -1), ((0, 0), (0, width - decay.size)))],
        axis=0,
    ).astype(jnp.bfloat16)
    received = spread_over_seq(packed)
    gathered = (
        received[:, -1, : decay.size].reshape((-1,) + decay.shape),
        received[:, :-1].reshape((-1,) + memory.shape),
    )
    state = jax.tree.map(lambda a, e: jnp.zeros_like(a) + jnp.asarray(e, a.dtype), array, neutral)

    def one(lap, state):
        return join(
            state,
            jax.tree.map(
                lambda a, own: lax.dynamic_index_in_dim(a, lap, 0, False).astype(own.dtype),
                gathered,
                array,
            ),
        )

    return lax.fori_loop(0, place, one, state)


def partner_kernel(rows, src_ref, dst_ref, send_sem, recv_sem):
    partner = 1 - lax.axis_index("hid")
    barrier = pltpu.get_barrier_semaphore()
    pl.semaphore_signal(
        barrier, inc=1, device_id={"hid": partner}, device_id_type=pl.DeviceIdType.MESH
    )
    pl.semaphore_wait(barrier, 1)
    start = pl.multiple_of(partner * rows, rows) if rows < src_ref.shape[0] else 0
    copy = pltpu.make_async_remote_copy(
        src_ref=src_ref.at[pl.ds(start, rows)],
        dst_ref=dst_ref,
        send_sem=send_sem,
        recv_sem=recv_sem,
        device_id={"hid": partner},
        device_id_type=pl.DeviceIdType.MESH,
    )
    copy.start()
    copy.wait()


def from_partner(value, rows, kernel_id):
    return pl.pallas_call(
        functools.partial(partner_kernel, rows),
        out_shape=jax.ShapeDtypeStruct((rows,) + value.shape[1:], value.dtype),
        in_specs=[pl.BlockSpec(memory_space=pl.ANY)],
        out_specs=pl.BlockSpec(memory_space=pl.ANY),
        scratch_shapes=[pltpu.SemaphoreType.DMA, pltpu.SemaphoreType.DMA],
        compiler_params=pltpu.CompilerParams(collective_id=kernel_id, has_side_effects=True),
    )(value)


def spread_kernel(src_ref, dst_ref, send_sem, recv_sem):
    count = lax.axis_size("seq")
    me = lax.axis_index("seq")
    barrier = pltpu.get_barrier_semaphore()
    for step in range(1, count):
        pl.semaphore_signal(
            barrier,
            inc=1,
            device_id={"seq": lax.rem(me + step, count)},
            device_id_type=pl.DeviceIdType.MESH,
        )
    pl.semaphore_wait(barrier, count - 1)
    copies = []
    for step in range(1, count):
        copy = pltpu.make_async_remote_copy(
            src_ref=src_ref,
            dst_ref=dst_ref.at[me],
            send_sem=send_sem.at[step - 1],
            recv_sem=recv_sem.at[me],
            device_id={"seq": jnp.minimum(me + step, count - 1)},
            device_id_type=pl.DeviceIdType.MESH,
        )
        copies.append(copy)

        @pl.when(me + step < count)
        def _():
            copy.start()

    for step, copy in zip(range(1, count), copies):

        @pl.when(me + step < count)
        def _():
            copy.wait_send()

    for step in range(1, count):
        source = jnp.maximum(me - step, 0)

        @pl.when(me - step >= 0)
        def _():
            pltpu.make_async_remote_copy(
                src_ref=src_ref,
                dst_ref=dst_ref.at[source],
                send_sem=send_sem.at[step - 1],
                recv_sem=recv_sem.at[source],
                device_id={"seq": source},
                device_id_type=pl.DeviceIdType.MESH,
            ).wait_recv()


def spread_over_seq(value):
    count = lax.axis_size("seq")
    return pl.pallas_call(
        spread_kernel,
        out_shape=jax.ShapeDtypeStruct((count,) + value.shape, value.dtype),
        in_specs=[pl.BlockSpec(memory_space=pl.ANY)],
        out_specs=pl.BlockSpec(memory_space=pl.ANY),
        scratch_shapes=[
            pltpu.SemaphoreType.DMA((count - 1,)),
            pltpu.SemaphoreType.DMA((count,)),
        ],
        compiler_params=pltpu.CompilerParams(collective_id=2, has_side_effects=True),
    )(value)


def rms_scaled(values, scale_gain):
    values = values.astype(jnp.float32)
    return (
        values
        * lax.rsqrt(jnp.mean(values * values, axis=-1, keepdims=True) + EPSILON)
        * scale_gain.astype(jnp.float32)
    )


def page_segments(page_counts, starts, total_pages):
    position = jnp.arange(total_pages, dtype=jnp.int32)
    inside = (position[None, :] >= starts[:, None]) & (
        position[None, :] < starts[:, None] + page_counts[:, None]
    )
    labels = jnp.arange(1, page_counts.shape[0] + 1, dtype=jnp.int32)
    segment = jnp.sum(jnp.where(inside, labels[:, None], 0), axis=0) - 1
    earlier = jnp.concatenate([jnp.full((1,), -1, jnp.int32), segment[:-1]])
    return ((segment == earlier) & (segment >= 0)).astype(jnp.float32)


def short_conv(by_page, before, carried, conv_taps):
    kept_rows = before.astype(jnp.float32) * carried[:, None, None]
    widened = jnp.concatenate([kept_rows, by_page.astype(jnp.float32)], axis=1)
    tap_count = conv_taps.shape[0]
    length = by_page.shape[1]
    result = jnp.zeros(by_page.shape, jnp.float32)
    for offset in range(tap_count):
        result = (
            result
            + conv_taps[offset].astype(jnp.float32)
            * widened[:, tap_count - 1 - offset : tap_count - 1 - offset + length]
        )
    return result


def split_features(mixed_rows, key_width):
    query_rows = jax.nn.silu(mixed_rows[..., :key_width])
    key_rows = jax.nn.silu(mixed_rows[..., key_width : 2 * key_width]) * key_width ** (-0.5)
    value_matrix = mixed_rows[..., 2 * key_width :]
    return (
        query_rows.transpose(0, 2, 1, 3),
        key_rows.transpose(0, 2, 1, 3),
        value_matrix.transpose(0, 2, 1, 3),
    )


def page_block(query_rows, key_rows, value_matrix, decay_sum, carried):
    length = query_rows.shape[2]
    page_count = query_rows.shape[0]
    raised_rows = query_rows * jnp.exp(decay_sum)
    lowered = key_rows * jnp.exp(-decay_sum)
    scores = jnp.einsum("phik,phjk->phij", raised_rows, lowered, precision=TOP_PRECISION)
    rows_index = jnp.arange(length)
    causal = rows_index[:, None] >= rows_index[None, :]
    scores = jnp.where(causal[None, None], scores, 0.0)
    layer_output = jnp.einsum("phij,phjv->phiv", scores, value_matrix, precision=TOP_PRECISION)
    closing_sum = decay_sum[:, :, -1, :]
    weighted_rows = key_rows * jnp.exp(closing_sum[:, :, None, :] - decay_sum)
    page_terms = jnp.einsum(
        "phte,phtb->pheb", weighted_rows, value_matrix, precision=TOP_PRECISION
    )
    through = jnp.cumsum(closing_sum, axis=0)
    resets = jnp.cumsum(1.0 - carried)
    pages = jnp.arange(page_count)
    valid = (pages[:, None] >= pages[None, :]) & (resets[:, None] == resets[None, :])
    spread = through[:, None] - through[None, :]
    spread = jnp.where(valid[:, :, None, None], spread, 0.0)
    weights = jnp.where(valid[:, :, None, None], jnp.exp(spread), 0.0)
    memories = jnp.einsum("pqhe,qheb->pheb", weights, page_terms, precision=TOP_PRECISION)
    previous = jnp.concatenate([jnp.zeros_like(memories[:1]), memories[:-1]], axis=0)
    previous = previous * carried[:, None, None, None]
    layer_output = layer_output + jnp.einsum(
        "phik,phkv->phiv", raised_rows, previous, precision=TOP_PRECISION
    )
    return memories[-1], layer_output, memories


def on_device(
    tokens,
    attention_gain,
    project_weight,
    conv_weight,
    decay_down,
    decay_up,
    decay_bias,
    output_gate,
    head_gain,
    output_weight,
    mixer_gain,
    gate_weight,
    up_weight,
    down_weight,
    prompt_pages,
    prompt_start,
):
    token_count = tokens.shape[0]
    page_count = token_count // PAGE
    local_heads = project_weight.shape[1] // CONVW
    rim_rows = KCONV - 1
    seq_index = lax.axis_index("seq")
    group_pages = page_count * lax.axis_size("seq")
    page_flags = page_segments(prompt_pages[0], prompt_start[0], group_pages)
    carried = lax.dynamic_slice_in_dim(page_flags, seq_index * page_count, page_count)
    normed = rms_scaled(tokens, attention_gain).astype(jnp.bfloat16)
    projected = jnp.dot(normed, project_weight, preferred_element_type=jnp.float32).astype(
        jnp.bfloat16
    )
    by_page = projected.reshape(page_count, PAGE, local_heads * CONVW)
    incoming = shifted(by_page[-1, PAGE - rim_rows :], "seq", 1)
    before = jnp.concatenate([incoming[None], by_page[:-1, PAGE - rim_rows :]], axis=0)
    mixed_rows = short_conv(by_page, before, carried, conv_weight).reshape(
        page_count, PAGE, local_heads, CONVW
    )
    query_rows, key_rows, value_matrix = split_features(mixed_rows, HK)
    lowrank = jnp.dot(normed, decay_down, preferred_element_type=jnp.float32).astype(jnp.bfloat16)
    decay_log = (
        jax.nn.log_sigmoid(
            jnp.dot(lowrank, decay_up, preferred_element_type=jnp.float32) + decay_bias
        )
        / 16.0
    )
    decay_log = decay_log.reshape(page_count, PAGE, local_heads, HK).transpose(0, 2, 1, 3)
    decay_sum = jnp.cumsum(decay_log, axis=2)
    local_memory, outputs, memories = page_block(
        query_rows, key_rows, value_matrix, decay_sum, carried
    )
    totals = decay_sum[:, :, -1, :]
    through = jnp.cumsum(totals, axis=0)
    alive_mask = jnp.cumprod(carried)
    block_decay = alive_mask[-1] * jnp.exp(through[-1])

    def compose(earlier, latter):
        return (earlier[0] * latter[0], latter[0][..., None] * earlier[1] + latter[1])

    prefix = prefix_2(
        (block_decay, local_memory),
        "seq",
        compose,
        (jnp.ones_like(block_decay), jnp.zeros_like(local_memory)),
    )
    incoming_state = prefix[1]
    before_sum = through - totals
    extent_factor = alive_mask[:, None, None, None] * jnp.exp(decay_sum + before_sum[:, :, None, :])
    outputs = outputs + jnp.einsum(
        "dlof,lfg->dlog", query_rows * extent_factor, incoming_state, precision=TOP_PRECISION
    )
    memories = (
        memories + (alive_mask[:, None, None] * jnp.exp(through))[..., None] * incoming_state[None]
    )
    attended = outputs.transpose(0, 2, 1, 3).reshape(token_count, local_heads, HV)
    normed_heads = rms_scaled(attended, head_gain)
    opening = jax.nn.silu(jnp.dot(normed, output_gate, preferred_element_type=jnp.float32)).reshape(
        token_count, local_heads, HV
    )
    gated_rows = (
        (normed_heads * opening).astype(jnp.bfloat16).reshape(token_count, local_heads * HV)
    )
    partial_value = jnp.dot(gated_rows, output_weight, preferred_element_type=jnp.float32)
    half_rows = token_count // lax.axis_size("hid")
    row_start = lax.axis_index("hid") * half_rows
    own_value = partial_value.astype(jnp.bfloat16)
    mixed_sum = own_value.astype(jnp.float32) + from_partner(own_value, token_count, 0).astype(
        jnp.float32
    )
    residual = (tokens.astype(jnp.float32) + mixed_sum).astype(jnp.bfloat16)
    feed_in = rms_scaled(residual, mixer_gain).astype(jnp.bfloat16)
    own_residual = lax.dynamic_slice_in_dim(residual, row_start, half_rows, 0)

    def widen(weight_rows):
        return jnp.dot(feed_in, weight_rows, preferred_element_type=jnp.float32)

    gate_part = widen(lax.all_gather(gate_weight, "req", axis=0, tiled=True))
    up_part = widen(lax.all_gather(up_weight, "req", axis=0, tiled=True))
    hidden = lax.optimization_barrier((jax.nn.silu(gate_part) * up_part).astype(jnp.bfloat16))
    partials = jnp.dot(
        hidden,
        lax.all_gather(down_weight, "req", axis=1, tiled=True),
        preferred_element_type=jnp.float32,
    )
    own_partials = partials.astype(jnp.bfloat16)
    feed_sum = lax.dynamic_slice_in_dim(own_partials, row_start, half_rows, 0).astype(
        jnp.float32
    ) + from_partner(own_partials, half_rows, 1).astype(jnp.float32)
    result = (own_residual.astype(jnp.float32) + feed_sum).astype(jnp.bfloat16)
    return (result, memories.astype(jnp.bfloat16), by_page[:, PAGE - rim_rows :])


def solution(mesh):
    return jax.shard_map(
        on_device,
        mesh=mesh,
        in_specs=(
            P(("req", "seq"), None),
            P(),
            P(None, "hid"),
            P(None, "hid"),
            P(),
            P(None, "hid"),
            P("hid"),
            P(None, "hid"),
            P(),
            P("hid", None),
            P(),
            P("req", "hid"),
            P("req", "hid"),
            P("hid", "req"),
            P("req", None),
            P("req", None),
        ),
        out_specs=(
            P(("req", "seq", "hid"), None),
            P(("req", "seq"), "hid", None, None),
            P(("req", "seq"), None, "hid"),
        ),
        check_vma=False,
    )
```

```python
import functools

import jax
import jax.numpy as jnp
from jax import lax
from jax.sharding import PartitionSpec as P
from jax.experimental import pallas as pl
from jax.experimental.pallas import tpu as pltpu

HK = 256
HV = 512
KCONV = 4
PAGE = 64
CONVW = 1024


EPSILON = 1e-06
TOP_PRECISION = lax.Precision.HIGHEST


def shifted(value, axis, steps):
    count = lax.axis_size(axis)
    first, last = (max(0, -steps), min(count, count - steps))
    return lax.ppermute(value, axis, [(source, source + steps) for source in range(first, last)])


def prefix_2(array, axis, join, neutral):
    place = lax.axis_index(axis)
    decay, memory = array
    width = memory.shape[-1]
    packed = jnp.concatenate(
        [memory.reshape(-1, width), jnp.pad(decay.reshape(1, -1), ((0, 0), (0, width - decay.size)))],
        axis=0,
    ).astype(jnp.bfloat16)
    received = spread_over_seq(packed)
    gathered = (
        received[:, -1, : decay.size].reshape((-1,) + decay.shape),
        received[:, :-1].reshape((-1,) + memory.shape),
    )
    state = jax.tree.map(lambda a, e: jnp.zeros_like(a) + jnp.asarray(e, a.dtype), array, neutral)

    def one(lap, state):
        return join(
            state,
            jax.tree.map(
                lambda a, own: lax.dynamic_index_in_dim(a, lap, 0, False).astype(own.dtype),
                gathered,
                array,
            ),
        )

    return lax.fori_loop(0, place, one, state)


def partner_kernel(rows, src_ref, dst_ref, send_sem, recv_sem):
    partner = 1 - lax.axis_index("hid")
    barrier = pltpu.get_barrier_semaphore()
    pl.semaphore_signal(
        barrier, inc=1, device_id={"hid": partner}, device_id_type=pl.DeviceIdType.MESH
    )
    pl.semaphore_wait(barrier, 1)
    start = pl.multiple_of(partner * rows, rows) if rows < src_ref.shape[0] else 0
    copy = pltpu.make_async_remote_copy(
        src_ref=src_ref.at[pl.ds(start, rows)],
        dst_ref=dst_ref,
        send_sem=send_sem,
        recv_sem=recv_sem,
        device_id={"hid": partner},
        device_id_type=pl.DeviceIdType.MESH,
    )
    copy.start()
    copy.wait()


def from_partner(value, rows, kernel_id):
    return pl.pallas_call(
        functools.partial(partner_kernel, rows),
        out_shape=jax.ShapeDtypeStruct((rows,) + value.shape[1:], value.dtype),
        in_specs=[pl.BlockSpec(memory_space=pl.ANY)],
        out_specs=pl.BlockSpec(memory_space=pl.ANY),
        scratch_shapes=[pltpu.SemaphoreType.DMA, pltpu.SemaphoreType.DMA],
        compiler_params=pltpu.CompilerParams(collective_id=kernel_id, has_side_effects=True),
    )(value)


def spread_kernel(src_ref, dst_ref, send_sem, recv_sem):
    count = lax.axis_size("seq")
    me = lax.axis_index("seq")
    barrier = pltpu.get_barrier_semaphore()
    for step in range(1, count):
        pl.semaphore_signal(
            barrier,
            inc=1,
            device_id={"seq": lax.rem(me + step, count)},
            device_id_type=pl.DeviceIdType.MESH,
        )
    pl.semaphore_wait(barrier, count - 1)
    copies = []
    for step in range(1, count):
        copy = pltpu.make_async_remote_copy(
            src_ref=src_ref,
            dst_ref=dst_ref.at[me],
            send_sem=send_sem.at[step - 1],
            recv_sem=recv_sem.at[me],
            device_id={"seq": jnp.minimum(me + step, count - 1)},
            device_id_type=pl.DeviceIdType.MESH,
        )
        copies.append(copy)

        @pl.when(me + step < count)
        def _():
            copy.start()

    for step, copy in zip(range(1, count), copies):

        @pl.when(me + step < count)
        def _():
            copy.wait_send()

    for step in range(1, count):
        source = jnp.maximum(me - step, 0)

        @pl.when(me - step >= 0)
        def _():
            pltpu.make_async_remote_copy(
                src_ref=src_ref,
                dst_ref=dst_ref.at[source],
                send_sem=send_sem.at[step - 1],
                recv_sem=recv_sem.at[source],
                device_id={"seq": source},
                device_id_type=pl.DeviceIdType.MESH,
            ).wait_recv()


def spread_over_seq(value):
    count = lax.axis_size("seq")
    return pl.pallas_call(
        spread_kernel,
        out_shape=jax.ShapeDtypeStruct((count,) + value.shape, value.dtype),
        in_specs=[pl.BlockSpec(memory_space=pl.ANY)],
        out_specs=pl.BlockSpec(memory_space=pl.ANY),
        scratch_shapes=[
            pltpu.SemaphoreType.DMA((count - 1,)),
            pltpu.SemaphoreType.DMA((count,)),
        ],
        compiler_params=pltpu.CompilerParams(collective_id=2, has_side_effects=True),
    )(value)


def rms_scaled(values, scale_gain):
    values = values.astype(jnp.float32)
    return (
        values
        * lax.rsqrt(jnp.mean(values * values, axis=-1, keepdims=True) + EPSILON)
        * scale_gain.astype(jnp.float32)
    )


def page_segments(page_counts, starts, total_pages):
    position = jnp.arange(total_pages, dtype=jnp.int32)
    inside = (position[None, :] >= starts[:, None]) & (
        position[None, :] < starts[:, None] + page_counts[:, None]
    )
    labels = jnp.arange(1, page_counts.shape[0] + 1, dtype=jnp.int32)
    segment = jnp.sum(jnp.where(inside, labels[:, None], 0), axis=0) - 1
    earlier = jnp.concatenate([jnp.full((1,), -1, jnp.int32), segment[:-1]])
    return ((segment == earlier) & (segment >= 0)).astype(jnp.float32)


def short_conv(by_page, before, carried, conv_taps):
    kept_rows = before.astype(jnp.float32) * carried[:, None, None]
    widened = jnp.concatenate([kept_rows, by_page.astype(jnp.float32)], axis=1)
    tap_count = conv_taps.shape[0]
    length = by_page.shape[1]
    result = jnp.zeros(by_page.shape, jnp.float32)
    for offset in range(tap_count):
        result = (
            result
            + conv_taps[offset].astype(jnp.float32)
            * widened[:, tap_count - 1 - offset : tap_count - 1 - offset + length]
        )
    return result


def split_features(mixed_rows, key_width):
    query_rows = jax.nn.silu(mixed_rows[..., :key_width])
    key_rows = jax.nn.silu(mixed_rows[..., key_width : 2 * key_width]) * key_width ** (-0.5)
    value_matrix = mixed_rows[..., 2 * key_width :]
    return (
        query_rows.transpose(0, 2, 1, 3),
        key_rows.transpose(0, 2, 1, 3),
        value_matrix.transpose(0, 2, 1, 3),
    )


def page_block(query_rows, key_rows, value_matrix, decay_sum, carried):
    length = query_rows.shape[2]
    page_count = query_rows.shape[0]
    raised_rows = query_rows * jnp.exp(decay_sum)
    lowered = key_rows * jnp.exp(-decay_sum)
    scores = jnp.einsum("phik,phjk->phij", raised_rows, lowered, precision=TOP_PRECISION)
    rows_index = jnp.arange(length)
    causal = rows_index[:, None] >= rows_index[None, :]
    scores = jnp.where(causal[None, None], scores, 0.0)
    layer_output = jnp.einsum("phij,phjv->phiv", scores, value_matrix, precision=TOP_PRECISION)
    closing_sum = decay_sum[:, :, -1, :]
    weighted_rows = key_rows * jnp.exp(closing_sum[:, :, None, :] - decay_sum)
    page_terms = jnp.einsum(
        "phte,phtb->pheb", weighted_rows, value_matrix, precision=TOP_PRECISION
    )
    page_decay = jnp.exp(closing_sum) * carried[:, None, None]
    state = page_terms[0]
    states = [state]
    for page in range(1, page_count):
        state = page_decay[page][..., None] * state + page_terms[page]
        states.append(state)
    memories = jnp.stack(states)
    previous = jnp.concatenate([jnp.zeros_like(memories[:1]), memories[:-1]], axis=0)
    previous = previous * carried[:, None, None, None]
    layer_output = layer_output + jnp.einsum(
        "phik,phkv->phiv", raised_rows, previous, precision=TOP_PRECISION
    )
    return memories[-1], layer_output, memories


def on_device(
    tokens,
    attention_gain,
    project_weight,
    conv_weight,
    decay_down,
    decay_up,
    decay_bias,
    output_gate,
    head_gain,
    output_weight,
    mixer_gain,
    gate_weight,
    up_weight,
    down_weight,
    prompt_pages,
    prompt_start,
):
    token_count = tokens.shape[0]
    page_count = token_count // PAGE
    local_heads = project_weight.shape[1] // CONVW
    rim_rows = KCONV - 1
    seq_index = lax.axis_index("seq")
    group_pages = page_count * lax.axis_size("seq")
    page_flags = page_segments(prompt_pages[0], prompt_start[0], group_pages)
    carried = lax.dynamic_slice_in_dim(page_flags, seq_index * page_count, page_count)
    normed = rms_scaled(tokens, attention_gain).astype(jnp.bfloat16)
    projected = jnp.dot(normed, project_weight, preferred_element_type=jnp.float32).astype(
        jnp.bfloat16
    )
    by_page = projected.reshape(page_count, PAGE, local_heads * CONVW)
    incoming = shifted(by_page[-1, PAGE - rim_rows :], "seq", 1)
    before = jnp.concatenate([incoming[None], by_page[:-1, PAGE - rim_rows :]], axis=0)
    mixed_rows = short_conv(by_page, before, carried, conv_weight).reshape(
        page_count, PAGE, local_heads, CONVW
    )
    query_rows, key_rows, value_matrix = split_features(mixed_rows, HK)
    lowrank = jnp.dot(normed, decay_down, preferred_element_type=jnp.float32).astype(jnp.bfloat16)
    decay_log = (
        jax.nn.log_sigmoid(
            jnp.dot(lowrank, decay_up, preferred_element_type=jnp.float32) + decay_bias
        )
        / 16.0
    )
    decay_log = decay_log.reshape(page_count, PAGE, local_heads, HK).transpose(0, 2, 1, 3)
    decay_sum = jnp.cumsum(decay_log, axis=2)
    local_memory, outputs, memories = page_block(
        query_rows, key_rows, value_matrix, decay_sum, carried
    )
    totals = decay_sum[:, :, -1, :]
    through = jnp.cumsum(totals, axis=0)
    alive_mask = jnp.cumprod(carried)
    block_decay = alive_mask[-1] * jnp.exp(through[-1])

    def compose(earlier, latter):
        return (earlier[0] * latter[0], latter[0][..., None] * earlier[1] + latter[1])

    prefix = prefix_2(
        (block_decay, local_memory),
        "seq",
        compose,
        (jnp.ones_like(block_decay), jnp.zeros_like(local_memory)),
    )
    incoming_state = prefix[1]
    before_sum = through - totals
    extent_factor = alive_mask[:, None, None, None] * jnp.exp(decay_sum + before_sum[:, :, None, :])
    outputs = outputs + jnp.einsum(
        "dlof,lfg->dlog", query_rows * extent_factor, incoming_state, precision=TOP_PRECISION
    )
    memories = (
        memories + (alive_mask[:, None, None] * jnp.exp(through))[..., None] * incoming_state[None]
    )
    attended = outputs.transpose(0, 2, 1, 3).reshape(token_count, local_heads, HV)
    normed_heads = rms_scaled(attended, head_gain)
    opening = jax.nn.silu(jnp.dot(normed, output_gate, preferred_element_type=jnp.float32)).reshape(
        token_count, local_heads, HV
    )
    gated_rows = (
        (normed_heads * opening).astype(jnp.bfloat16).reshape(token_count, local_heads * HV)
    )
    partial_value = jnp.dot(gated_rows, output_weight, preferred_element_type=jnp.float32)
    half_rows = token_count // lax.axis_size("hid")
    row_start = lax.axis_index("hid") * half_rows
    own_value = partial_value.astype(jnp.bfloat16)
    mixed_sum = own_value.astype(jnp.float32) + from_partner(own_value, token_count, 0).astype(
        jnp.float32
    )
    residual = (tokens.astype(jnp.float32) + mixed_sum).astype(jnp.bfloat16)
    feed_in = rms_scaled(residual, mixer_gain).astype(jnp.bfloat16)
    own_residual = lax.dynamic_slice_in_dim(residual, row_start, half_rows, 0)

    def widen(weight_rows):
        return jnp.dot(feed_in, weight_rows, preferred_element_type=jnp.float32)

    gate_part = widen(lax.all_gather(gate_weight, "req", axis=0, tiled=True))
    up_part = widen(lax.all_gather(up_weight, "req", axis=0, tiled=True))
    hidden = lax.optimization_barrier((jax.nn.silu(gate_part) * up_part).astype(jnp.bfloat16))
    partials = jnp.dot(
        hidden,
        lax.all_gather(down_weight, "req", axis=1, tiled=True),
        preferred_element_type=jnp.float32,
    )
    own_partials = partials.astype(jnp.bfloat16)
    feed_sum = lax.dynamic_slice_in_dim(own_partials, row_start, half_rows, 0).astype(
        jnp.float32
    ) + from_partner(own_partials, half_rows, 1).astype(jnp.float32)
    result = (own_residual.astype(jnp.float32) + feed_sum).astype(jnp.bfloat16)
    return (result, memories.astype(jnp.bfloat16), by_page[:, PAGE - rim_rows :])


def solution(mesh):
    return jax.shard_map(
        on_device,
        mesh=mesh,
        in_specs=(
            P(("req", "seq"), None),
            P(),
            P(None, "hid"),
            P(None, "hid"),
            P(),
            P(None, "hid"),
            P("hid"),
            P(None, "hid"),
            P(),
            P("hid", None),
            P(),
            P("req", "hid"),
            P("req", "hid"),
            P("hid", "req"),
            P("req", None),
            P("req", None),
        ),
        out_specs=(
            P(("req", "seq", "hid"), None),
            P(("req", "seq"), "hid", None, None),
            P(("req", "seq"), None, "hid"),
        ),
        check_vma=False,
    )
```

```python
import functools

import jax
import jax.numpy as jnp
from jax import lax
from jax.sharding import PartitionSpec as P
from jax.experimental import pallas as pl
from jax.experimental.pallas import tpu as pltpu

HK = 256
HV = 512
KCONV = 4
PAGE = 64
CONVW = 1024


EPSILON = 1e-06
TOP_PRECISION = lax.Precision.HIGHEST


def shifted(value, axis, steps):
    count = lax.axis_size(axis)
    first, last = (max(0, -steps), min(count, count - steps))
    return lax.ppermute(value, axis, [(source, source + steps) for source in range(first, last)])


def prefix_2(array, axis, join, neutral):
    place = lax.axis_index(axis)
    decay, memory = array
    width = memory.shape[-1]
    packed = jnp.concatenate(
        [memory.reshape(-1, width), jnp.pad(decay.reshape(1, -1), ((0, 0), (0, width - decay.size)))],
        axis=0,
    ).astype(jnp.bfloat16)
    received = spread_over_seq(packed)
    gathered = (
        received[:, -1, : decay.size].reshape((-1,) + decay.shape),
        received[:, :-1].reshape((-1,) + memory.shape),
    )
    state = jax.tree.map(lambda a, e: jnp.zeros_like(a) + jnp.asarray(e, a.dtype), array, neutral)

    def one(lap, state):
        return join(
            state,
            jax.tree.map(
                lambda a, own: lax.dynamic_index_in_dim(a, lap, 0, False).astype(own.dtype),
                gathered,
                array,
            ),
        )

    return lax.fori_loop(0, place, one, state)


def partner_kernel(rows, src_ref, dst_ref, send_sem, recv_sem):
    partner = 1 - lax.axis_index("hid")
    barrier = pltpu.get_barrier_semaphore()
    pl.semaphore_signal(
        barrier, inc=1, device_id={"hid": partner}, device_id_type=pl.DeviceIdType.MESH
    )
    pl.semaphore_wait(barrier, 1)
    start = pl.multiple_of(partner * rows, rows) if rows < src_ref.shape[0] else 0
    copy = pltpu.make_async_remote_copy(
        src_ref=src_ref.at[pl.ds(start, rows)],
        dst_ref=dst_ref,
        send_sem=send_sem,
        recv_sem=recv_sem,
        device_id={"hid": partner},
        device_id_type=pl.DeviceIdType.MESH,
    )
    copy.start()
    copy.wait()


def from_partner(value, rows, kernel_id):
    return pl.pallas_call(
        functools.partial(partner_kernel, rows),
        out_shape=jax.ShapeDtypeStruct((rows,) + value.shape[1:], value.dtype),
        in_specs=[pl.BlockSpec(memory_space=pl.ANY)],
        out_specs=pl.BlockSpec(memory_space=pl.ANY),
        scratch_shapes=[pltpu.SemaphoreType.DMA, pltpu.SemaphoreType.DMA],
        compiler_params=pltpu.CompilerParams(collective_id=kernel_id, has_side_effects=True),
    )(value)


def spread_kernel(src_ref, dst_ref, send_sem, recv_sem):
    count = lax.axis_size("seq")
    me = lax.axis_index("seq")
    barrier = pltpu.get_barrier_semaphore()
    for step in range(1, count):
        pl.semaphore_signal(
            barrier,
            inc=1,
            device_id={"seq": lax.rem(me + step, count)},
            device_id_type=pl.DeviceIdType.MESH,
        )
    pl.semaphore_wait(barrier, count - 1)
    copies = []
    for step in range(1, count):
        copy = pltpu.make_async_remote_copy(
            src_ref=src_ref,
            dst_ref=dst_ref.at[me],
            send_sem=send_sem.at[step - 1],
            recv_sem=recv_sem.at[me],
            device_id={"seq": jnp.minimum(me + step, count - 1)},
            device_id_type=pl.DeviceIdType.MESH,
        )
        copies.append(copy)

        @pl.when(me + step < count)
        def _():
            copy.start()

    for step, copy in zip(range(1, count), copies):

        @pl.when(me + step < count)
        def _():
            copy.wait_send()

    for step in range(1, count):
        source = jnp.maximum(me - step, 0)

        @pl.when(me - step >= 0)
        def _():
            pltpu.make_async_remote_copy(
                src_ref=src_ref,
                dst_ref=dst_ref.at[source],
                send_sem=send_sem.at[step - 1],
                recv_sem=recv_sem.at[source],
                device_id={"seq": source},
                device_id_type=pl.DeviceIdType.MESH,
            ).wait_recv()


def spread_over_seq(value):
    count = lax.axis_size("seq")
    return pl.pallas_call(
        spread_kernel,
        out_shape=jax.ShapeDtypeStruct((count,) + value.shape, value.dtype),
        in_specs=[pl.BlockSpec(memory_space=pl.ANY)],
        out_specs=pl.BlockSpec(memory_space=pl.ANY),
        scratch_shapes=[
            pltpu.SemaphoreType.DMA((count - 1,)),
            pltpu.SemaphoreType.DMA((count,)),
        ],
        compiler_params=pltpu.CompilerParams(collective_id=2, has_side_effects=True),
    )(value)


def rms_scaled(values, scale_gain):
    values = values.astype(jnp.float32)
    return (
        values
        * lax.rsqrt(jnp.mean(values * values, axis=-1, keepdims=True) + EPSILON)
        * scale_gain.astype(jnp.float32)
    )


def page_segments(page_counts, starts, total_pages):
    position = jnp.arange(total_pages, dtype=jnp.int32)
    inside = (position[None, :] >= starts[:, None]) & (
        position[None, :] < starts[:, None] + page_counts[:, None]
    )
    labels = jnp.arange(1, page_counts.shape[0] + 1, dtype=jnp.int32)
    segment = jnp.sum(jnp.where(inside, labels[:, None], 0), axis=0) - 1
    earlier = jnp.concatenate([jnp.full((1,), -1, jnp.int32), segment[:-1]])
    return ((segment == earlier) & (segment >= 0)).astype(jnp.float32)


def short_conv(by_page, before, carried, conv_taps):
    kept_rows = before.astype(jnp.float32) * carried[:, None, None]
    widened = jnp.concatenate([kept_rows, by_page.astype(jnp.float32)], axis=1)
    tap_count = conv_taps.shape[0]
    length = by_page.shape[1]
    result = jnp.zeros(by_page.shape, jnp.float32)
    for offset in range(tap_count):
        result = (
            result
            + conv_taps[offset].astype(jnp.float32)
            * widened[:, tap_count - 1 - offset : tap_count - 1 - offset + length]
        )
    return result


def split_features(mixed_rows, key_width):
    query_rows = jax.nn.silu(mixed_rows[..., :key_width])
    key_rows = jax.nn.silu(mixed_rows[..., key_width : 2 * key_width]) * key_width ** (-0.5)
    value_matrix = mixed_rows[..., 2 * key_width :]
    return (
        query_rows.transpose(0, 2, 1, 3),
        key_rows.transpose(0, 2, 1, 3),
        value_matrix.transpose(0, 2, 1, 3),
    )


def page_block(query_rows, key_rows, value_matrix, decay_sum, carried):
    length = query_rows.shape[2]
    page_count = query_rows.shape[0]
    raised_rows = query_rows * jnp.exp(decay_sum)
    lowered = key_rows * jnp.exp(-decay_sum)
    scores = jnp.einsum("phik,phjk->phij", raised_rows, lowered, precision=TOP_PRECISION)
    rows_index = jnp.arange(length)
    causal = rows_index[:, None] >= rows_index[None, :]
    scores = jnp.where(causal[None, None], scores, 0.0)
    layer_output = jnp.einsum("phij,phjv->phiv", scores, value_matrix, precision=TOP_PRECISION)
    closing_sum = decay_sum[:, :, -1, :]
    weighted_rows = key_rows * jnp.exp(closing_sum[:, :, None, :] - decay_sum)
    page_terms = jnp.einsum(
        "phte,phtb->pheb", weighted_rows, value_matrix, precision=TOP_PRECISION
    )
    through = jnp.cumsum(closing_sum, axis=0)
    resets = jnp.cumsum(1.0 - carried)
    pages = jnp.arange(page_count)
    valid = (pages[:, None] >= pages[None, :]) & (resets[:, None] == resets[None, :])
    spread = through[:, None] - through[None, :]
    spread = jnp.where(valid[:, :, None, None], spread, 0.0)
    weights = jnp.where(valid[:, :, None, None], jnp.exp(spread), 0.0)
    memories = jnp.einsum("pqhe,qheb->pheb", weights, page_terms, precision=TOP_PRECISION)
    previous = jnp.concatenate([jnp.zeros_like(memories[:1]), memories[:-1]], axis=0)
    previous = previous * carried[:, None, None, None]
    layer_output = layer_output + jnp.einsum(
        "phik,phkv->phiv", raised_rows, previous, precision=TOP_PRECISION
    )
    return memories[-1], layer_output, memories


def on_device(
    tokens,
    attention_gain,
    project_weight,
    conv_weight,
    decay_down,
    decay_up,
    decay_bias,
    output_gate,
    head_gain,
    output_weight,
    mixer_gain,
    gate_weight,
    up_weight,
    down_weight,
    prompt_pages,
    prompt_start,
):
    token_count = tokens.shape[0]
    page_count = token_count // PAGE
    local_heads = project_weight.shape[1] // CONVW
    rim_rows = KCONV - 1
    seq_index = lax.axis_index("seq")
    group_pages = page_count * lax.axis_size("seq")
    page_flags = page_segments(prompt_pages[0], prompt_start[0], group_pages)
    carried = lax.dynamic_slice_in_dim(page_flags, seq_index * page_count, page_count)
    normed = rms_scaled(tokens, attention_gain).astype(jnp.bfloat16)
    projected = jnp.dot(normed, project_weight, preferred_element_type=jnp.float32).astype(
        jnp.bfloat16
    )
    by_page = projected.reshape(page_count, PAGE, local_heads * CONVW)
    incoming = shifted(by_page[-1, PAGE - rim_rows :], "seq", 1)
    before = jnp.concatenate([incoming[None], by_page[:-1, PAGE - rim_rows :]], axis=0)
    mixed_rows = short_conv(by_page, before, carried, conv_weight).reshape(
        page_count, PAGE, local_heads, CONVW
    )
    query_rows, key_rows, value_matrix = split_features(mixed_rows, HK)
    lowrank = jnp.dot(normed, decay_down, preferred_element_type=jnp.float32).astype(jnp.bfloat16)
    decay_log = (
        jax.nn.log_sigmoid(
            jnp.dot(lowrank, decay_up, preferred_element_type=jnp.float32) + decay_bias
        )
        / 16.0
    )
    decay_log = decay_log.reshape(page_count, PAGE, local_heads, HK).transpose(0, 2, 1, 3)
    decay_sum = jnp.cumsum(decay_log, axis=2)
    local_memory, outputs, memories = page_block(
        query_rows, key_rows, value_matrix, decay_sum, carried
    )
    totals = decay_sum[:, :, -1, :]
    through = jnp.cumsum(totals, axis=0)
    alive_mask = jnp.cumprod(carried)
    block_decay = alive_mask[-1] * jnp.exp(through[-1])

    def compose(earlier, latter):
        return (earlier[0] * latter[0], latter[0][..., None] * earlier[1] + latter[1])

    prefix = prefix_2(
        (block_decay, local_memory),
        "seq",
        compose,
        (jnp.ones_like(block_decay), jnp.zeros_like(local_memory)),
    )
    incoming_state = prefix[1]
    before_sum = through - totals
    extent_factor = alive_mask[:, None, None, None] * jnp.exp(decay_sum + before_sum[:, :, None, :])
    outputs = outputs + jnp.einsum(
        "dlof,lfg->dlog", query_rows * extent_factor, incoming_state, precision=TOP_PRECISION
    )
    memories = (
        memories + (alive_mask[:, None, None] * jnp.exp(through))[..., None] * incoming_state[None]
    )
    attended = outputs.transpose(0, 2, 1, 3).reshape(token_count, local_heads, HV)
    normed_heads = rms_scaled(attended, head_gain)
    opening = jax.nn.silu(jnp.dot(normed, output_gate, preferred_element_type=jnp.float32)).reshape(
        token_count, local_heads, HV
    )
    gated_rows = (
        (normed_heads * opening).astype(jnp.bfloat16).reshape(token_count, local_heads * HV)
    )
    partial_value = jnp.dot(gated_rows, output_weight, preferred_element_type=jnp.float32)
    half_rows = token_count // lax.axis_size("hid")
    row_start = lax.axis_index("hid") * half_rows
    own_value = partial_value.astype(jnp.bfloat16)
    mixed_sum = own_value.astype(jnp.float32) + from_partner(own_value, token_count, 0).astype(
        jnp.float32
    )
    residual = (tokens.astype(jnp.float32) + mixed_sum).astype(jnp.bfloat16)
    feed_in = rms_scaled(residual, mixer_gain).astype(jnp.bfloat16)
    own_residual = lax.dynamic_slice_in_dim(residual, row_start, half_rows, 0)

    def widen(weight_rows):
        return jnp.dot(feed_in, weight_rows, preferred_element_type=jnp.float32)

    width = gate_weight.shape[1]
    both_part = widen(
        lax.all_gather(
            jnp.concatenate([gate_weight, up_weight], axis=1), "req", axis=0, tiled=True
        )
    )
    gate_part = both_part[:, :width]
    up_part = both_part[:, width:]
    hidden = lax.optimization_barrier((jax.nn.silu(gate_part) * up_part).astype(jnp.bfloat16))
    middle = down_weight.shape[0] // 2
    partials = jnp.dot(
        hidden[:, :middle],
        lax.all_gather(down_weight[:middle], "req", axis=1, tiled=True),
        preferred_element_type=jnp.float32,
    ) + jnp.dot(
        hidden[:, middle:],
        lax.all_gather(down_weight[middle:], "req", axis=1, tiled=True),
        preferred_element_type=jnp.float32,
    )
    own_partials = partials.astype(jnp.bfloat16)
    feed_sum = lax.dynamic_slice_in_dim(own_partials, row_start, half_rows, 0).astype(
        jnp.float32
    ) + from_partner(own_partials, half_rows, 1).astype(jnp.float32)
    result = (own_residual.astype(jnp.float32) + feed_sum).astype(jnp.bfloat16)
    return (result, memories.astype(jnp.bfloat16), by_page[:, PAGE - rim_rows :])


def solution(mesh):
    return jax.shard_map(
        on_device,
        mesh=mesh,
        in_specs=(
            P(("req", "seq"), None),
            P(),
            P(None, "hid"),
            P(None, "hid"),
            P(),
            P(None, "hid"),
            P("hid"),
            P(None, "hid"),
            P(),
            P("hid", None),
            P(),
            P("req", "hid"),
            P("req", "hid"),
            P("hid", "req"),
            P("req", None),
            P("req", None),
        ),
        out_specs=(
            P(("req", "seq", "hid"), None),
            P(("req", "seq"), "hid", None, None),
            P(("req", "seq"), None, "hid"),
        ),
        check_vma=False,
    )
```

```python
import functools

import jax
import jax.numpy as jnp
from jax import lax
from jax.experimental.layout import Layout, with_layout_constraint
from jax.sharding import PartitionSpec as P
from jax.experimental import pallas as pl
from jax.experimental.pallas import tpu as pltpu

HK = 256
HV = 512
KCONV = 4
PAGE = 64
CONVW = 1024


EPSILON = 1e-06
TOP_PRECISION = lax.Precision.HIGHEST


def shifted(value, axis, steps):
    count = lax.axis_size(axis)
    first, last = (max(0, -steps), min(count, count - steps))
    return lax.ppermute(value, axis, [(source, source + steps) for source in range(first, last)])


def prefix_2(array, axis, join, neutral):
    place = lax.axis_index(axis)
    decay, memory = array
    width = memory.shape[-1]
    packed = jnp.concatenate(
        [memory.reshape(-1, width), jnp.pad(decay.reshape(1, -1), ((0, 0), (0, width - decay.size)))],
        axis=0,
    ).astype(jnp.bfloat16)
    received = spread_over_seq(packed)
    gathered = (
        received[:, -1, : decay.size].reshape((-1,) + decay.shape),
        received[:, :-1].reshape((-1,) + memory.shape),
    )
    state = jax.tree.map(lambda a, e: jnp.zeros_like(a) + jnp.asarray(e, a.dtype), array, neutral)

    def one(lap, state):
        return join(
            state,
            jax.tree.map(
                lambda a, own: lax.dynamic_index_in_dim(a, lap, 0, False).astype(own.dtype),
                gathered,
                array,
            ),
        )

    return lax.fori_loop(0, place, one, state)


def partner_kernel(rows, src_ref, dst_ref, send_sem, recv_sem):
    partner = 1 - lax.axis_index("hid")
    barrier = pltpu.get_barrier_semaphore()
    pl.semaphore_signal(
        barrier, inc=1, device_id={"hid": partner}, device_id_type=pl.DeviceIdType.MESH
    )
    pl.semaphore_wait(barrier, 1)
    start = pl.multiple_of(partner * rows, rows) if rows < src_ref.shape[0] else 0
    copy = pltpu.make_async_remote_copy(
        src_ref=src_ref.at[pl.ds(start, rows)],
        dst_ref=dst_ref,
        send_sem=send_sem,
        recv_sem=recv_sem,
        device_id={"hid": partner},
        device_id_type=pl.DeviceIdType.MESH,
    )
    copy.start()
    copy.wait()


def from_partner(value, rows, kernel_id):
    return pl.pallas_call(
        functools.partial(partner_kernel, rows),
        out_shape=jax.ShapeDtypeStruct((rows,) + value.shape[1:], value.dtype),
        in_specs=[pl.BlockSpec(memory_space=pl.ANY)],
        out_specs=pl.BlockSpec(memory_space=pl.ANY),
        scratch_shapes=[pltpu.SemaphoreType.DMA, pltpu.SemaphoreType.DMA],
        compiler_params=pltpu.CompilerParams(collective_id=kernel_id, has_side_effects=True),
    )(value)


def spread_kernel(src_ref, dst_ref, send_sem, recv_sem):
    count = lax.axis_size("seq")
    me = lax.axis_index("seq")
    barrier = pltpu.get_barrier_semaphore()
    for step in range(1, count):
        pl.semaphore_signal(
            barrier,
            inc=1,
            device_id={"seq": lax.rem(me + step, count)},
            device_id_type=pl.DeviceIdType.MESH,
        )
    pl.semaphore_wait(barrier, count - 1)
    copies = []
    for step in range(1, count):
        copy = pltpu.make_async_remote_copy(
            src_ref=src_ref,
            dst_ref=dst_ref.at[me],
            send_sem=send_sem.at[step - 1],
            recv_sem=recv_sem.at[me],
            device_id={"seq": jnp.minimum(me + step, count - 1)},
            device_id_type=pl.DeviceIdType.MESH,
        )
        copies.append(copy)

        @pl.when(me + step < count)
        def _():
            copy.start()

    for step, copy in zip(range(1, count), copies):

        @pl.when(me + step < count)
        def _():
            copy.wait_send()

    for step in range(1, count):
        source = jnp.maximum(me - step, 0)

        @pl.when(me - step >= 0)
        def _():
            pltpu.make_async_remote_copy(
                src_ref=src_ref,
                dst_ref=dst_ref.at[source],
                send_sem=send_sem.at[step - 1],
                recv_sem=recv_sem.at[source],
                device_id={"seq": source},
                device_id_type=pl.DeviceIdType.MESH,
            ).wait_recv()


def spread_over_seq(value):
    count = lax.axis_size("seq")
    return pl.pallas_call(
        spread_kernel,
        out_shape=jax.ShapeDtypeStruct((count,) + value.shape, value.dtype),
        in_specs=[pl.BlockSpec(memory_space=pl.ANY)],
        out_specs=pl.BlockSpec(memory_space=pl.ANY),
        scratch_shapes=[
            pltpu.SemaphoreType.DMA((count - 1,)),
            pltpu.SemaphoreType.DMA((count,)),
        ],
        compiler_params=pltpu.CompilerParams(collective_id=2, has_side_effects=True),
    )(value)


def rms_scaled(values, scale_gain):
    values = values.astype(jnp.float32)
    return (
        values
        * lax.rsqrt(jnp.mean(values * values, axis=-1, keepdims=True) + EPSILON)
        * scale_gain.astype(jnp.float32)
    )


def page_segments(page_counts, starts, total_pages):
    position = jnp.arange(total_pages, dtype=jnp.int32)
    inside = (position[None, :] >= starts[:, None]) & (
        position[None, :] < starts[:, None] + page_counts[:, None]
    )
    labels = jnp.arange(1, page_counts.shape[0] + 1, dtype=jnp.int32)
    segment = jnp.sum(jnp.where(inside, labels[:, None], 0), axis=0) - 1
    earlier = jnp.concatenate([jnp.full((1,), -1, jnp.int32), segment[:-1]])
    return ((segment == earlier) & (segment >= 0)).astype(jnp.float32)


def short_conv(by_page, before, carried, conv_taps):
    kept_rows = before.astype(jnp.float32) * carried[:, None, None]
    widened = jnp.concatenate([kept_rows, by_page.astype(jnp.float32)], axis=1)
    tap_count = conv_taps.shape[0]
    length = by_page.shape[1]
    result = jnp.zeros(by_page.shape, jnp.float32)
    for offset in range(tap_count):
        result = (
            result
            + conv_taps[offset].astype(jnp.float32)
            * widened[:, tap_count - 1 - offset : tap_count - 1 - offset + length]
        )
    return result


def split_features(mixed_rows, key_width):
    query_rows = jax.nn.silu(mixed_rows[..., :key_width])
    key_rows = jax.nn.silu(mixed_rows[..., key_width : 2 * key_width]) * key_width ** (-0.5)
    value_matrix = mixed_rows[..., 2 * key_width :]
    return (
        query_rows.transpose(0, 2, 1, 3),
        key_rows.transpose(0, 2, 1, 3),
        value_matrix.transpose(0, 2, 1, 3),
    )


def page_block(query_rows, key_rows, value_matrix, decay_sum, carried):
    length = query_rows.shape[2]
    page_count = query_rows.shape[0]
    raised_rows = query_rows * jnp.exp(decay_sum)
    lowered = key_rows * jnp.exp(-decay_sum)
    scores = jnp.einsum("phik,phjk->phij", raised_rows, lowered, precision=TOP_PRECISION)
    rows_index = jnp.arange(length)
    causal = rows_index[:, None] >= rows_index[None, :]
    scores = jnp.where(causal[None, None], scores, 0.0)
    layer_output = jnp.einsum("phij,phjv->phiv", scores, value_matrix, precision=TOP_PRECISION)
    closing_sum = decay_sum[:, :, -1, :]
    weighted_rows = key_rows * jnp.exp(closing_sum[:, :, None, :] - decay_sum)
    page_terms = jnp.einsum(
        "phte,phtb->pheb", weighted_rows, value_matrix, precision=TOP_PRECISION
    )
    through = jnp.cumsum(closing_sum, axis=0)
    resets = jnp.cumsum(1.0 - carried)
    pages = jnp.arange(page_count)
    valid = (pages[:, None] >= pages[None, :]) & (resets[:, None] == resets[None, :])
    spread = through[:, None] - through[None, :]
    spread = jnp.where(valid[:, :, None, None], spread, 0.0)
    weights = jnp.where(valid[:, :, None, None], jnp.exp(spread), 0.0)
    memories = jnp.einsum("pqhe,qheb->pheb", weights, page_terms, precision=TOP_PRECISION)
    previous = jnp.concatenate([jnp.zeros_like(memories[:1]), memories[:-1]], axis=0)
    previous = previous * carried[:, None, None, None]
    layer_output = layer_output + jnp.einsum(
        "phik,phkv->phiv", raised_rows, previous, precision=TOP_PRECISION
    )
    return memories[-1], layer_output, memories


def on_device(
    tokens,
    attention_gain,
    project_weight,
    conv_weight,
    decay_down,
    decay_up,
    decay_bias,
    output_gate,
    head_gain,
    output_weight,
    mixer_gain,
    gate_weight,
    up_weight,
    down_weight,
    prompt_pages,
    prompt_start,
):
    token_count = tokens.shape[0]
    page_count = token_count // PAGE
    local_heads = project_weight.shape[1] // CONVW
    rim_rows = KCONV - 1
    seq_index = lax.axis_index("seq")
    group_pages = page_count * lax.axis_size("seq")
    page_flags = page_segments(prompt_pages[0], prompt_start[0], group_pages)
    carried = lax.dynamic_slice_in_dim(page_flags, seq_index * page_count, page_count)
    normed = rms_scaled(tokens, attention_gain).astype(jnp.bfloat16)
    projected = jnp.dot(normed, project_weight, preferred_element_type=jnp.float32).astype(
        jnp.bfloat16
    )
    by_page = projected.reshape(page_count, PAGE, local_heads * CONVW)
    incoming = shifted(by_page[-1, PAGE - rim_rows :], "seq", 1)
    before = jnp.concatenate([incoming[None], by_page[:-1, PAGE - rim_rows :]], axis=0)
    mixed_rows = short_conv(by_page, before, carried, conv_weight).reshape(
        page_count, PAGE, local_heads, CONVW
    )
    query_rows, key_rows, value_matrix = split_features(mixed_rows, HK)
    lowrank = jnp.dot(normed, decay_down, preferred_element_type=jnp.float32).astype(jnp.bfloat16)
    decay_log = (
        jax.nn.log_sigmoid(
            jnp.dot(lowrank, decay_up, preferred_element_type=jnp.float32) + decay_bias
        )
        / 16.0
    )
    decay_log = decay_log.reshape(page_count, PAGE, local_heads, HK).transpose(0, 2, 1, 3)
    decay_sum = jnp.cumsum(decay_log, axis=2)
    local_memory, outputs, memories = page_block(
        query_rows, key_rows, value_matrix, decay_sum, carried
    )
    totals = decay_sum[:, :, -1, :]
    through = jnp.cumsum(totals, axis=0)
    alive_mask = jnp.cumprod(carried)
    block_decay = alive_mask[-1] * jnp.exp(through[-1])

    def compose(earlier, latter):
        return (earlier[0] * latter[0], latter[0][..., None] * earlier[1] + latter[1])

    prefix = prefix_2(
        (block_decay, local_memory),
        "seq",
        compose,
        (jnp.ones_like(block_decay), jnp.zeros_like(local_memory)),
    )
    incoming_state = prefix[1]
    before_sum = through - totals
    extent_factor = alive_mask[:, None, None, None] * jnp.exp(decay_sum + before_sum[:, :, None, :])
    outputs = outputs + jnp.einsum(
        "dlof,lfg->dlog", query_rows * extent_factor, incoming_state, precision=TOP_PRECISION
    )
    memories = (
        memories + (alive_mask[:, None, None] * jnp.exp(through))[..., None] * incoming_state[None]
    )
    attended = outputs.transpose(0, 2, 1, 3).reshape(token_count, local_heads, HV)
    normed_heads = rms_scaled(attended, head_gain)
    opening = jax.nn.silu(jnp.dot(normed, output_gate, preferred_element_type=jnp.float32)).reshape(
        token_count, local_heads, HV
    )
    gated_rows = (
        (normed_heads * opening).astype(jnp.bfloat16).reshape(token_count, local_heads * HV)
    )
    partial_value = jnp.dot(gated_rows, output_weight, preferred_element_type=jnp.float32)
    half_rows = token_count // lax.axis_size("hid")
    row_start = lax.axis_index("hid") * half_rows
    own_value = partial_value.astype(jnp.bfloat16)
    mixed_sum = own_value.astype(jnp.float32) + from_partner(own_value, token_count, 0).astype(
        jnp.float32
    )
    residual = (tokens.astype(jnp.float32) + mixed_sum).astype(jnp.bfloat16)
    feed_in = rms_scaled(residual, mixer_gain).astype(jnp.bfloat16)
    own_residual = lax.dynamic_slice_in_dim(residual, row_start, half_rows, 0)

    def widen(weight_rows):
        return jnp.dot(feed_in, weight_rows, preferred_element_type=jnp.float32)

    width = gate_weight.shape[1]
    both_part = widen(
        lax.all_gather(
            jnp.concatenate([gate_weight, up_weight], axis=1), "req", axis=0, tiled=True
        )
    )
    gate_part = both_part[:, :width]
    up_part = both_part[:, width:]
    hidden = lax.optimization_barrier((jax.nn.silu(gate_part) * up_part).astype(jnp.bfloat16))
    down_block = with_layout_constraint(down_weight.T, Layout((0, 1)))
    down_rows = lax.all_gather(down_block, "req", axis=0, tiled=True)
    partials = lax.dot_general(
        hidden, down_rows, (((1,), (1,)), ((), ())), preferred_element_type=jnp.float32
    )
    own_partials = partials.astype(jnp.bfloat16)
    feed_sum = lax.dynamic_slice_in_dim(own_partials, row_start, half_rows, 0).astype(
        jnp.float32
    ) + from_partner(own_partials, half_rows, 1).astype(jnp.float32)
    result = (own_residual.astype(jnp.float32) + feed_sum).astype(jnp.bfloat16)
    return (result, memories.astype(jnp.bfloat16), by_page[:, PAGE - rim_rows :])


def solution(mesh):
    return jax.shard_map(
        on_device,
        mesh=mesh,
        in_specs=(
            P(("req", "seq"), None),
            P(),
            P(None, "hid"),
            P(None, "hid"),
            P(),
            P(None, "hid"),
            P("hid"),
            P(None, "hid"),
            P(),
            P("hid", None),
            P(),
            P("req", "hid"),
            P("req", "hid"),
            P("hid", "req"),
            P("req", None),
            P("req", None),
        ),
        out_specs=(
            P(("req", "seq", "hid"), None),
            P(("req", "seq"), "hid", None, None),
            P(("req", "seq"), None, "hid"),
        ),
        check_vma=False,
    )
```

```python
import functools

import jax
import jax.numpy as jnp
from jax import lax
from jax.experimental.layout import Layout, with_layout_constraint
from jax.sharding import PartitionSpec as P
from jax.experimental import pallas as pl
from jax.experimental.pallas import tpu as pltpu

HK = 256
HV = 512
KCONV = 4
PAGE = 64
CONVW = 1024


EPSILON = 1e-06
TOP_PRECISION = lax.Precision.HIGHEST


def shifted(value, axis, steps):
    count = lax.axis_size(axis)
    first, last = (max(0, -steps), min(count, count - steps))
    return lax.ppermute(value, axis, [(source, source + steps) for source in range(first, last)])


def prefix_2(array, axis, join, neutral):
    place = lax.axis_index(axis)
    decay, memory = array
    width = memory.shape[-1]
    packed = jnp.concatenate(
        [memory.reshape(-1, width), jnp.pad(decay.reshape(1, -1), ((0, 0), (0, width - decay.size)))],
        axis=0,
    ).astype(jnp.bfloat16)
    received = spread_over_seq(packed)
    gathered = (
        received[:, -1, : decay.size].reshape((-1,) + decay.shape),
        received[:, :-1].reshape((-1,) + memory.shape),
    )
    state = jax.tree.map(lambda a, e: jnp.zeros_like(a) + jnp.asarray(e, a.dtype), array, neutral)

    def one(lap, state):
        return join(
            state,
            jax.tree.map(
                lambda a, own: lax.dynamic_index_in_dim(a, lap, 0, False).astype(own.dtype),
                gathered,
                array,
            ),
        )

    return lax.fori_loop(0, place, one, state)


def partner_kernel(rows, src_ref, dst_ref, send_sem, recv_sem):
    partner = 1 - lax.axis_index("hid")
    barrier = pltpu.get_barrier_semaphore()
    pl.semaphore_signal(
        barrier, inc=1, device_id={"hid": partner}, device_id_type=pl.DeviceIdType.MESH
    )
    pl.semaphore_wait(barrier, 1)
    start = pl.multiple_of(partner * rows, rows) if rows < src_ref.shape[0] else 0
    copy = pltpu.make_async_remote_copy(
        src_ref=src_ref.at[pl.ds(start, rows)],
        dst_ref=dst_ref,
        send_sem=send_sem,
        recv_sem=recv_sem,
        device_id={"hid": partner},
        device_id_type=pl.DeviceIdType.MESH,
    )
    copy.start()
    copy.wait()


def from_partner(value, rows, kernel_id):
    return pl.pallas_call(
        functools.partial(partner_kernel, rows),
        out_shape=jax.ShapeDtypeStruct((rows,) + value.shape[1:], value.dtype),
        in_specs=[pl.BlockSpec(memory_space=pl.ANY)],
        out_specs=pl.BlockSpec(memory_space=pl.ANY),
        scratch_shapes=[pltpu.SemaphoreType.DMA, pltpu.SemaphoreType.DMA],
        compiler_params=pltpu.CompilerParams(collective_id=kernel_id, has_side_effects=True),
    )(value)


def spread_kernel(src_ref, dst_ref, send_sem, recv_sem):
    count = lax.axis_size("seq")
    me = lax.axis_index("seq")
    barrier = pltpu.get_barrier_semaphore()
    for step in range(1, count):
        pl.semaphore_signal(
            barrier,
            inc=1,
            device_id={"seq": lax.rem(me + step, count)},
            device_id_type=pl.DeviceIdType.MESH,
        )
    pl.semaphore_wait(barrier, count - 1)
    copies = []
    for step in range(1, count):
        copy = pltpu.make_async_remote_copy(
            src_ref=src_ref,
            dst_ref=dst_ref.at[me],
            send_sem=send_sem.at[step - 1],
            recv_sem=recv_sem.at[me],
            device_id={"seq": jnp.minimum(me + step, count - 1)},
            device_id_type=pl.DeviceIdType.MESH,
        )
        copies.append(copy)

        @pl.when(me + step < count)
        def _():
            copy.start()

    for step, copy in zip(range(1, count), copies):

        @pl.when(me + step < count)
        def _():
            copy.wait_send()

    for step in range(1, count):
        source = jnp.maximum(me - step, 0)

        @pl.when(me - step >= 0)
        def _():
            pltpu.make_async_remote_copy(
                src_ref=src_ref,
                dst_ref=dst_ref.at[source],
                send_sem=send_sem.at[step - 1],
                recv_sem=recv_sem.at[source],
                device_id={"seq": source},
                device_id_type=pl.DeviceIdType.MESH,
            ).wait_recv()


def spread_over_seq(value):
    count = lax.axis_size("seq")
    return pl.pallas_call(
        spread_kernel,
        out_shape=jax.ShapeDtypeStruct((count,) + value.shape, value.dtype),
        in_specs=[pl.BlockSpec(memory_space=pl.ANY)],
        out_specs=pl.BlockSpec(memory_space=pl.ANY),
        scratch_shapes=[
            pltpu.SemaphoreType.DMA((count - 1,)),
            pltpu.SemaphoreType.DMA((count,)),
        ],
        compiler_params=pltpu.CompilerParams(collective_id=2, has_side_effects=True),
    )(value)


def recurrence_kernel(decay_ref, terms_ref, out_ref, state_ref):
    page = pl.program_id(0)

    @pl.when(page == 0)
    def _():
        state_ref[...] = terms_ref[0]

    @pl.when(page > 0)
    def _():
        state_ref[...] = decay_ref[0] * state_ref[...] + terms_ref[0]

    out_ref[0] = state_ref[...]


def page_recurrence(decay, terms):
    page_count, rows, width = terms.shape
    return pl.pallas_call(
        recurrence_kernel,
        out_shape=jax.ShapeDtypeStruct(terms.shape, terms.dtype),
        grid=(page_count,),
        in_specs=[
            pl.BlockSpec((1, rows, 1), lambda p: (p, 0, 0)),
            pl.BlockSpec((1, rows, width), lambda p: (p, 0, 0)),
        ],
        out_specs=pl.BlockSpec((1, rows, width), lambda p: (p, 0, 0)),
        scratch_shapes=[pltpu.VMEM((rows, width), jnp.float32)],
    )(decay, terms)


def rms_scaled(values, scale_gain):
    values = values.astype(jnp.float32)
    return (
        values
        * lax.rsqrt(jnp.mean(values * values, axis=-1, keepdims=True) + EPSILON)
        * scale_gain.astype(jnp.float32)
    )


def page_segments(page_counts, starts, total_pages):
    position = jnp.arange(total_pages, dtype=jnp.int32)
    inside = (position[None, :] >= starts[:, None]) & (
        position[None, :] < starts[:, None] + page_counts[:, None]
    )
    labels = jnp.arange(1, page_counts.shape[0] + 1, dtype=jnp.int32)
    segment = jnp.sum(jnp.where(inside, labels[:, None], 0), axis=0) - 1
    earlier = jnp.concatenate([jnp.full((1,), -1, jnp.int32), segment[:-1]])
    return ((segment == earlier) & (segment >= 0)).astype(jnp.float32)


def short_conv(by_page, before, carried, conv_taps):
    kept_rows = before.astype(jnp.float32) * carried[:, None, None]
    widened = jnp.concatenate([kept_rows, by_page.astype(jnp.float32)], axis=1)
    tap_count = conv_taps.shape[0]
    length = by_page.shape[1]
    result = jnp.zeros(by_page.shape, jnp.float32)
    for offset in range(tap_count):
        result = (
            result
            + conv_taps[offset].astype(jnp.float32)
            * widened[:, tap_count - 1 - offset : tap_count - 1 - offset + length]
        )
    return result


def split_features(mixed_rows, key_width):
    query_rows = jax.nn.silu(mixed_rows[..., :key_width])
    key_rows = jax.nn.silu(mixed_rows[..., key_width : 2 * key_width]) * key_width ** (-0.5)
    value_matrix = mixed_rows[..., 2 * key_width :]
    return (
        query_rows.transpose(0, 2, 1, 3),
        key_rows.transpose(0, 2, 1, 3),
        value_matrix.transpose(0, 2, 1, 3),
    )


def page_block(query_rows, key_rows, value_matrix, decay_sum, carried):
    length = query_rows.shape[2]
    page_count = query_rows.shape[0]
    raised_rows = query_rows * jnp.exp(decay_sum)
    lowered = key_rows * jnp.exp(-decay_sum)
    scores = jnp.einsum("phik,phjk->phij", raised_rows, lowered, precision=TOP_PRECISION)
    rows_index = jnp.arange(length)
    causal = rows_index[:, None] >= rows_index[None, :]
    scores = jnp.where(causal[None, None], scores, 0.0)
    layer_output = jnp.einsum("phij,phjv->phiv", scores, value_matrix, precision=TOP_PRECISION)
    closing_sum = decay_sum[:, :, -1, :]
    weighted_rows = key_rows * jnp.exp(closing_sum[:, :, None, :] - decay_sum)
    page_terms = jnp.einsum(
        "phte,phtb->pheb", weighted_rows, value_matrix, precision=TOP_PRECISION
    )
    page_decay = jnp.exp(closing_sum) * carried[:, None, None]
    memories = page_recurrence(
        page_decay.reshape(page_count, -1, 1),
        page_terms.reshape(page_count, -1, page_terms.shape[-1]),
    ).reshape(page_terms.shape)
    previous = jnp.concatenate([jnp.zeros_like(memories[:1]), memories[:-1]], axis=0)
    previous = previous * carried[:, None, None, None]
    layer_output = layer_output + jnp.einsum(
        "phik,phkv->phiv", raised_rows, previous, precision=TOP_PRECISION
    )
    return memories[-1], layer_output, memories


def on_device(
    tokens,
    attention_gain,
    project_weight,
    conv_weight,
    decay_down,
    decay_up,
    decay_bias,
    output_gate,
    head_gain,
    output_weight,
    mixer_gain,
    gate_weight,
    up_weight,
    down_weight,
    prompt_pages,
    prompt_start,
):
    token_count = tokens.shape[0]
    page_count = token_count // PAGE
    local_heads = project_weight.shape[1] // CONVW
    rim_rows = KCONV - 1
    seq_index = lax.axis_index("seq")
    group_pages = page_count * lax.axis_size("seq")
    page_flags = page_segments(prompt_pages[0], prompt_start[0], group_pages)
    carried = lax.dynamic_slice_in_dim(page_flags, seq_index * page_count, page_count)
    normed = rms_scaled(tokens, attention_gain).astype(jnp.bfloat16)
    projected = jnp.dot(normed, project_weight, preferred_element_type=jnp.float32).astype(
        jnp.bfloat16
    )
    by_page = projected.reshape(page_count, PAGE, local_heads * CONVW)
    incoming = shifted(by_page[-1, PAGE - rim_rows :], "seq", 1)
    before = jnp.concatenate([incoming[None], by_page[:-1, PAGE - rim_rows :]], axis=0)
    mixed_rows = short_conv(by_page, before, carried, conv_weight).reshape(
        page_count, PAGE, local_heads, CONVW
    )
    query_rows, key_rows, value_matrix = split_features(mixed_rows, HK)
    lowrank = jnp.dot(normed, decay_down, preferred_element_type=jnp.float32).astype(jnp.bfloat16)
    decay_log = (
        jax.nn.log_sigmoid(
            jnp.dot(lowrank, decay_up, preferred_element_type=jnp.float32) + decay_bias
        )
        / 16.0
    )
    decay_log = decay_log.reshape(page_count, PAGE, local_heads, HK).transpose(0, 2, 1, 3)
    decay_sum = jnp.cumsum(decay_log, axis=2)
    local_memory, outputs, memories = page_block(
        query_rows, key_rows, value_matrix, decay_sum, carried
    )
    totals = decay_sum[:, :, -1, :]
    through = jnp.cumsum(totals, axis=0)
    alive_mask = jnp.cumprod(carried)
    block_decay = alive_mask[-1] * jnp.exp(through[-1])

    def compose(earlier, latter):
        return (earlier[0] * latter[0], latter[0][..., None] * earlier[1] + latter[1])

    prefix = prefix_2(
        (block_decay, local_memory),
        "seq",
        compose,
        (jnp.ones_like(block_decay), jnp.zeros_like(local_memory)),
    )
    incoming_state = prefix[1]
    before_sum = through - totals
    extent_factor = alive_mask[:, None, None, None] * jnp.exp(decay_sum + before_sum[:, :, None, :])
    outputs = outputs + jnp.einsum(
        "dlof,lfg->dlog", query_rows * extent_factor, incoming_state, precision=TOP_PRECISION
    )
    memories = (
        memories + (alive_mask[:, None, None] * jnp.exp(through))[..., None] * incoming_state[None]
    )
    attended = outputs.transpose(0, 2, 1, 3).reshape(token_count, local_heads, HV)
    normed_heads = rms_scaled(attended, head_gain)
    opening = jax.nn.silu(jnp.dot(normed, output_gate, preferred_element_type=jnp.float32)).reshape(
        token_count, local_heads, HV
    )
    gated_rows = (
        (normed_heads * opening).astype(jnp.bfloat16).reshape(token_count, local_heads * HV)
    )
    partial_value = jnp.dot(gated_rows, output_weight, preferred_element_type=jnp.float32)
    half_rows = token_count // lax.axis_size("hid")
    row_start = lax.axis_index("hid") * half_rows
    own_value = partial_value.astype(jnp.bfloat16)
    mixed_sum = own_value.astype(jnp.float32) + from_partner(own_value, token_count, 0).astype(
        jnp.float32
    )
    residual = (tokens.astype(jnp.float32) + mixed_sum).astype(jnp.bfloat16)
    feed_in = rms_scaled(residual, mixer_gain).astype(jnp.bfloat16)
    own_residual = lax.dynamic_slice_in_dim(residual, row_start, half_rows, 0)

    def widen(weight_rows):
        return jnp.dot(feed_in, weight_rows, preferred_element_type=jnp.float32)

    width = gate_weight.shape[1]
    both_part = widen(
        lax.all_gather(
            jnp.concatenate([gate_weight, up_weight], axis=1), "req", axis=0, tiled=True
        )
    )
    gate_part = both_part[:, :width]
    up_part = both_part[:, width:]
    hidden = lax.optimization_barrier((jax.nn.silu(gate_part) * up_part).astype(jnp.bfloat16))
    down_block = with_layout_constraint(down_weight.T, Layout((0, 1)))
    down_rows = lax.all_gather(down_block, "req", axis=0, tiled=True)
    partials = lax.dot_general(
        hidden, down_rows, (((1,), (1,)), ((), ())), preferred_element_type=jnp.float32
    )
    own_partials = partials.astype(jnp.bfloat16)
    feed_sum = lax.dynamic_slice_in_dim(own_partials, row_start, half_rows, 0).astype(
        jnp.float32
    ) + from_partner(own_partials, half_rows, 1).astype(jnp.float32)
    result = (own_residual.astype(jnp.float32) + feed_sum).astype(jnp.bfloat16)
    return (result, memories.astype(jnp.bfloat16), by_page[:, PAGE - rim_rows :])


def solution(mesh):
    return jax.shard_map(
        on_device,
        mesh=mesh,
        in_specs=(
            P(("req", "seq"), None),
            P(),
            P(None, "hid"),
            P(None, "hid"),
            P(),
            P(None, "hid"),
            P("hid"),
            P(None, "hid"),
            P(),
            P("hid", None),
            P(),
            P("req", "hid"),
            P("req", "hid"),
            P("hid", "req"),
            P("req", None),
            P("req", None),
        ),
        out_specs=(
            P(("req", "seq", "hid"), None),
            P(("req", "seq"), "hid", None, None),
            P(("req", "seq"), None, "hid"),
        ),
        check_vma=False,
    )
```

```python
import functools

import jax
import jax.numpy as jnp
from jax import lax
from jax.experimental.layout import Layout, with_layout_constraint
from jax.sharding import PartitionSpec as P
from jax.experimental import pallas as pl
from jax.experimental.pallas import tpu as pltpu

HK = 256
HV = 512
KCONV = 4
PAGE = 64
CONVW = 1024


EPSILON = 1e-06
TOP_PRECISION = lax.Precision.HIGHEST


def shifted(value, axis, steps):
    count = lax.axis_size(axis)
    first, last = (max(0, -steps), min(count, count - steps))
    return lax.ppermute(value, axis, [(source, source + steps) for source in range(first, last)])


def prefix_2(array, axis, join, neutral):
    place = lax.axis_index(axis)
    decay, memory = array
    width = memory.shape[-1]
    packed = jnp.concatenate(
        [memory.reshape(-1, width), jnp.pad(decay.reshape(1, -1), ((0, 0), (0, width - decay.size)))],
        axis=0,
    ).astype(jnp.bfloat16)
    received = spread_over_seq(packed)
    gathered = (
        received[:, -1, : decay.size].reshape((-1,) + decay.shape),
        received[:, :-1].reshape((-1,) + memory.shape),
    )
    state = jax.tree.map(lambda a, e: jnp.zeros_like(a) + jnp.asarray(e, a.dtype), array, neutral)

    def one(lap, state):
        return join(
            state,
            jax.tree.map(
                lambda a, own: lax.dynamic_index_in_dim(a, lap, 0, False).astype(own.dtype),
                gathered,
                array,
            ),
        )

    return lax.fori_loop(0, place, one, state)


def partner_kernel(rows, src_ref, dst_ref, send_sem, recv_sem):
    partner = 1 - lax.axis_index("hid")
    barrier = pltpu.get_barrier_semaphore()
    pl.semaphore_signal(
        barrier, inc=1, device_id={"hid": partner}, device_id_type=pl.DeviceIdType.MESH
    )
    pl.semaphore_wait(barrier, 1)
    start = pl.multiple_of(partner * rows, rows) if rows < src_ref.shape[0] else 0
    copy = pltpu.make_async_remote_copy(
        src_ref=src_ref.at[pl.ds(start, rows)],
        dst_ref=dst_ref,
        send_sem=send_sem,
        recv_sem=recv_sem,
        device_id={"hid": partner},
        device_id_type=pl.DeviceIdType.MESH,
    )
    copy.start()
    copy.wait()


def from_partner(value, rows, kernel_id):
    return pl.pallas_call(
        functools.partial(partner_kernel, rows),
        out_shape=jax.ShapeDtypeStruct((rows,) + value.shape[1:], value.dtype),
        in_specs=[pl.BlockSpec(memory_space=pl.ANY)],
        out_specs=pl.BlockSpec(memory_space=pl.ANY),
        scratch_shapes=[pltpu.SemaphoreType.DMA, pltpu.SemaphoreType.DMA],
        compiler_params=pltpu.CompilerParams(collective_id=kernel_id, has_side_effects=True),
    )(value)


def spread_kernel(src_ref, dst_ref, send_sem, recv_sem):
    count = lax.axis_size("seq")
    me = lax.axis_index("seq")
    barrier = pltpu.get_barrier_semaphore()
    for step in range(1, count):
        pl.semaphore_signal(
            barrier,
            inc=1,
            device_id={"seq": lax.rem(me + step, count)},
            device_id_type=pl.DeviceIdType.MESH,
        )
    pl.semaphore_wait(barrier, count - 1)
    copies = []
    for step in range(1, count):
        copy = pltpu.make_async_remote_copy(
            src_ref=src_ref,
            dst_ref=dst_ref.at[me],
            send_sem=send_sem.at[step - 1],
            recv_sem=recv_sem.at[me],
            device_id={"seq": jnp.minimum(me + step, count - 1)},
            device_id_type=pl.DeviceIdType.MESH,
        )
        copies.append(copy)

        @pl.when(me + step < count)
        def _():
            copy.start()

    for step, copy in zip(range(1, count), copies):

        @pl.when(me + step < count)
        def _():
            copy.wait_send()

    for step in range(1, count):
        source = jnp.maximum(me - step, 0)

        @pl.when(me - step >= 0)
        def _():
            pltpu.make_async_remote_copy(
                src_ref=src_ref,
                dst_ref=dst_ref.at[source],
                send_sem=send_sem.at[step - 1],
                recv_sem=recv_sem.at[source],
                device_id={"seq": source},
                device_id_type=pl.DeviceIdType.MESH,
            ).wait_recv()


def spread_over_seq(value):
    count = lax.axis_size("seq")
    return pl.pallas_call(
        spread_kernel,
        out_shape=jax.ShapeDtypeStruct((count,) + value.shape, value.dtype),
        in_specs=[pl.BlockSpec(memory_space=pl.ANY)],
        out_specs=pl.BlockSpec(memory_space=pl.ANY),
        scratch_shapes=[
            pltpu.SemaphoreType.DMA((count - 1,)),
            pltpu.SemaphoreType.DMA((count,)),
        ],
        compiler_params=pltpu.CompilerParams(collective_id=2, has_side_effects=True),
    )(value)


def recurrence_kernel(decay_ref, carried_ref, terms_ref, out_ref, previous_ref, state_ref):
    step = pl.program_id(0)
    chunk = terms_ref.shape[0]
    reach = terms_ref.shape[-1] // decay_ref.shape[-1]

    @pl.when(step == 0)
    def _():
        state_ref[...] = jnp.zeros_like(state_ref)

    for page in range(chunk):
        kept = jnp.concatenate([carried_ref[page]] * reach, axis=-1) * state_ref[...]
        previous_ref[page] = kept
        state = jnp.concatenate([decay_ref[page]] * reach, axis=-1) * kept + terms_ref[page]
        state_ref[...] = state
        out_ref[page] = state


def page_recurrence(decay, carried, terms, chunk=4):
    page_count, rows, width = terms.shape
    lanes = decay.shape[-1]
    block = pl.BlockSpec((chunk, rows, width), lambda p: (p, 0, 0))
    flags = pl.BlockSpec((chunk, rows, lanes), lambda p: (p, 0, 0))
    return pl.pallas_call(
        recurrence_kernel,
        out_shape=(
            jax.ShapeDtypeStruct(terms.shape, terms.dtype),
            jax.ShapeDtypeStruct(terms.shape, terms.dtype),
        ),
        grid=(page_count // chunk,),
        in_specs=[flags, flags, block],
        out_specs=(block, block),
        scratch_shapes=[pltpu.VMEM((rows, width), jnp.float32)],
    )(decay, carried, terms)


def rms_scaled(values, scale_gain):
    values = values.astype(jnp.float32)
    return (
        values
        * lax.rsqrt(jnp.mean(values * values, axis=-1, keepdims=True) + EPSILON)
        * scale_gain.astype(jnp.float32)
    )


def page_segments(page_counts, starts, total_pages):
    position = jnp.arange(total_pages, dtype=jnp.int32)
    inside = (position[None, :] >= starts[:, None]) & (
        position[None, :] < starts[:, None] + page_counts[:, None]
    )
    labels = jnp.arange(1, page_counts.shape[0] + 1, dtype=jnp.int32)
    segment = jnp.sum(jnp.where(inside, labels[:, None], 0), axis=0) - 1
    earlier = jnp.concatenate([jnp.full((1,), -1, jnp.int32), segment[:-1]])
    return ((segment == earlier) & (segment >= 0)).astype(jnp.float32)


def short_conv(by_page, before, carried, conv_taps):
    kept_rows = before.astype(jnp.float32) * carried[:, None, None]
    widened = jnp.concatenate([kept_rows, by_page.astype(jnp.float32)], axis=1)
    tap_count = conv_taps.shape[0]
    length = by_page.shape[1]
    result = jnp.zeros(by_page.shape, jnp.float32)
    for offset in range(tap_count):
        result = (
            result
            + conv_taps[offset].astype(jnp.float32)
            * widened[:, tap_count - 1 - offset : tap_count - 1 - offset + length]
        )
    return result


def split_features(mixed_rows, key_width):
    query_rows = jax.nn.silu(mixed_rows[..., :key_width])
    key_rows = jax.nn.silu(mixed_rows[..., key_width : 2 * key_width]) * key_width ** (-0.5)
    value_matrix = mixed_rows[..., 2 * key_width :]
    return (
        query_rows.transpose(0, 2, 1, 3),
        key_rows.transpose(0, 2, 1, 3),
        value_matrix.transpose(0, 2, 1, 3),
    )


def page_block(query_rows, key_rows, value_matrix, decay_sum, carried):
    length = query_rows.shape[2]
    page_count = query_rows.shape[0]
    raised_rows = query_rows * jnp.exp(decay_sum)
    lowered = key_rows * jnp.exp(-decay_sum)
    scores = jnp.einsum("phik,phjk->phij", raised_rows, lowered, precision=TOP_PRECISION)
    rows_index = jnp.arange(length)
    causal = rows_index[:, None] >= rows_index[None, :]
    scores = jnp.where(causal[None, None], scores, 0.0)
    layer_output = jnp.einsum("phij,phjv->phiv", scores, value_matrix, precision=TOP_PRECISION)
    closing_sum = decay_sum[:, :, -1, :]
    weighted_rows = key_rows * jnp.exp(closing_sum[:, :, None, :] - decay_sum)
    page_terms = jnp.einsum(
        "phte,phtb->pheb", weighted_rows, value_matrix, precision=TOP_PRECISION
    )
    lanes = 128
    rows = closing_sum.shape[1] * closing_sum.shape[2]
    memories, previous = page_recurrence(
        jnp.broadcast_to(jnp.exp(closing_sum).reshape(page_count, rows, 1), (page_count, rows, lanes)),
        jnp.broadcast_to(carried[:, None, None], (page_count, rows, lanes)),
        page_terms.reshape(page_count, rows, page_terms.shape[-1]),
    )
    memories = memories.reshape(page_terms.shape)
    previous = previous.reshape(page_terms.shape)
    layer_output = layer_output + jnp.einsum(
        "phik,phkv->phiv", raised_rows, previous, precision=TOP_PRECISION
    )
    return memories[-1], layer_output, memories


def on_device(
    tokens,
    attention_gain,
    project_weight,
    conv_weight,
    decay_down,
    decay_up,
    decay_bias,
    output_gate,
    head_gain,
    output_weight,
    mixer_gain,
    gate_weight,
    up_weight,
    down_weight,
    prompt_pages,
    prompt_start,
):
    token_count = tokens.shape[0]
    page_count = token_count // PAGE
    local_heads = project_weight.shape[1] // CONVW
    rim_rows = KCONV - 1
    seq_index = lax.axis_index("seq")
    group_pages = page_count * lax.axis_size("seq")
    page_flags = page_segments(prompt_pages[0], prompt_start[0], group_pages)
    carried = lax.dynamic_slice_in_dim(page_flags, seq_index * page_count, page_count)
    normed = rms_scaled(tokens, attention_gain).astype(jnp.bfloat16)
    projected = jnp.dot(normed, project_weight, preferred_element_type=jnp.float32).astype(
        jnp.bfloat16
    )
    by_page = projected.reshape(page_count, PAGE, local_heads * CONVW)
    incoming = shifted(by_page[-1, PAGE - rim_rows :], "seq", 1)
    before = jnp.concatenate([incoming[None], by_page[:-1, PAGE - rim_rows :]], axis=0)
    mixed_rows = short_conv(by_page, before, carried, conv_weight).reshape(
        page_count, PAGE, local_heads, CONVW
    )
    query_rows, key_rows, value_matrix = split_features(mixed_rows, HK)
    lowrank = jnp.dot(normed, decay_down, preferred_element_type=jnp.float32).astype(jnp.bfloat16)
    decay_log = (
        jax.nn.log_sigmoid(
            jnp.dot(lowrank, decay_up, preferred_element_type=jnp.float32) + decay_bias
        )
        / 16.0
    )
    decay_log = decay_log.reshape(page_count, PAGE, local_heads, HK).transpose(0, 2, 1, 3)
    decay_sum = jnp.cumsum(decay_log, axis=2)
    local_memory, outputs, memories = page_block(
        query_rows, key_rows, value_matrix, decay_sum, carried
    )
    totals = decay_sum[:, :, -1, :]
    through = jnp.cumsum(totals, axis=0)
    alive_mask = jnp.cumprod(carried)
    block_decay = alive_mask[-1] * jnp.exp(through[-1])

    def compose(earlier, latter):
        return (earlier[0] * latter[0], latter[0][..., None] * earlier[1] + latter[1])

    prefix = prefix_2(
        (block_decay, local_memory),
        "seq",
        compose,
        (jnp.ones_like(block_decay), jnp.zeros_like(local_memory)),
    )
    incoming_state = prefix[1]
    before_sum = through - totals
    extent_factor = alive_mask[:, None, None, None] * jnp.exp(decay_sum + before_sum[:, :, None, :])
    outputs = outputs + jnp.einsum(
        "dlof,lfg->dlog", query_rows * extent_factor, incoming_state, precision=TOP_PRECISION
    )
    memories = (
        memories + (alive_mask[:, None, None] * jnp.exp(through))[..., None] * incoming_state[None]
    )
    attended = outputs.transpose(0, 2, 1, 3).reshape(token_count, local_heads, HV)
    normed_heads = rms_scaled(attended, head_gain)
    opening = jax.nn.silu(jnp.dot(normed, output_gate, preferred_element_type=jnp.float32)).reshape(
        token_count, local_heads, HV
    )
    gated_rows = (
        (normed_heads * opening).astype(jnp.bfloat16).reshape(token_count, local_heads * HV)
    )
    partial_value = jnp.dot(gated_rows, output_weight, preferred_element_type=jnp.float32)
    half_rows = token_count // lax.axis_size("hid")
    row_start = lax.axis_index("hid") * half_rows
    own_value = partial_value.astype(jnp.bfloat16)
    mixed_sum = own_value.astype(jnp.float32) + from_partner(own_value, token_count, 0).astype(
        jnp.float32
    )
    residual = (tokens.astype(jnp.float32) + mixed_sum).astype(jnp.bfloat16)
    feed_in = rms_scaled(residual, mixer_gain).astype(jnp.bfloat16)
    own_residual = lax.dynamic_slice_in_dim(residual, row_start, half_rows, 0)

    def widen(weight_rows):
        return jnp.dot(feed_in, weight_rows, preferred_element_type=jnp.float32)

    width = gate_weight.shape[1]
    both_part = widen(
        lax.all_gather(
            jnp.concatenate([gate_weight, up_weight], axis=1), "req", axis=0, tiled=True
        )
    )
    gate_part = both_part[:, :width]
    up_part = both_part[:, width:]
    hidden = lax.optimization_barrier((jax.nn.silu(gate_part) * up_part).astype(jnp.bfloat16))
    down_block = with_layout_constraint(down_weight.T, Layout((0, 1)))
    down_rows = lax.all_gather(down_block, "req", axis=0, tiled=True)
    partials = lax.dot_general(
        hidden, down_rows, (((1,), (1,)), ((), ())), preferred_element_type=jnp.float32
    )
    own_partials = partials.astype(jnp.bfloat16)
    feed_sum = lax.dynamic_slice_in_dim(own_partials, row_start, half_rows, 0).astype(
        jnp.float32
    ) + from_partner(own_partials, half_rows, 1).astype(jnp.float32)
    result = (own_residual.astype(jnp.float32) + feed_sum).astype(jnp.bfloat16)
    return (result, memories.astype(jnp.bfloat16), by_page[:, PAGE - rim_rows :])


def solution(mesh):
    return jax.shard_map(
        on_device,
        mesh=mesh,
        in_specs=(
            P(("req", "seq"), None),
            P(),
            P(None, "hid"),
            P(None, "hid"),
            P(),
            P(None, "hid"),
            P("hid"),
            P(None, "hid"),
            P(),
            P("hid", None),
            P(),
            P("req", "hid"),
            P("req", "hid"),
            P("hid", "req"),
            P("req", None),
            P("req", None),
        ),
        out_specs=(
            P(("req", "seq", "hid"), None),
            P(("req", "seq"), "hid", None, None),
            P(("req", "seq"), None, "hid"),
        ),
        check_vma=False,
    )
```

```python
import functools

import jax
import jax.numpy as jnp
from jax import lax
from jax.experimental.layout import Layout, with_layout_constraint
from jax.sharding import PartitionSpec as P
from jax.experimental import pallas as pl
from jax.experimental.pallas import tpu as pltpu

HK = 256
HV = 512
KCONV = 4
PAGE = 64
CONVW = 1024


EPSILON = 1e-06
TOP_PRECISION = lax.Precision.HIGH


def shifted(value, axis, steps):
    count = lax.axis_size(axis)
    first, last = (max(0, -steps), min(count, count - steps))
    return lax.ppermute(value, axis, [(source, source + steps) for source in range(first, last)])


def prefix_2(array, axis, join, neutral):
    place = lax.axis_index(axis)
    decay, memory = array
    width = memory.shape[-1]
    packed = jnp.concatenate(
        [memory.reshape(-1, width), jnp.pad(decay.reshape(1, -1), ((0, 0), (0, width - decay.size)))],
        axis=0,
    ).astype(jnp.bfloat16)
    received = spread_over_seq(packed)
    gathered = (
        received[:, -1, : decay.size].reshape((-1,) + decay.shape),
        received[:, :-1].reshape((-1,) + memory.shape),
    )
    state = jax.tree.map(lambda a, e: jnp.zeros_like(a) + jnp.asarray(e, a.dtype), array, neutral)

    def one(lap, state):
        return join(
            state,
            jax.tree.map(
                lambda a, own: lax.dynamic_index_in_dim(a, lap, 0, False).astype(own.dtype),
                gathered,
                array,
            ),
        )

    return lax.fori_loop(0, place, one, state)


def partner_kernel(rows, src_ref, dst_ref, send_sem, recv_sem):
    partner = 1 - lax.axis_index("hid")
    barrier = pltpu.get_barrier_semaphore()
    pl.semaphore_signal(
        barrier, inc=1, device_id={"hid": partner}, device_id_type=pl.DeviceIdType.MESH
    )
    pl.semaphore_wait(barrier, 1)
    start = pl.multiple_of(partner * rows, rows) if rows < src_ref.shape[0] else 0
    copy = pltpu.make_async_remote_copy(
        src_ref=src_ref.at[pl.ds(start, rows)],
        dst_ref=dst_ref,
        send_sem=send_sem,
        recv_sem=recv_sem,
        device_id={"hid": partner},
        device_id_type=pl.DeviceIdType.MESH,
    )
    copy.start()
    copy.wait()


def from_partner(value, rows, kernel_id):
    return pl.pallas_call(
        functools.partial(partner_kernel, rows),
        out_shape=jax.ShapeDtypeStruct((rows,) + value.shape[1:], value.dtype),
        in_specs=[pl.BlockSpec(memory_space=pl.ANY)],
        out_specs=pl.BlockSpec(memory_space=pl.ANY),
        scratch_shapes=[pltpu.SemaphoreType.DMA, pltpu.SemaphoreType.DMA],
        compiler_params=pltpu.CompilerParams(collective_id=kernel_id, has_side_effects=True),
    )(value)


def spread_kernel(src_ref, dst_ref, send_sem, recv_sem):
    count = lax.axis_size("seq")
    me = lax.axis_index("seq")
    barrier = pltpu.get_barrier_semaphore()
    for step in range(1, count):
        pl.semaphore_signal(
            barrier,
            inc=1,
            device_id={"seq": lax.rem(me + step, count)},
            device_id_type=pl.DeviceIdType.MESH,
        )
    pl.semaphore_wait(barrier, count - 1)
    copies = []
    for step in range(1, count):
        copy = pltpu.make_async_remote_copy(
            src_ref=src_ref,
            dst_ref=dst_ref.at[me],
            send_sem=send_sem.at[step - 1],
            recv_sem=recv_sem.at[me],
            device_id={"seq": jnp.minimum(me + step, count - 1)},
            device_id_type=pl.DeviceIdType.MESH,
        )
        copies.append(copy)

        @pl.when(me + step < count)
        def _():
            copy.start()

    for step, copy in zip(range(1, count), copies):

        @pl.when(me + step < count)
        def _():
            copy.wait_send()

    for step in range(1, count):
        source = jnp.maximum(me - step, 0)

        @pl.when(me - step >= 0)
        def _():
            pltpu.make_async_remote_copy(
                src_ref=src_ref,
                dst_ref=dst_ref.at[source],
                send_sem=send_sem.at[step - 1],
                recv_sem=recv_sem.at[source],
                device_id={"seq": source},
                device_id_type=pl.DeviceIdType.MESH,
            ).wait_recv()


def spread_over_seq(value):
    count = lax.axis_size("seq")
    return pl.pallas_call(
        spread_kernel,
        out_shape=jax.ShapeDtypeStruct((count,) + value.shape, value.dtype),
        in_specs=[pl.BlockSpec(memory_space=pl.ANY)],
        out_specs=pl.BlockSpec(memory_space=pl.ANY),
        scratch_shapes=[
            pltpu.SemaphoreType.DMA((count - 1,)),
            pltpu.SemaphoreType.DMA((count,)),
        ],
        compiler_params=pltpu.CompilerParams(collective_id=2, has_side_effects=True),
    )(value)


def recurrence_kernel(decay_ref, carried_ref, terms_ref, out_ref, previous_ref, state_ref):
    step = pl.program_id(0)
    chunk = terms_ref.shape[0]
    reach = terms_ref.shape[-1] // decay_ref.shape[-1]

    @pl.when(step == 0)
    def _():
        state_ref[...] = jnp.zeros_like(state_ref)

    for page in range(chunk):
        kept = jnp.concatenate([carried_ref[page]] * reach, axis=-1) * state_ref[...]
        previous_ref[page] = kept
        state = jnp.concatenate([decay_ref[page]] * reach, axis=-1) * kept + terms_ref[page]
        state_ref[...] = state
        out_ref[page] = state


def page_recurrence(decay, carried, terms, chunk=4):
    page_count, rows, width = terms.shape
    lanes = decay.shape[-1]
    block = pl.BlockSpec((chunk, rows, width), lambda p: (p, 0, 0))
    flags = pl.BlockSpec((chunk, rows, lanes), lambda p: (p, 0, 0))
    return pl.pallas_call(
        recurrence_kernel,
        out_shape=(
            jax.ShapeDtypeStruct(terms.shape, terms.dtype),
            jax.ShapeDtypeStruct(terms.shape, terms.dtype),
        ),
        grid=(page_count // chunk,),
        in_specs=[flags, flags, block],
        out_specs=(block, block),
        scratch_shapes=[pltpu.VMEM((rows, width), jnp.float32)],
    )(decay, carried, terms)


def rms_scaled(values, scale_gain):
    values = values.astype(jnp.float32)
    return (
        values
        * lax.rsqrt(jnp.mean(values * values, axis=-1, keepdims=True) + EPSILON)
        * scale_gain.astype(jnp.float32)
    )


def page_segments(page_counts, starts, total_pages):
    position = jnp.arange(total_pages, dtype=jnp.int32)
    inside = (position[None, :] >= starts[:, None]) & (
        position[None, :] < starts[:, None] + page_counts[:, None]
    )
    labels = jnp.arange(1, page_counts.shape[0] + 1, dtype=jnp.int32)
    segment = jnp.sum(jnp.where(inside, labels[:, None], 0), axis=0) - 1
    earlier = jnp.concatenate([jnp.full((1,), -1, jnp.int32), segment[:-1]])
    return ((segment == earlier) & (segment >= 0)).astype(jnp.float32)


def short_conv(by_page, before, carried, conv_taps):
    kept_rows = before.astype(jnp.float32) * carried[:, None, None]
    widened = jnp.concatenate([kept_rows, by_page.astype(jnp.float32)], axis=1)
    tap_count = conv_taps.shape[0]
    length = by_page.shape[1]
    result = jnp.zeros(by_page.shape, jnp.float32)
    for offset in range(tap_count):
        result = (
            result
            + conv_taps[offset].astype(jnp.float32)
            * widened[:, tap_count - 1 - offset : tap_count - 1 - offset + length]
        )
    return result


def split_features(mixed_rows, key_width):
    query_rows = jax.nn.silu(mixed_rows[..., :key_width])
    key_rows = jax.nn.silu(mixed_rows[..., key_width : 2 * key_width]) * key_width ** (-0.5)
    value_matrix = mixed_rows[..., 2 * key_width :]
    return (
        query_rows.transpose(0, 2, 1, 3),
        key_rows.transpose(0, 2, 1, 3),
        value_matrix.transpose(0, 2, 1, 3),
    )


def page_block(query_rows, key_rows, value_matrix, decay_sum, carried):
    length = query_rows.shape[2]
    page_count = query_rows.shape[0]
    raised_rows = query_rows * jnp.exp(decay_sum)
    lowered = key_rows * jnp.exp(-decay_sum)
    scores = jnp.einsum("phik,phjk->phij", raised_rows, lowered, precision=TOP_PRECISION)
    rows_index = jnp.arange(length)
    causal = rows_index[:, None] >= rows_index[None, :]
    scores = jnp.where(causal[None, None], scores, 0.0)
    layer_output = jnp.einsum("phij,phjv->phiv", scores, value_matrix, precision=TOP_PRECISION)
    closing_sum = decay_sum[:, :, -1, :]
    weighted_rows = key_rows * jnp.exp(closing_sum[:, :, None, :] - decay_sum)
    page_terms = jnp.einsum(
        "phte,phtb->pheb", weighted_rows, value_matrix, precision=TOP_PRECISION
    )
    lanes = 128
    rows = closing_sum.shape[1] * closing_sum.shape[2]
    memories, previous = page_recurrence(
        jnp.broadcast_to(jnp.exp(closing_sum).reshape(page_count, rows, 1), (page_count, rows, lanes)),
        jnp.broadcast_to(carried[:, None, None], (page_count, rows, lanes)),
        page_terms.reshape(page_count, rows, page_terms.shape[-1]),
    )
    memories = memories.reshape(page_terms.shape)
    previous = previous.reshape(page_terms.shape)
    layer_output = layer_output + jnp.einsum(
        "phik,phkv->phiv", raised_rows, previous, precision=TOP_PRECISION
    )
    return memories[-1], layer_output, memories


def on_device(
    tokens,
    attention_gain,
    project_weight,
    conv_weight,
    decay_down,
    decay_up,
    decay_bias,
    output_gate,
    head_gain,
    output_weight,
    mixer_gain,
    gate_weight,
    up_weight,
    down_weight,
    prompt_pages,
    prompt_start,
):
    token_count = tokens.shape[0]
    page_count = token_count // PAGE
    local_heads = project_weight.shape[1] // CONVW
    rim_rows = KCONV - 1
    seq_index = lax.axis_index("seq")
    group_pages = page_count * lax.axis_size("seq")
    page_flags = page_segments(prompt_pages[0], prompt_start[0], group_pages)
    carried = lax.dynamic_slice_in_dim(page_flags, seq_index * page_count, page_count)
    normed = rms_scaled(tokens, attention_gain).astype(jnp.bfloat16)
    projected = jnp.dot(normed, project_weight, preferred_element_type=jnp.float32).astype(
        jnp.bfloat16
    )
    by_page = projected.reshape(page_count, PAGE, local_heads * CONVW)
    incoming = shifted(by_page[-1, PAGE - rim_rows :], "seq", 1)
    before = jnp.concatenate([incoming[None], by_page[:-1, PAGE - rim_rows :]], axis=0)
    mixed_rows = short_conv(by_page, before, carried, conv_weight).reshape(
        page_count, PAGE, local_heads, CONVW
    )
    query_rows, key_rows, value_matrix = split_features(mixed_rows, HK)
    lowrank = jnp.dot(normed, decay_down, preferred_element_type=jnp.float32).astype(jnp.bfloat16)
    decay_log = (
        jax.nn.log_sigmoid(
            jnp.dot(lowrank, decay_up, preferred_element_type=jnp.float32) + decay_bias
        )
        / 16.0
    )
    decay_log = decay_log.reshape(page_count, PAGE, local_heads, HK).transpose(0, 2, 1, 3)
    decay_sum = jnp.cumsum(decay_log, axis=2)
    local_memory, outputs, memories = page_block(
        query_rows, key_rows, value_matrix, decay_sum, carried
    )
    totals = decay_sum[:, :, -1, :]
    through = jnp.cumsum(totals, axis=0)
    alive_mask = jnp.cumprod(carried)
    block_decay = alive_mask[-1] * jnp.exp(through[-1])

    def compose(earlier, latter):
        return (earlier[0] * latter[0], latter[0][..., None] * earlier[1] + latter[1])

    prefix = prefix_2(
        (block_decay, local_memory),
        "seq",
        compose,
        (jnp.ones_like(block_decay), jnp.zeros_like(local_memory)),
    )
    incoming_state = prefix[1]
    before_sum = through - totals
    extent_factor = alive_mask[:, None, None, None] * jnp.exp(decay_sum + before_sum[:, :, None, :])
    outputs = outputs + jnp.einsum(
        "dlof,lfg->dlog", query_rows * extent_factor, incoming_state, precision=TOP_PRECISION
    )
    memories = (
        memories + (alive_mask[:, None, None] * jnp.exp(through))[..., None] * incoming_state[None]
    )
    attended = outputs.transpose(0, 2, 1, 3).reshape(token_count, local_heads, HV)
    normed_heads = rms_scaled(attended, head_gain)
    opening = jax.nn.silu(jnp.dot(normed, output_gate, preferred_element_type=jnp.float32)).reshape(
        token_count, local_heads, HV
    )
    gated_rows = (
        (normed_heads * opening).astype(jnp.bfloat16).reshape(token_count, local_heads * HV)
    )
    partial_value = jnp.dot(gated_rows, output_weight, preferred_element_type=jnp.float32)
    half_rows = token_count // lax.axis_size("hid")
    row_start = lax.axis_index("hid") * half_rows
    own_value = partial_value.astype(jnp.bfloat16)
    mixed_sum = own_value.astype(jnp.float32) + from_partner(own_value, token_count, 0).astype(
        jnp.float32
    )
    residual = (tokens.astype(jnp.float32) + mixed_sum).astype(jnp.bfloat16)
    feed_in = rms_scaled(residual, mixer_gain).astype(jnp.bfloat16)
    own_residual = lax.dynamic_slice_in_dim(residual, row_start, half_rows, 0)

    def widen(weight_rows):
        return jnp.dot(feed_in, weight_rows, preferred_element_type=jnp.float32)

    width = gate_weight.shape[1]
    both_part = widen(
        lax.all_gather(
            jnp.concatenate([gate_weight, up_weight], axis=1), "req", axis=0, tiled=True
        )
    )
    gate_part = both_part[:, :width]
    up_part = both_part[:, width:]
    hidden = lax.optimization_barrier((jax.nn.silu(gate_part) * up_part).astype(jnp.bfloat16))
    down_block = with_layout_constraint(down_weight.T, Layout((0, 1)))
    down_rows = lax.all_gather(down_block, "req", axis=0, tiled=True)
    partials = lax.dot_general(
        hidden, down_rows, (((1,), (1,)), ((), ())), preferred_element_type=jnp.float32
    )
    own_partials = partials.astype(jnp.bfloat16)
    feed_sum = lax.dynamic_slice_in_dim(own_partials, row_start, half_rows, 0).astype(
        jnp.float32
    ) + from_partner(own_partials, half_rows, 1).astype(jnp.float32)
    result = (own_residual.astype(jnp.float32) + feed_sum).astype(jnp.bfloat16)
    return (result, memories.astype(jnp.bfloat16), by_page[:, PAGE - rim_rows :])


def solution(mesh):
    return jax.shard_map(
        on_device,
        mesh=mesh,
        in_specs=(
            P(("req", "seq"), None),
            P(),
            P(None, "hid"),
            P(None, "hid"),
            P(),
            P(None, "hid"),
            P("hid"),
            P(None, "hid"),
            P(),
            P("hid", None),
            P(),
            P("req", "hid"),
            P("req", "hid"),
            P("hid", "req"),
            P("req", None),
            P("req", None),
        ),
        out_specs=(
            P(("req", "seq", "hid"), None),
            P(("req", "seq"), "hid", None, None),
            P(("req", "seq"), None, "hid"),
        ),
        check_vma=False,
    )
```

```python
import functools

import jax
import jax.numpy as jnp
from jax import lax
from jax.experimental.layout import Layout, with_layout_constraint
from jax.sharding import PartitionSpec as P
from jax.experimental import pallas as pl
from jax.experimental.pallas import tpu as pltpu

HK = 256
HV = 512
KCONV = 4
PAGE = 64
CONVW = 1024


EPSILON = 1e-06
TOP_PRECISION = lax.Precision.HIGH


def shifted(value, axis, steps):
    count = lax.axis_size(axis)
    first, last = (max(0, -steps), min(count, count - steps))
    return lax.ppermute(value, axis, [(source, source + steps) for source in range(first, last)])


def prefix_2(array, axis, join, neutral):
    place = lax.axis_index(axis)
    decay, memory = array
    width = memory.shape[-1]
    packed = jnp.concatenate(
        [memory.reshape(-1, width), jnp.pad(decay.reshape(1, -1), ((0, 0), (0, width - decay.size)))],
        axis=0,
    ).astype(jnp.bfloat16)
    received = spread_over_seq(packed)
    gathered = (
        received[:, -1, : decay.size].reshape((-1,) + decay.shape),
        received[:, :-1].reshape((-1,) + memory.shape),
    )
    state = jax.tree.map(lambda a, e: jnp.zeros_like(a) + jnp.asarray(e, a.dtype), array, neutral)

    def one(lap, state):
        return join(
            state,
            jax.tree.map(
                lambda a, own: lax.dynamic_index_in_dim(a, lap, 0, False).astype(own.dtype),
                gathered,
                array,
            ),
        )

    return lax.fori_loop(0, place, one, state)


def partner_kernel(rows, pieces, src_ref, dst_ref, send_sem, recv_sem):
    partner = 1 - lax.axis_index("hid")
    barrier = pltpu.get_barrier_semaphore()
    pl.semaphore_signal(
        barrier, inc=1, device_id={"hid": partner}, device_id_type=pl.DeviceIdType.MESH
    )
    pl.semaphore_wait(barrier, 1)
    start = partner * rows if rows < src_ref.shape[0] else 0
    share = rows // pieces
    copies = []
    for piece in range(pieces):
        copy = pltpu.make_async_remote_copy(
            src_ref=src_ref.at[pl.ds(start + piece * share, share)],
            dst_ref=dst_ref.at[pl.ds(piece * share, share)],
            send_sem=send_sem.at[piece],
            recv_sem=recv_sem.at[piece],
            device_id={"hid": partner},
            device_id_type=pl.DeviceIdType.MESH,
        )
        copy.start()
        copies.append(copy)
    for copy in copies:
        copy.wait()


def from_partner(value, rows, kernel_id, pieces=4):
    return pl.pallas_call(
        functools.partial(partner_kernel, rows, pieces),
        out_shape=jax.ShapeDtypeStruct((rows,) + value.shape[1:], value.dtype),
        in_specs=[pl.BlockSpec(memory_space=pl.ANY)],
        out_specs=pl.BlockSpec(memory_space=pl.ANY),
        scratch_shapes=[
            pltpu.SemaphoreType.DMA((pieces,)),
            pltpu.SemaphoreType.DMA((pieces,)),
        ],
        compiler_params=pltpu.CompilerParams(collective_id=kernel_id, has_side_effects=True),
    )(value)


def spread_kernel(src_ref, dst_ref, send_sem, recv_sem):
    count = lax.axis_size("seq")
    me = lax.axis_index("seq")
    barrier = pltpu.get_barrier_semaphore()
    for step in range(1, count):
        pl.semaphore_signal(
            barrier,
            inc=1,
            device_id={"seq": lax.rem(me + step, count)},
            device_id_type=pl.DeviceIdType.MESH,
        )
    pl.semaphore_wait(barrier, count - 1)
    copies = []
    for step in range(1, count):
        copy = pltpu.make_async_remote_copy(
            src_ref=src_ref,
            dst_ref=dst_ref.at[me],
            send_sem=send_sem.at[step - 1],
            recv_sem=recv_sem.at[me],
            device_id={"seq": jnp.minimum(me + step, count - 1)},
            device_id_type=pl.DeviceIdType.MESH,
        )
        copies.append(copy)

        @pl.when(me + step < count)
        def _():
            copy.start()

    for step, copy in zip(range(1, count), copies):

        @pl.when(me + step < count)
        def _():
            copy.wait_send()

    for step in range(1, count):
        source = jnp.maximum(me - step, 0)

        @pl.when(me - step >= 0)
        def _():
            pltpu.make_async_remote_copy(
                src_ref=src_ref,
                dst_ref=dst_ref.at[source],
                send_sem=send_sem.at[step - 1],
                recv_sem=recv_sem.at[source],
                device_id={"seq": source},
                device_id_type=pl.DeviceIdType.MESH,
            ).wait_recv()


def spread_over_seq(value):
    count = lax.axis_size("seq")
    return pl.pallas_call(
        spread_kernel,
        out_shape=jax.ShapeDtypeStruct((count,) + value.shape, value.dtype),
        in_specs=[pl.BlockSpec(memory_space=pl.ANY)],
        out_specs=pl.BlockSpec(memory_space=pl.ANY),
        scratch_shapes=[
            pltpu.SemaphoreType.DMA((count - 1,)),
            pltpu.SemaphoreType.DMA((count,)),
        ],
        compiler_params=pltpu.CompilerParams(collective_id=2, has_side_effects=True),
    )(value)


def recurrence_kernel(decay_ref, carried_ref, terms_ref, out_ref, previous_ref, state_ref):
    step = pl.program_id(0)
    chunk = terms_ref.shape[0]
    reach = terms_ref.shape[-1] // decay_ref.shape[-1]

    @pl.when(step == 0)
    def _():
        state_ref[...] = jnp.zeros_like(state_ref)

    for page in range(chunk):
        kept = jnp.concatenate([carried_ref[page]] * reach, axis=-1) * state_ref[...]
        previous_ref[page] = kept
        state = jnp.concatenate([decay_ref[page]] * reach, axis=-1) * kept + terms_ref[page]
        state_ref[...] = state
        out_ref[page] = state


def page_recurrence(decay, carried, terms, chunk=4):
    page_count, rows, width = terms.shape
    lanes = decay.shape[-1]
    block = pl.BlockSpec((chunk, rows, width), lambda p: (p, 0, 0))
    flags = pl.BlockSpec((chunk, rows, lanes), lambda p: (p, 0, 0))
    return pl.pallas_call(
        recurrence_kernel,
        out_shape=(
            jax.ShapeDtypeStruct(terms.shape, terms.dtype),
            jax.ShapeDtypeStruct(terms.shape, terms.dtype),
        ),
        grid=(page_count // chunk,),
        in_specs=[flags, flags, block],
        out_specs=(block, block),
        scratch_shapes=[pltpu.VMEM((rows, width), jnp.float32)],
    )(decay, carried, terms)


def rms_scaled(values, scale_gain):
    values = values.astype(jnp.float32)
    return (
        values
        * lax.rsqrt(jnp.mean(values * values, axis=-1, keepdims=True) + EPSILON)
        * scale_gain.astype(jnp.float32)
    )


def page_segments(page_counts, starts, total_pages):
    position = jnp.arange(total_pages, dtype=jnp.int32)
    inside = (position[None, :] >= starts[:, None]) & (
        position[None, :] < starts[:, None] + page_counts[:, None]
    )
    labels = jnp.arange(1, page_counts.shape[0] + 1, dtype=jnp.int32)
    segment = jnp.sum(jnp.where(inside, labels[:, None], 0), axis=0) - 1
    earlier = jnp.concatenate([jnp.full((1,), -1, jnp.int32), segment[:-1]])
    return ((segment == earlier) & (segment >= 0)).astype(jnp.float32)


def short_conv(by_page, before, carried, conv_taps):
    kept_rows = before.astype(jnp.float32) * carried[:, None, None]
    widened = jnp.concatenate([kept_rows, by_page.astype(jnp.float32)], axis=1)
    tap_count = conv_taps.shape[0]
    length = by_page.shape[1]
    result = jnp.zeros(by_page.shape, jnp.float32)
    for offset in range(tap_count):
        result = (
            result
            + conv_taps[offset].astype(jnp.float32)
            * widened[:, tap_count - 1 - offset : tap_count - 1 - offset + length]
        )
    return result


def split_features(mixed_rows, key_width):
    query_rows = jax.nn.silu(mixed_rows[..., :key_width])
    key_rows = jax.nn.silu(mixed_rows[..., key_width : 2 * key_width]) * key_width ** (-0.5)
    value_matrix = mixed_rows[..., 2 * key_width :]
    return (
        query_rows.transpose(0, 2, 1, 3),
        key_rows.transpose(0, 2, 1, 3),
        value_matrix.transpose(0, 2, 1, 3),
    )


def page_block(query_rows, key_rows, value_matrix, decay_sum, carried):
    length = query_rows.shape[2]
    page_count = query_rows.shape[0]
    raised_rows = query_rows * jnp.exp(decay_sum)
    lowered = key_rows * jnp.exp(-decay_sum)
    scores = jnp.einsum("phik,phjk->phij", raised_rows, lowered, precision=TOP_PRECISION)
    rows_index = jnp.arange(length)
    causal = rows_index[:, None] >= rows_index[None, :]
    scores = jnp.where(causal[None, None], scores, 0.0)
    layer_output = jnp.einsum("phij,phjv->phiv", scores, value_matrix, precision=TOP_PRECISION)
    closing_sum = decay_sum[:, :, -1, :]
    weighted_rows = key_rows * jnp.exp(closing_sum[:, :, None, :] - decay_sum)
    page_terms = jnp.einsum(
        "phte,phtb->pheb", weighted_rows, value_matrix, precision=TOP_PRECISION
    )
    lanes = 128
    rows = closing_sum.shape[1] * closing_sum.shape[2]
    memories, previous = page_recurrence(
        jnp.broadcast_to(jnp.exp(closing_sum).reshape(page_count, rows, 1), (page_count, rows, lanes)),
        jnp.broadcast_to(carried[:, None, None], (page_count, rows, lanes)),
        page_terms.reshape(page_count, rows, page_terms.shape[-1]),
    )
    memories = memories.reshape(page_terms.shape)
    previous = previous.reshape(page_terms.shape)
    layer_output = layer_output + jnp.einsum(
        "phik,phkv->phiv", raised_rows, previous, precision=TOP_PRECISION
    )
    return memories[-1], layer_output, memories


def on_device(
    tokens,
    attention_gain,
    project_weight,
    conv_weight,
    decay_down,
    decay_up,
    decay_bias,
    output_gate,
    head_gain,
    output_weight,
    mixer_gain,
    gate_weight,
    up_weight,
    down_weight,
    prompt_pages,
    prompt_start,
):
    token_count = tokens.shape[0]
    page_count = token_count // PAGE
    local_heads = project_weight.shape[1] // CONVW
    rim_rows = KCONV - 1
    seq_index = lax.axis_index("seq")
    group_pages = page_count * lax.axis_size("seq")
    page_flags = page_segments(prompt_pages[0], prompt_start[0], group_pages)
    carried = lax.dynamic_slice_in_dim(page_flags, seq_index * page_count, page_count)
    normed = rms_scaled(tokens, attention_gain).astype(jnp.bfloat16)
    projected = jnp.dot(normed, project_weight, preferred_element_type=jnp.float32).astype(
        jnp.bfloat16
    )
    by_page = projected.reshape(page_count, PAGE, local_heads * CONVW)
    incoming = shifted(by_page[-1, PAGE - rim_rows :], "seq", 1)
    before = jnp.concatenate([incoming[None], by_page[:-1, PAGE - rim_rows :]], axis=0)
    mixed_rows = short_conv(by_page, before, carried, conv_weight).reshape(
        page_count, PAGE, local_heads, CONVW
    )
    query_rows, key_rows, value_matrix = split_features(mixed_rows, HK)
    lowrank = jnp.dot(normed, decay_down, preferred_element_type=jnp.float32).astype(jnp.bfloat16)
    decay_log = (
        jax.nn.log_sigmoid(
            jnp.dot(lowrank, decay_up, preferred_element_type=jnp.float32) + decay_bias
        )
        / 16.0
    )
    decay_log = decay_log.reshape(page_count, PAGE, local_heads, HK).transpose(0, 2, 1, 3)
    decay_sum = jnp.cumsum(decay_log, axis=2)
    local_memory, outputs, memories = page_block(
        query_rows, key_rows, value_matrix, decay_sum, carried
    )
    totals = decay_sum[:, :, -1, :]
    through = jnp.cumsum(totals, axis=0)
    alive_mask = jnp.cumprod(carried)
    block_decay = alive_mask[-1] * jnp.exp(through[-1])

    def compose(earlier, latter):
        return (earlier[0] * latter[0], latter[0][..., None] * earlier[1] + latter[1])

    prefix = prefix_2(
        (block_decay, local_memory),
        "seq",
        compose,
        (jnp.ones_like(block_decay), jnp.zeros_like(local_memory)),
    )
    incoming_state = prefix[1]
    before_sum = through - totals
    extent_factor = alive_mask[:, None, None, None] * jnp.exp(decay_sum + before_sum[:, :, None, :])
    outputs = outputs + jnp.einsum(
        "dlof,lfg->dlog", query_rows * extent_factor, incoming_state, precision=TOP_PRECISION
    )
    memories = (
        memories + (alive_mask[:, None, None] * jnp.exp(through))[..., None] * incoming_state[None]
    )
    attended = outputs.transpose(0, 2, 1, 3).reshape(token_count, local_heads, HV)
    normed_heads = rms_scaled(attended, head_gain)
    opening = jax.nn.silu(jnp.dot(normed, output_gate, preferred_element_type=jnp.float32)).reshape(
        token_count, local_heads, HV
    )
    gated_rows = (
        (normed_heads * opening).astype(jnp.bfloat16).reshape(token_count, local_heads * HV)
    )
    partial_value = jnp.dot(gated_rows, output_weight, preferred_element_type=jnp.float32)
    half_rows = token_count // lax.axis_size("hid")
    row_start = lax.axis_index("hid") * half_rows
    own_value = partial_value.astype(jnp.bfloat16)
    mixed_sum = own_value.astype(jnp.float32) + from_partner(own_value, token_count, 0).astype(
        jnp.float32
    )
    residual = (tokens.astype(jnp.float32) + mixed_sum).astype(jnp.bfloat16)
    feed_in = rms_scaled(residual, mixer_gain).astype(jnp.bfloat16)
    own_residual = lax.dynamic_slice_in_dim(residual, row_start, half_rows, 0)

    def widen(weight_rows):
        return jnp.dot(feed_in, weight_rows, preferred_element_type=jnp.float32)

    width = gate_weight.shape[1]
    both_part = widen(
        lax.all_gather(
            jnp.concatenate([gate_weight, up_weight], axis=1), "req", axis=0, tiled=True
        )
    )
    gate_part = both_part[:, :width]
    up_part = both_part[:, width:]
    hidden = lax.optimization_barrier((jax.nn.silu(gate_part) * up_part).astype(jnp.bfloat16))
    down_block = with_layout_constraint(down_weight.T, Layout((0, 1)))
    down_rows = lax.all_gather(down_block, "req", axis=0, tiled=True)
    partials = lax.dot_general(
        hidden, down_rows, (((1,), (1,)), ((), ())), preferred_element_type=jnp.float32
    )
    own_partials = partials.astype(jnp.bfloat16)
    feed_sum = lax.dynamic_slice_in_dim(own_partials, row_start, half_rows, 0).astype(
        jnp.float32
    ) + from_partner(own_partials, half_rows, 1).astype(jnp.float32)
    result = (own_residual.astype(jnp.float32) + feed_sum).astype(jnp.bfloat16)
    return (result, memories.astype(jnp.bfloat16), by_page[:, PAGE - rim_rows :])


def solution(mesh):
    return jax.shard_map(
        on_device,
        mesh=mesh,
        in_specs=(
            P(("req", "seq"), None),
            P(),
            P(None, "hid"),
            P(None, "hid"),
            P(),
            P(None, "hid"),
            P("hid"),
            P(None, "hid"),
            P(),
            P("hid", None),
            P(),
            P("req", "hid"),
            P("req", "hid"),
            P("hid", "req"),
            P("req", None),
            P("req", None),
        ),
        out_specs=(
            P(("req", "seq", "hid"), None),
            P(("req", "seq"), "hid", None, None),
            P(("req", "seq"), None, "hid"),
        ),
        check_vma=False,
    )
```

```python
import functools

import jax
import jax.numpy as jnp
from jax import lax
from jax.experimental.layout import Layout, with_layout_constraint
from jax.sharding import PartitionSpec as P
from jax.experimental import pallas as pl
from jax.experimental.pallas import tpu as pltpu

HK = 256
HV = 512
KCONV = 4
PAGE = 64
CONVW = 1024


EPSILON = 1e-06
TOP_PRECISION = lax.Precision.HIGH


def shifted(value, axis, steps):
    count = lax.axis_size(axis)
    first, last = (max(0, -steps), min(count, count - steps))
    return lax.ppermute(value, axis, [(source, source + steps) for source in range(first, last)])


def prefix_2(array, axis, join, neutral):
    place = lax.axis_index(axis)
    decay, memory = array
    width = memory.shape[-1]
    packed = jnp.concatenate(
        [memory.reshape(-1, width), jnp.pad(decay.reshape(1, -1), ((0, 0), (0, width - decay.size)))],
        axis=0,
    ).astype(jnp.bfloat16)
    received = spread_over_seq(packed)
    gathered = (
        received[:, -1, : decay.size].reshape((-1,) + decay.shape),
        received[:, :-1].reshape((-1,) + memory.shape),
    )
    state = jax.tree.map(lambda a, e: jnp.zeros_like(a) + jnp.asarray(e, a.dtype), array, neutral)

    def one(lap, state):
        return join(
            state,
            jax.tree.map(
                lambda a, own: lax.dynamic_index_in_dim(a, lap, 0, False).astype(own.dtype),
                gathered,
                array,
            ),
        )

    return lax.fori_loop(0, place, one, state)


def partner_kernel(rows, src_ref, dst_ref, send_sem, recv_sem):
    partner = 1 - lax.axis_index("hid")
    barrier = pltpu.get_barrier_semaphore()
    pl.semaphore_signal(
        barrier, inc=1, device_id={"hid": partner}, device_id_type=pl.DeviceIdType.MESH
    )
    pl.semaphore_wait(barrier, 1)
    start = pl.multiple_of(partner * rows, rows) if rows < src_ref.shape[0] else 0
    copy = pltpu.make_async_remote_copy(
        src_ref=src_ref.at[pl.ds(start, rows)],
        dst_ref=dst_ref,
        send_sem=send_sem,
        recv_sem=recv_sem,
        device_id={"hid": partner},
        device_id_type=pl.DeviceIdType.MESH,
    )
    copy.start()
    copy.wait()


def from_partner(value, rows, kernel_id):
    return pl.pallas_call(
        functools.partial(partner_kernel, rows),
        out_shape=jax.ShapeDtypeStruct((rows,) + value.shape[1:], value.dtype),
        in_specs=[pl.BlockSpec(memory_space=pl.ANY)],
        out_specs=pl.BlockSpec(memory_space=pl.ANY),
        scratch_shapes=[pltpu.SemaphoreType.DMA, pltpu.SemaphoreType.DMA],
        compiler_params=pltpu.CompilerParams(collective_id=kernel_id, has_side_effects=True),
    )(value)


def spread_kernel(src_ref, dst_ref, send_sem, recv_sem):
    count = lax.axis_size("seq")
    me = lax.axis_index("seq")
    barrier = pltpu.get_barrier_semaphore()
    for step in range(1, count):
        pl.semaphore_signal(
            barrier,
            inc=1,
            device_id={"seq": lax.rem(me + step, count)},
            device_id_type=pl.DeviceIdType.MESH,
        )
    pl.semaphore_wait(barrier, count - 1)
    copies = []
    for step in range(1, count):
        copy = pltpu.make_async_remote_copy(
            src_ref=src_ref,
            dst_ref=dst_ref.at[me],
            send_sem=send_sem.at[step - 1],
            recv_sem=recv_sem.at[me],
            device_id={"seq": jnp.minimum(me + step, count - 1)},
            device_id_type=pl.DeviceIdType.MESH,
        )
        copies.append(copy)

        @pl.when(me + step < count)
        def _():
            copy.start()

    for step, copy in zip(range(1, count), copies):

        @pl.when(me + step < count)
        def _():
            copy.wait_send()

    for step in range(1, count):
        source = jnp.maximum(me - step, 0)

        @pl.when(me - step >= 0)
        def _():
            pltpu.make_async_remote_copy(
                src_ref=src_ref,
                dst_ref=dst_ref.at[source],
                send_sem=send_sem.at[step - 1],
                recv_sem=recv_sem.at[source],
                device_id={"seq": source},
                device_id_type=pl.DeviceIdType.MESH,
            ).wait_recv()


def spread_over_seq(value):
    count = lax.axis_size("seq")
    return pl.pallas_call(
        spread_kernel,
        out_shape=jax.ShapeDtypeStruct((count,) + value.shape, value.dtype),
        in_specs=[pl.BlockSpec(memory_space=pl.ANY)],
        out_specs=pl.BlockSpec(memory_space=pl.ANY),
        scratch_shapes=[
            pltpu.SemaphoreType.DMA((count - 1,)),
            pltpu.SemaphoreType.DMA((count,)),
        ],
        compiler_params=pltpu.CompilerParams(collective_id=2, has_side_effects=True),
    )(value)


def recurrence_kernel(decay_ref, carried_ref, terms_ref, raised_ref, out_ref, inter_ref, state_ref):
    step = pl.program_id(0)
    chunk = terms_ref.shape[0]
    reach = terms_ref.shape[-1] // decay_ref.shape[-1]
    heads = raised_ref.shape[1]
    keys = raised_ref.shape[-1]

    @pl.when(step == 0)
    def _():
        state_ref[...] = jnp.zeros_like(state_ref)

    for page in range(chunk):
        kept = jnp.concatenate([carried_ref[page]] * reach, axis=-1) * state_ref[...]
        for head in range(heads):
            inter_ref[page, head] = jnp.dot(
                raised_ref[page, head],
                kept[head * keys : (head + 1) * keys],
                preferred_element_type=jnp.float32,
                precision=lax.Precision.HIGHEST,
            )
        state = jnp.concatenate([decay_ref[page]] * reach, axis=-1) * kept + terms_ref[page]
        state_ref[...] = state
        out_ref[page] = state


def page_recurrence(decay, carried, terms, raised, chunk=4):
    page_count, rows, width = terms.shape
    lanes = decay.shape[-1]
    heads, length = raised.shape[1], raised.shape[2]
    block = pl.BlockSpec((chunk, rows, width), lambda p: (p, 0, 0))
    flags = pl.BlockSpec((chunk, rows, lanes), lambda p: (p, 0, 0))
    return pl.pallas_call(
        recurrence_kernel,
        out_shape=(
            jax.ShapeDtypeStruct(terms.shape, terms.dtype),
            jax.ShapeDtypeStruct((page_count, heads, length, width), jnp.float32),
        ),
        grid=(page_count // chunk,),
        in_specs=[
            flags,
            flags,
            block,
            pl.BlockSpec((chunk,) + raised.shape[1:], lambda p: (p, 0, 0, 0)),
        ],
        out_specs=(block, pl.BlockSpec((chunk, heads, length, width), lambda p: (p, 0, 0, 0))),
        scratch_shapes=[pltpu.VMEM((rows, width), jnp.float32)],
    )(decay, carried, terms, raised)


def rms_scaled(values, scale_gain):
    values = values.astype(jnp.float32)
    return (
        values
        * lax.rsqrt(jnp.mean(values * values, axis=-1, keepdims=True) + EPSILON)
        * scale_gain.astype(jnp.float32)
    )


def page_segments(page_counts, starts, total_pages):
    position = jnp.arange(total_pages, dtype=jnp.int32)
    inside = (position[None, :] >= starts[:, None]) & (
        position[None, :] < starts[:, None] + page_counts[:, None]
    )
    labels = jnp.arange(1, page_counts.shape[0] + 1, dtype=jnp.int32)
    segment = jnp.sum(jnp.where(inside, labels[:, None], 0), axis=0) - 1
    earlier = jnp.concatenate([jnp.full((1,), -1, jnp.int32), segment[:-1]])
    return ((segment == earlier) & (segment >= 0)).astype(jnp.float32)


def short_conv(by_page, before, carried, conv_taps):
    kept_rows = before.astype(jnp.float32) * carried[:, None, None]
    widened = jnp.concatenate([kept_rows, by_page.astype(jnp.float32)], axis=1)
    tap_count = conv_taps.shape[0]
    length = by_page.shape[1]
    result = jnp.zeros(by_page.shape, jnp.float32)
    for offset in range(tap_count):
        result = (
            result
            + conv_taps[offset].astype(jnp.float32)
            * widened[:, tap_count - 1 - offset : tap_count - 1 - offset + length]
        )
    return result


def split_features(mixed_rows, key_width):
    query_rows = jax.nn.silu(mixed_rows[..., :key_width])
    key_rows = jax.nn.silu(mixed_rows[..., key_width : 2 * key_width]) * key_width ** (-0.5)
    value_matrix = mixed_rows[..., 2 * key_width :]
    return (
        query_rows.transpose(0, 2, 1, 3),
        key_rows.transpose(0, 2, 1, 3),
        value_matrix.transpose(0, 2, 1, 3),
    )


def page_block(query_rows, key_rows, value_matrix, decay_sum, carried):
    length = query_rows.shape[2]
    page_count = query_rows.shape[0]
    raised_rows = query_rows * jnp.exp(decay_sum)
    lowered = key_rows * jnp.exp(-decay_sum)
    scores = jnp.einsum("phik,phjk->phij", raised_rows, lowered, precision=TOP_PRECISION)
    rows_index = jnp.arange(length)
    causal = rows_index[:, None] >= rows_index[None, :]
    scores = jnp.where(causal[None, None], scores, 0.0)
    layer_output = jnp.einsum("phij,phjv->phiv", scores, value_matrix, precision=TOP_PRECISION)
    closing_sum = decay_sum[:, :, -1, :]
    weighted_rows = key_rows * jnp.exp(closing_sum[:, :, None, :] - decay_sum)
    page_terms = jnp.einsum(
        "phte,phtb->pheb", weighted_rows, value_matrix, precision=TOP_PRECISION
    )
    lanes = 128
    rows = closing_sum.shape[1] * closing_sum.shape[2]
    memories, inter_output = page_recurrence(
        jnp.broadcast_to(jnp.exp(closing_sum).reshape(page_count, rows, 1), (page_count, rows, lanes)),
        jnp.broadcast_to(carried[:, None, None], (page_count, rows, lanes)),
        page_terms.reshape(page_count, rows, page_terms.shape[-1]),
        raised_rows,
    )
    memories = memories.reshape(page_terms.shape)
    layer_output = layer_output + inter_output
    return memories[-1], layer_output, memories


def on_device(
    tokens,
    attention_gain,
    project_weight,
    conv_weight,
    decay_down,
    decay_up,
    decay_bias,
    output_gate,
    head_gain,
    output_weight,
    mixer_gain,
    gate_weight,
    up_weight,
    down_weight,
    prompt_pages,
    prompt_start,
):
    token_count = tokens.shape[0]
    page_count = token_count // PAGE
    local_heads = project_weight.shape[1] // CONVW
    rim_rows = KCONV - 1
    seq_index = lax.axis_index("seq")
    group_pages = page_count * lax.axis_size("seq")
    page_flags = page_segments(prompt_pages[0], prompt_start[0], group_pages)
    carried = lax.dynamic_slice_in_dim(page_flags, seq_index * page_count, page_count)
    normed = rms_scaled(tokens, attention_gain).astype(jnp.bfloat16)
    projected = jnp.dot(normed, project_weight, preferred_element_type=jnp.float32).astype(
        jnp.bfloat16
    )
    by_page = projected.reshape(page_count, PAGE, local_heads * CONVW)
    incoming = shifted(by_page[-1, PAGE - rim_rows :], "seq", 1)
    before = jnp.concatenate([incoming[None], by_page[:-1, PAGE - rim_rows :]], axis=0)
    mixed_rows = short_conv(by_page, before, carried, conv_weight).reshape(
        page_count, PAGE, local_heads, CONVW
    )
    query_rows, key_rows, value_matrix = split_features(mixed_rows, HK)
    lowrank = jnp.dot(normed, decay_down, preferred_element_type=jnp.float32).astype(jnp.bfloat16)
    decay_log = (
        jax.nn.log_sigmoid(
            jnp.dot(lowrank, decay_up, preferred_element_type=jnp.float32) + decay_bias
        )
        / 16.0
    )
    decay_log = decay_log.reshape(page_count, PAGE, local_heads, HK).transpose(0, 2, 1, 3)
    decay_sum = jnp.cumsum(decay_log, axis=2)
    local_memory, outputs, memories = page_block(
        query_rows, key_rows, value_matrix, decay_sum, carried
    )
    totals = decay_sum[:, :, -1, :]
    through = jnp.cumsum(totals, axis=0)
    alive_mask = jnp.cumprod(carried)
    block_decay = alive_mask[-1] * jnp.exp(through[-1])

    def compose(earlier, latter):
        return (earlier[0] * latter[0], latter[0][..., None] * earlier[1] + latter[1])

    prefix = prefix_2(
        (block_decay, local_memory),
        "seq",
        compose,
        (jnp.ones_like(block_decay), jnp.zeros_like(local_memory)),
    )
    incoming_state = prefix[1]
    before_sum = through - totals
    extent_factor = alive_mask[:, None, None, None] * jnp.exp(decay_sum + before_sum[:, :, None, :])
    outputs = outputs + jnp.einsum(
        "dlof,lfg->dlog", query_rows * extent_factor, incoming_state, precision=TOP_PRECISION
    )
    memories = (
        memories + (alive_mask[:, None, None] * jnp.exp(through))[..., None] * incoming_state[None]
    )
    attended = outputs.transpose(0, 2, 1, 3).reshape(token_count, local_heads, HV)
    normed_heads = rms_scaled(attended, head_gain)
    opening = jax.nn.silu(jnp.dot(normed, output_gate, preferred_element_type=jnp.float32)).reshape(
        token_count, local_heads, HV
    )
    gated_rows = (
        (normed_heads * opening).astype(jnp.bfloat16).reshape(token_count, local_heads * HV)
    )
    partial_value = jnp.dot(gated_rows, output_weight, preferred_element_type=jnp.float32)
    half_rows = token_count // lax.axis_size("hid")
    row_start = lax.axis_index("hid") * half_rows
    own_value = partial_value.astype(jnp.bfloat16)
    mixed_sum = own_value.astype(jnp.float32) + from_partner(own_value, token_count, 0).astype(
        jnp.float32
    )
    residual = (tokens.astype(jnp.float32) + mixed_sum).astype(jnp.bfloat16)
    feed_in = rms_scaled(residual, mixer_gain).astype(jnp.bfloat16)
    own_residual = lax.dynamic_slice_in_dim(residual, row_start, half_rows, 0)

    def widen(weight_rows):
        return jnp.dot(feed_in, weight_rows, preferred_element_type=jnp.float32)

    width = gate_weight.shape[1]
    both_part = widen(
        lax.all_gather(
            jnp.concatenate([gate_weight, up_weight], axis=1), "req", axis=0, tiled=True
        )
    )
    gate_part = both_part[:, :width]
    up_part = both_part[:, width:]
    hidden = lax.optimization_barrier((jax.nn.silu(gate_part) * up_part).astype(jnp.bfloat16))
    down_block = with_layout_constraint(down_weight.T, Layout((0, 1)))
    down_rows = lax.all_gather(down_block, "req", axis=0, tiled=True)
    partials = lax.dot_general(
        hidden, down_rows, (((1,), (1,)), ((), ())), preferred_element_type=jnp.float32
    )
    own_partials = partials.astype(jnp.bfloat16)
    feed_sum = lax.dynamic_slice_in_dim(own_partials, row_start, half_rows, 0).astype(
        jnp.float32
    ) + from_partner(own_partials, half_rows, 1).astype(jnp.float32)
    result = (own_residual.astype(jnp.float32) + feed_sum).astype(jnp.bfloat16)
    return (result, memories.astype(jnp.bfloat16), by_page[:, PAGE - rim_rows :])


def solution(mesh):
    return jax.shard_map(
        on_device,
        mesh=mesh,
        in_specs=(
            P(("req", "seq"), None),
            P(),
            P(None, "hid"),
            P(None, "hid"),
            P(),
            P(None, "hid"),
            P("hid"),
            P(None, "hid"),
            P(),
            P("hid", None),
            P(),
            P("req", "hid"),
            P("req", "hid"),
            P("hid", "req"),
            P("req", None),
            P("req", None),
        ),
        out_specs=(
            P(("req", "seq", "hid"), None),
            P(("req", "seq"), "hid", None, None),
            P(("req", "seq"), None, "hid"),
        ),
        check_vma=False,
    )
```

```python
import functools

import jax
import jax.numpy as jnp
from jax import lax
from jax.experimental.layout import Layout, with_layout_constraint
from jax.sharding import PartitionSpec as P
from jax.experimental import pallas as pl
from jax.experimental.pallas import tpu as pltpu

HK = 256
HV = 512
KCONV = 4
PAGE = 64
CONVW = 1024


EPSILON = 1e-06
TOP_PRECISION = lax.Precision.HIGH


def shifted(value, axis, steps):
    count = lax.axis_size(axis)
    first, last = (max(0, -steps), min(count, count - steps))
    return lax.ppermute(value, axis, [(source, source + steps) for source in range(first, last)])


def prefix_2(array, axis, join, neutral):
    place = lax.axis_index(axis)
    decay, memory = array
    width = memory.shape[-1]
    packed = jnp.concatenate(
        [memory.reshape(-1, width), jnp.pad(decay.reshape(1, -1), ((0, 0), (0, width - decay.size)))],
        axis=0,
    ).astype(jnp.bfloat16)
    received = spread_over_seq(packed)
    gathered = (
        received[:, -1, : decay.size].reshape((-1,) + decay.shape),
        received[:, :-1].reshape((-1,) + memory.shape),
    )
    state = jax.tree.map(lambda a, e: jnp.zeros_like(a) + jnp.asarray(e, a.dtype), array, neutral)

    def one(lap, state):
        return join(
            state,
            jax.tree.map(
                lambda a, own: lax.dynamic_index_in_dim(a, lap, 0, False).astype(own.dtype),
                gathered,
                array,
            ),
        )

    return lax.fori_loop(0, place, one, state)


def partner_kernel(rows, src_ref, dst_ref, send_sem, recv_sem):
    partner = 1 - lax.axis_index("hid")
    barrier = pltpu.get_barrier_semaphore()
    pl.semaphore_signal(
        barrier, inc=1, device_id={"hid": partner}, device_id_type=pl.DeviceIdType.MESH
    )
    pl.semaphore_wait(barrier, 1)
    start = pl.multiple_of(partner * rows, rows) if rows < src_ref.shape[0] else 0
    copy = pltpu.make_async_remote_copy(
        src_ref=src_ref.at[pl.ds(start, rows)],
        dst_ref=dst_ref,
        send_sem=send_sem,
        recv_sem=recv_sem,
        device_id={"hid": partner},
        device_id_type=pl.DeviceIdType.MESH,
    )
    copy.start()
    copy.wait()


def from_partner(value, rows, kernel_id):
    return pl.pallas_call(
        functools.partial(partner_kernel, rows),
        out_shape=jax.ShapeDtypeStruct((rows,) + value.shape[1:], value.dtype),
        in_specs=[pl.BlockSpec(memory_space=pl.ANY)],
        out_specs=pl.BlockSpec(memory_space=pl.ANY),
        scratch_shapes=[pltpu.SemaphoreType.DMA, pltpu.SemaphoreType.DMA],
        compiler_params=pltpu.CompilerParams(collective_id=kernel_id, has_side_effects=True),
    )(value)


def spread_kernel(src_ref, dst_ref, send_sem, recv_sem):
    count = lax.axis_size("seq")
    me = lax.axis_index("seq")
    barrier = pltpu.get_barrier_semaphore()
    for step in range(1, count):
        pl.semaphore_signal(
            barrier,
            inc=1,
            device_id={"seq": lax.rem(me + step, count)},
            device_id_type=pl.DeviceIdType.MESH,
        )
    pl.semaphore_wait(barrier, count - 1)
    copies = []
    for step in range(1, count):
        copy = pltpu.make_async_remote_copy(
            src_ref=src_ref,
            dst_ref=dst_ref.at[me],
            send_sem=send_sem.at[step - 1],
            recv_sem=recv_sem.at[me],
            device_id={"seq": jnp.minimum(me + step, count - 1)},
            device_id_type=pl.DeviceIdType.MESH,
        )
        copies.append(copy)

        @pl.when(me + step < count)
        def _():
            copy.start()

    for step, copy in zip(range(1, count), copies):

        @pl.when(me + step < count)
        def _():
            copy.wait_send()

    for step in range(1, count):
        source = jnp.maximum(me - step, 0)

        @pl.when(me - step >= 0)
        def _():
            pltpu.make_async_remote_copy(
                src_ref=src_ref,
                dst_ref=dst_ref.at[source],
                send_sem=send_sem.at[step - 1],
                recv_sem=recv_sem.at[source],
                device_id={"seq": source},
                device_id_type=pl.DeviceIdType.MESH,
            ).wait_recv()


def spread_over_seq(value):
    count = lax.axis_size("seq")
    return pl.pallas_call(
        spread_kernel,
        out_shape=jax.ShapeDtypeStruct((count,) + value.shape, value.dtype),
        in_specs=[pl.BlockSpec(memory_space=pl.ANY)],
        out_specs=pl.BlockSpec(memory_space=pl.ANY),
        scratch_shapes=[
            pltpu.SemaphoreType.DMA((count - 1,)),
            pltpu.SemaphoreType.DMA((count,)),
        ],
        compiler_params=pltpu.CompilerParams(collective_id=2, has_side_effects=True),
    )(value)


def recurrence_kernel(
    decay_ref, carried_ref, weighted_ref, value_ref, raised_ref, out_ref, inter_ref, state_ref
):
    step = pl.program_id(0)
    chunk = weighted_ref.shape[0]
    heads = raised_ref.shape[1]
    keys = raised_ref.shape[-1]
    reach = value_ref.shape[-1] // decay_ref.shape[-1]

    @pl.when(step == 0)
    def _():
        state_ref[...] = jnp.zeros_like(state_ref)

    for page in range(chunk):
        kept = jnp.concatenate([carried_ref[page]] * reach, axis=-1) * state_ref[...]
        fading = jnp.concatenate([decay_ref[page]] * reach, axis=-1)
        for head in range(heads):
            rows = slice(head * keys, (head + 1) * keys)
            inter_ref[page, head] = jnp.dot(
                raised_ref[page, head],
                kept[rows],
                preferred_element_type=jnp.float32,
                precision=lax.Precision.HIGHEST,
            )
            term = jnp.dot(
                weighted_ref[page, head],
                value_ref[page, head],
                preferred_element_type=jnp.float32,
                precision=lax.Precision.HIGHEST,
            )
            state = fading[rows] * kept[rows] + term
            state_ref[rows, :] = state
            out_ref[page, rows, :] = state


def page_recurrence(decay, carried, weighted, values, raised, chunk=4):
    page_count, heads, keys, length = weighted.shape
    width = values.shape[-1]
    rows = heads * keys
    lanes = decay.shape[-1]
    flags = pl.BlockSpec((chunk, rows, lanes), lambda p: (p, 0, 0))

    def pages(shape):
        return pl.BlockSpec((chunk,) + shape, lambda p: (p, 0, 0, 0))

    return pl.pallas_call(
        recurrence_kernel,
        out_shape=(
            jax.ShapeDtypeStruct((page_count, rows, width), jnp.float32),
            jax.ShapeDtypeStruct((page_count, heads, length, width), jnp.float32),
        ),
        grid=(page_count // chunk,),
        in_specs=[
            flags,
            flags,
            pages((heads, keys, length)),
            pages((heads, length, width)),
            pages((heads, length, keys)),
        ],
        out_specs=(
            pl.BlockSpec((chunk, rows, width), lambda p: (p, 0, 0)),
            pages((heads, length, width)),
        ),
        scratch_shapes=[pltpu.VMEM((rows, width), jnp.float32)],
    )(decay, carried, weighted, values, raised)


def rms_scaled(values, scale_gain):
    values = values.astype(jnp.float32)
    return (
        values
        * lax.rsqrt(jnp.mean(values * values, axis=-1, keepdims=True) + EPSILON)
        * scale_gain.astype(jnp.float32)
    )


def page_segments(page_counts, starts, total_pages):
    position = jnp.arange(total_pages, dtype=jnp.int32)
    inside = (position[None, :] >= starts[:, None]) & (
        position[None, :] < starts[:, None] + page_counts[:, None]
    )
    labels = jnp.arange(1, page_counts.shape[0] + 1, dtype=jnp.int32)
    segment = jnp.sum(jnp.where(inside, labels[:, None], 0), axis=0) - 1
    earlier = jnp.concatenate([jnp.full((1,), -1, jnp.int32), segment[:-1]])
    return ((segment == earlier) & (segment >= 0)).astype(jnp.float32)


def short_conv(by_page, before, carried, conv_taps):
    kept_rows = before.astype(jnp.float32) * carried[:, None, None]
    widened = jnp.concatenate([kept_rows, by_page.astype(jnp.float32)], axis=1)
    tap_count = conv_taps.shape[0]
    length = by_page.shape[1]
    result = jnp.zeros(by_page.shape, jnp.float32)
    for offset in range(tap_count):
        result = (
            result
            + conv_taps[offset].astype(jnp.float32)
            * widened[:, tap_count - 1 - offset : tap_count - 1 - offset + length]
        )
    return result


def split_features(mixed_rows, key_width):
    query_rows = jax.nn.silu(mixed_rows[..., :key_width])
    key_rows = jax.nn.silu(mixed_rows[..., key_width : 2 * key_width]) * key_width ** (-0.5)
    value_matrix = mixed_rows[..., 2 * key_width :]
    return (
        query_rows.transpose(0, 2, 1, 3),
        key_rows.transpose(0, 2, 1, 3),
        value_matrix.transpose(0, 2, 1, 3),
    )


def page_block(query_rows, key_rows, value_matrix, decay_sum, carried):
    length = query_rows.shape[2]
    page_count = query_rows.shape[0]
    raised_rows = query_rows * jnp.exp(decay_sum)
    lowered = key_rows * jnp.exp(-decay_sum)
    scores = jnp.einsum("phik,phjk->phij", raised_rows, lowered, precision=TOP_PRECISION)
    rows_index = jnp.arange(length)
    causal = rows_index[:, None] >= rows_index[None, :]
    scores = jnp.where(causal[None, None], scores, 0.0)
    layer_output = jnp.einsum("phij,phjv->phiv", scores, value_matrix, precision=TOP_PRECISION)
    closing_sum = decay_sum[:, :, -1, :]
    weighted_rows = key_rows * jnp.exp(closing_sum[:, :, None, :] - decay_sum)
    lanes = 128
    rows = closing_sum.shape[1] * closing_sum.shape[2]
    memories, inter_output = page_recurrence(
        jnp.broadcast_to(jnp.exp(closing_sum).reshape(page_count, rows, 1), (page_count, rows, lanes)),
        jnp.broadcast_to(carried[:, None, None], (page_count, rows, lanes)),
        weighted_rows.transpose(0, 1, 3, 2),
        value_matrix,
        raised_rows,
    )
    memories = memories.reshape(closing_sum.shape + (value_matrix.shape[-1],))
    layer_output = layer_output + inter_output
    return memories[-1], layer_output, memories


def on_device(
    tokens,
    attention_gain,
    project_weight,
    conv_weight,
    decay_down,
    decay_up,
    decay_bias,
    output_gate,
    head_gain,
    output_weight,
    mixer_gain,
    gate_weight,
    up_weight,
    down_weight,
    prompt_pages,
    prompt_start,
):
    token_count = tokens.shape[0]
    page_count = token_count // PAGE
    local_heads = project_weight.shape[1] // CONVW
    rim_rows = KCONV - 1
    seq_index = lax.axis_index("seq")
    group_pages = page_count * lax.axis_size("seq")
    page_flags = page_segments(prompt_pages[0], prompt_start[0], group_pages)
    carried = lax.dynamic_slice_in_dim(page_flags, seq_index * page_count, page_count)
    normed = rms_scaled(tokens, attention_gain).astype(jnp.bfloat16)
    projected = jnp.dot(normed, project_weight, preferred_element_type=jnp.float32).astype(
        jnp.bfloat16
    )
    by_page = projected.reshape(page_count, PAGE, local_heads * CONVW)
    incoming = shifted(by_page[-1, PAGE - rim_rows :], "seq", 1)
    before = jnp.concatenate([incoming[None], by_page[:-1, PAGE - rim_rows :]], axis=0)
    mixed_rows = short_conv(by_page, before, carried, conv_weight).reshape(
        page_count, PAGE, local_heads, CONVW
    )
    query_rows, key_rows, value_matrix = split_features(mixed_rows, HK)
    lowrank = jnp.dot(normed, decay_down, preferred_element_type=jnp.float32).astype(jnp.bfloat16)
    decay_log = (
        jax.nn.log_sigmoid(
            jnp.dot(lowrank, decay_up, preferred_element_type=jnp.float32) + decay_bias
        )
        / 16.0
    )
    decay_log = decay_log.reshape(page_count, PAGE, local_heads, HK).transpose(0, 2, 1, 3)
    decay_sum = jnp.cumsum(decay_log, axis=2)
    local_memory, outputs, memories = page_block(
        query_rows, key_rows, value_matrix, decay_sum, carried
    )
    totals = decay_sum[:, :, -1, :]
    through = jnp.cumsum(totals, axis=0)
    alive_mask = jnp.cumprod(carried)
    block_decay = alive_mask[-1] * jnp.exp(through[-1])

    def compose(earlier, latter):
        return (earlier[0] * latter[0], latter[0][..., None] * earlier[1] + latter[1])

    prefix = prefix_2(
        (block_decay, local_memory),
        "seq",
        compose,
        (jnp.ones_like(block_decay), jnp.zeros_like(local_memory)),
    )
    incoming_state = prefix[1]
    before_sum = through - totals
    extent_factor = alive_mask[:, None, None, None] * jnp.exp(decay_sum + before_sum[:, :, None, :])
    outputs = outputs + jnp.einsum(
        "dlof,lfg->dlog", query_rows * extent_factor, incoming_state, precision=TOP_PRECISION
    )
    memories = (
        memories + (alive_mask[:, None, None] * jnp.exp(through))[..., None] * incoming_state[None]
    )
    attended = outputs.transpose(0, 2, 1, 3).reshape(token_count, local_heads, HV)
    normed_heads = rms_scaled(attended, head_gain)
    opening = jax.nn.silu(jnp.dot(normed, output_gate, preferred_element_type=jnp.float32)).reshape(
        token_count, local_heads, HV
    )
    gated_rows = (
        (normed_heads * opening).astype(jnp.bfloat16).reshape(token_count, local_heads * HV)
    )
    partial_value = jnp.dot(gated_rows, output_weight, preferred_element_type=jnp.float32)
    half_rows = token_count // lax.axis_size("hid")
    row_start = lax.axis_index("hid") * half_rows
    own_value = partial_value.astype(jnp.bfloat16)
    mixed_sum = own_value.astype(jnp.float32) + from_partner(own_value, token_count, 0).astype(
        jnp.float32
    )
    residual = (tokens.astype(jnp.float32) + mixed_sum).astype(jnp.bfloat16)
    feed_in = rms_scaled(residual, mixer_gain).astype(jnp.bfloat16)
    own_residual = lax.dynamic_slice_in_dim(residual, row_start, half_rows, 0)

    def widen(weight_rows):
        return jnp.dot(feed_in, weight_rows, preferred_element_type=jnp.float32)

    width = gate_weight.shape[1]
    both_part = widen(
        lax.all_gather(
            jnp.concatenate([gate_weight, up_weight], axis=1), "req", axis=0, tiled=True
        )
    )
    gate_part = both_part[:, :width]
    up_part = both_part[:, width:]
    hidden = lax.optimization_barrier((jax.nn.silu(gate_part) * up_part).astype(jnp.bfloat16))
    down_block = with_layout_constraint(down_weight.T, Layout((0, 1)))
    down_rows = lax.all_gather(down_block, "req", axis=0, tiled=True)
    partials = lax.dot_general(
        hidden, down_rows, (((1,), (1,)), ((), ())), preferred_element_type=jnp.float32
    )
    own_partials = partials.astype(jnp.bfloat16)
    feed_sum = lax.dynamic_slice_in_dim(own_partials, row_start, half_rows, 0).astype(
        jnp.float32
    ) + from_partner(own_partials, half_rows, 1).astype(jnp.float32)
    result = (own_residual.astype(jnp.float32) + feed_sum).astype(jnp.bfloat16)
    return (result, memories.astype(jnp.bfloat16), by_page[:, PAGE - rim_rows :])


def solution(mesh):
    return jax.shard_map(
        on_device,
        mesh=mesh,
        in_specs=(
            P(("req", "seq"), None),
            P(),
            P(None, "hid"),
            P(None, "hid"),
            P(),
            P(None, "hid"),
            P("hid"),
            P(None, "hid"),
            P(),
            P("hid", None),
            P(),
            P("req", "hid"),
            P("req", "hid"),
            P("hid", "req"),
            P("req", None),
            P("req", None),
        ),
        out_specs=(
            P(("req", "seq", "hid"), None),
            P(("req", "seq"), "hid", None, None),
            P(("req", "seq"), None, "hid"),
        ),
        check_vma=False,
    )
```

```python
import functools

import jax
import jax.numpy as jnp
from jax import lax
from jax.experimental.layout import Layout, with_layout_constraint
from jax.sharding import PartitionSpec as P
from jax.experimental import pallas as pl
from jax.experimental.pallas import tpu as pltpu

HK = 256
HV = 512
KCONV = 4
PAGE = 64
CONVW = 1024


EPSILON = 1e-06
TOP_PRECISION = lax.Precision.DEFAULT


def shifted(value, axis, steps):
    count = lax.axis_size(axis)
    first, last = (max(0, -steps), min(count, count - steps))
    return lax.ppermute(value, axis, [(source, source + steps) for source in range(first, last)])


def prefix_2(array, axis, join, neutral):
    place = lax.axis_index(axis)
    decay, memory = array
    width = memory.shape[-1]
    packed = jnp.concatenate(
        [memory.reshape(-1, width), jnp.pad(decay.reshape(1, -1), ((0, 0), (0, width - decay.size)))],
        axis=0,
    ).astype(jnp.bfloat16)
    received = spread_over_seq(packed)
    gathered = (
        received[:, -1, : decay.size].reshape((-1,) + decay.shape),
        received[:, :-1].reshape((-1,) + memory.shape),
    )
    state = jax.tree.map(lambda a, e: jnp.zeros_like(a) + jnp.asarray(e, a.dtype), array, neutral)

    def one(lap, state):
        return join(
            state,
            jax.tree.map(
                lambda a, own: lax.dynamic_index_in_dim(a, lap, 0, False).astype(own.dtype),
                gathered,
                array,
            ),
        )

    return lax.fori_loop(0, place, one, state)


def partner_kernel(rows, src_ref, dst_ref, send_sem, recv_sem):
    partner = 1 - lax.axis_index("hid")
    barrier = pltpu.get_barrier_semaphore()
    pl.semaphore_signal(
        barrier, inc=1, device_id={"hid": partner}, device_id_type=pl.DeviceIdType.MESH
    )
    pl.semaphore_wait(barrier, 1)
    start = pl.multiple_of(partner * rows, rows) if rows < src_ref.shape[0] else 0
    copy = pltpu.make_async_remote_copy(
        src_ref=src_ref.at[pl.ds(start, rows)],
        dst_ref=dst_ref,
        send_sem=send_sem,
        recv_sem=recv_sem,
        device_id={"hid": partner},
        device_id_type=pl.DeviceIdType.MESH,
    )
    copy.start()
    copy.wait()


def from_partner(value, rows, kernel_id):
    return pl.pallas_call(
        functools.partial(partner_kernel, rows),
        out_shape=jax.ShapeDtypeStruct((rows,) + value.shape[1:], value.dtype),
        in_specs=[pl.BlockSpec(memory_space=pl.ANY)],
        out_specs=pl.BlockSpec(memory_space=pl.ANY),
        scratch_shapes=[pltpu.SemaphoreType.DMA, pltpu.SemaphoreType.DMA],
        compiler_params=pltpu.CompilerParams(collective_id=kernel_id, has_side_effects=True),
    )(value)


def spread_kernel(src_ref, dst_ref, send_sem, recv_sem):
    count = lax.axis_size("seq")
    me = lax.axis_index("seq")
    barrier = pltpu.get_barrier_semaphore()
    for step in range(1, count):
        pl.semaphore_signal(
            barrier,
            inc=1,
            device_id={"seq": lax.rem(me + step, count)},
            device_id_type=pl.DeviceIdType.MESH,
        )
    pl.semaphore_wait(barrier, count - 1)
    copies = []
    for step in range(1, count):
        copy = pltpu.make_async_remote_copy(
            src_ref=src_ref,
            dst_ref=dst_ref.at[me],
            send_sem=send_sem.at[step - 1],
            recv_sem=recv_sem.at[me],
            device_id={"seq": jnp.minimum(me + step, count - 1)},
            device_id_type=pl.DeviceIdType.MESH,
        )
        copies.append(copy)

        @pl.when(me + step < count)
        def _():
            copy.start()

    for step, copy in zip(range(1, count), copies):

        @pl.when(me + step < count)
        def _():
            copy.wait_send()

    for step in range(1, count):
        source = jnp.maximum(me - step, 0)

        @pl.when(me - step >= 0)
        def _():
            pltpu.make_async_remote_copy(
                src_ref=src_ref,
                dst_ref=dst_ref.at[source],
                send_sem=send_sem.at[step - 1],
                recv_sem=recv_sem.at[source],
                device_id={"seq": source},
                device_id_type=pl.DeviceIdType.MESH,
            ).wait_recv()


def spread_over_seq(value):
    count = lax.axis_size("seq")
    return pl.pallas_call(
        spread_kernel,
        out_shape=jax.ShapeDtypeStruct((count,) + value.shape, value.dtype),
        in_specs=[pl.BlockSpec(memory_space=pl.ANY)],
        out_specs=pl.BlockSpec(memory_space=pl.ANY),
        scratch_shapes=[
            pltpu.SemaphoreType.DMA((count - 1,)),
            pltpu.SemaphoreType.DMA((count,)),
        ],
        compiler_params=pltpu.CompilerParams(collective_id=2, has_side_effects=True),
    )(value)


def recurrence_kernel(decay_ref, carried_ref, terms_ref, raised_ref, out_ref, inter_ref, state_ref):
    step = pl.program_id(0)
    chunk = terms_ref.shape[0]
    reach = terms_ref.shape[-1] // decay_ref.shape[-1]
    heads = raised_ref.shape[1]
    keys = raised_ref.shape[-1]

    @pl.when(step == 0)
    def _():
        state_ref[...] = jnp.zeros_like(state_ref)

    for page in range(chunk):
        kept = jnp.concatenate([carried_ref[page]] * reach, axis=-1) * state_ref[...]
        for head in range(heads):
            inter_ref[page, head] = jnp.dot(
                raised_ref[page, head],
                kept[head * keys : (head + 1) * keys],
                preferred_element_type=jnp.float32,
                precision=lax.Precision.HIGHEST,
            )
        state = jnp.concatenate([decay_ref[page]] * reach, axis=-1) * kept + terms_ref[page]
        state_ref[...] = state
        out_ref[page] = state


def page_recurrence(decay, carried, terms, raised, chunk=4):
    page_count, rows, width = terms.shape
    lanes = decay.shape[-1]
    heads, length = raised.shape[1], raised.shape[2]
    block = pl.BlockSpec((chunk, rows, width), lambda p: (p, 0, 0))
    flags = pl.BlockSpec((chunk, rows, lanes), lambda p: (p, 0, 0))
    return pl.pallas_call(
        recurrence_kernel,
        out_shape=(
            jax.ShapeDtypeStruct(terms.shape, terms.dtype),
            jax.ShapeDtypeStruct((page_count, heads, length, width), jnp.float32),
        ),
        grid=(page_count // chunk,),
        in_specs=[
            flags,
            flags,
            block,
            pl.BlockSpec((chunk,) + raised.shape[1:], lambda p: (p, 0, 0, 0)),
        ],
        out_specs=(block, pl.BlockSpec((chunk, heads, length, width), lambda p: (p, 0, 0, 0))),
        scratch_shapes=[pltpu.VMEM((rows, width), jnp.float32)],
    )(decay, carried, terms, raised)


def rms_scaled(values, scale_gain):
    values = values.astype(jnp.float32)
    return (
        values
        * lax.rsqrt(jnp.mean(values * values, axis=-1, keepdims=True) + EPSILON)
        * scale_gain.astype(jnp.float32)
    )


def page_segments(page_counts, starts, total_pages):
    position = jnp.arange(total_pages, dtype=jnp.int32)
    inside = (position[None, :] >= starts[:, None]) & (
        position[None, :] < starts[:, None] + page_counts[:, None]
    )
    labels = jnp.arange(1, page_counts.shape[0] + 1, dtype=jnp.int32)
    segment = jnp.sum(jnp.where(inside, labels[:, None], 0), axis=0) - 1
    earlier = jnp.concatenate([jnp.full((1,), -1, jnp.int32), segment[:-1]])
    return ((segment == earlier) & (segment >= 0)).astype(jnp.float32)


def short_conv(by_page, before, carried, conv_taps):
    kept_rows = before.astype(jnp.float32) * carried[:, None, None]
    widened = jnp.concatenate([kept_rows, by_page.astype(jnp.float32)], axis=1)
    tap_count = conv_taps.shape[0]
    length = by_page.shape[1]
    result = jnp.zeros(by_page.shape, jnp.float32)
    for offset in range(tap_count):
        result = (
            result
            + conv_taps[offset].astype(jnp.float32)
            * widened[:, tap_count - 1 - offset : tap_count - 1 - offset + length]
        )
    return result


def split_features(mixed_rows, key_width):
    query_rows = jax.nn.silu(mixed_rows[..., :key_width])
    key_rows = jax.nn.silu(mixed_rows[..., key_width : 2 * key_width]) * key_width ** (-0.5)
    value_matrix = mixed_rows[..., 2 * key_width :]
    return (
        query_rows.transpose(0, 2, 1, 3),
        key_rows.transpose(0, 2, 1, 3),
        value_matrix.transpose(0, 2, 1, 3),
    )


def page_block(query_rows, key_rows, value_matrix, decay_sum, carried):
    length = query_rows.shape[2]
    page_count = query_rows.shape[0]
    raised_rows = query_rows * jnp.exp(decay_sum)
    lowered = key_rows * jnp.exp(-decay_sum)
    scores = jnp.einsum("phik,phjk->phij", raised_rows, lowered, precision=TOP_PRECISION)
    rows_index = jnp.arange(length)
    causal = rows_index[:, None] >= rows_index[None, :]
    scores = jnp.where(causal[None, None], scores, 0.0)
    layer_output = jnp.einsum("phij,phjv->phiv", scores, value_matrix, precision=TOP_PRECISION)
    closing_sum = decay_sum[:, :, -1, :]
    weighted_rows = key_rows * jnp.exp(closing_sum[:, :, None, :] - decay_sum)
    page_terms = jnp.einsum(
        "phte,phtb->pheb", weighted_rows, value_matrix, precision=TOP_PRECISION
    )
    lanes = 128
    rows = closing_sum.shape[1] * closing_sum.shape[2]
    memories, inter_output = page_recurrence(
        jnp.broadcast_to(jnp.exp(closing_sum).reshape(page_count, rows, 1), (page_count, rows, lanes)),
        jnp.broadcast_to(carried[:, None, None], (page_count, rows, lanes)),
        page_terms.reshape(page_count, rows, page_terms.shape[-1]),
        raised_rows,
    )
    memories = memories.reshape(page_terms.shape)
    layer_output = layer_output + inter_output
    return memories[-1], layer_output, memories


def on_device(
    tokens,
    attention_gain,
    project_weight,
    conv_weight,
    decay_down,
    decay_up,
    decay_bias,
    output_gate,
    head_gain,
    output_weight,
    mixer_gain,
    gate_weight,
    up_weight,
    down_weight,
    prompt_pages,
    prompt_start,
):
    token_count = tokens.shape[0]
    page_count = token_count // PAGE
    local_heads = project_weight.shape[1] // CONVW
    rim_rows = KCONV - 1
    seq_index = lax.axis_index("seq")
    group_pages = page_count * lax.axis_size("seq")
    page_flags = page_segments(prompt_pages[0], prompt_start[0], group_pages)
    carried = lax.dynamic_slice_in_dim(page_flags, seq_index * page_count, page_count)
    normed = rms_scaled(tokens, attention_gain).astype(jnp.bfloat16)
    projected = jnp.dot(normed, project_weight, preferred_element_type=jnp.float32).astype(
        jnp.bfloat16
    )
    by_page = projected.reshape(page_count, PAGE, local_heads * CONVW)
    incoming = shifted(by_page[-1, PAGE - rim_rows :], "seq", 1)
    before = jnp.concatenate([incoming[None], by_page[:-1, PAGE - rim_rows :]], axis=0)
    mixed_rows = short_conv(by_page, before, carried, conv_weight).reshape(
        page_count, PAGE, local_heads, CONVW
    )
    query_rows, key_rows, value_matrix = split_features(mixed_rows, HK)
    lowrank = jnp.dot(normed, decay_down, preferred_element_type=jnp.float32).astype(jnp.bfloat16)
    decay_log = (
        jax.nn.log_sigmoid(
            jnp.dot(lowrank, decay_up, preferred_element_type=jnp.float32) + decay_bias
        )
        / 16.0
    )
    decay_log = decay_log.reshape(page_count, PAGE, local_heads, HK).transpose(0, 2, 1, 3)
    decay_sum = jnp.cumsum(decay_log, axis=2)
    local_memory, outputs, memories = page_block(
        query_rows, key_rows, value_matrix, decay_sum, carried
    )
    totals = decay_sum[:, :, -1, :]
    through = jnp.cumsum(totals, axis=0)
    alive_mask = jnp.cumprod(carried)
    block_decay = alive_mask[-1] * jnp.exp(through[-1])

    def compose(earlier, latter):
        return (earlier[0] * latter[0], latter[0][..., None] * earlier[1] + latter[1])

    prefix = prefix_2(
        (block_decay, local_memory),
        "seq",
        compose,
        (jnp.ones_like(block_decay), jnp.zeros_like(local_memory)),
    )
    incoming_state = prefix[1]
    before_sum = through - totals
    extent_factor = alive_mask[:, None, None, None] * jnp.exp(decay_sum + before_sum[:, :, None, :])
    outputs = outputs + jnp.einsum(
        "dlof,lfg->dlog", query_rows * extent_factor, incoming_state, precision=TOP_PRECISION
    )
    memories = (
        memories + (alive_mask[:, None, None] * jnp.exp(through))[..., None] * incoming_state[None]
    )
    attended = outputs.transpose(0, 2, 1, 3).reshape(token_count, local_heads, HV)
    normed_heads = rms_scaled(attended, head_gain)
    opening = jax.nn.silu(jnp.dot(normed, output_gate, preferred_element_type=jnp.float32)).reshape(
        token_count, local_heads, HV
    )
    gated_rows = (
        (normed_heads * opening).astype(jnp.bfloat16).reshape(token_count, local_heads * HV)
    )
    partial_value = jnp.dot(gated_rows, output_weight, preferred_element_type=jnp.float32)
    half_rows = token_count // lax.axis_size("hid")
    row_start = lax.axis_index("hid") * half_rows
    own_value = partial_value.astype(jnp.bfloat16)
    mixed_sum = own_value.astype(jnp.float32) + from_partner(own_value, token_count, 0).astype(
        jnp.float32
    )
    residual = (tokens.astype(jnp.float32) + mixed_sum).astype(jnp.bfloat16)
    feed_in = rms_scaled(residual, mixer_gain).astype(jnp.bfloat16)
    own_residual = lax.dynamic_slice_in_dim(residual, row_start, half_rows, 0)

    def widen(weight_rows):
        return jnp.dot(feed_in, weight_rows, preferred_element_type=jnp.float32)

    width = gate_weight.shape[1]
    both_part = widen(
        lax.all_gather(
            jnp.concatenate([gate_weight, up_weight], axis=1), "req", axis=0, tiled=True
        )
    )
    gate_part = both_part[:, :width]
    up_part = both_part[:, width:]
    hidden = lax.optimization_barrier((jax.nn.silu(gate_part) * up_part).astype(jnp.bfloat16))
    down_block = with_layout_constraint(down_weight.T, Layout((0, 1)))
    down_rows = lax.all_gather(down_block, "req", axis=0, tiled=True)
    partials = lax.dot_general(
        hidden, down_rows, (((1,), (1,)), ((), ())), preferred_element_type=jnp.float32
    )
    own_partials = partials.astype(jnp.bfloat16)
    feed_sum = lax.dynamic_slice_in_dim(own_partials, row_start, half_rows, 0).astype(
        jnp.float32
    ) + from_partner(own_partials, half_rows, 1).astype(jnp.float32)
    result = (own_residual.astype(jnp.float32) + feed_sum).astype(jnp.bfloat16)
    return (result, memories.astype(jnp.bfloat16), by_page[:, PAGE - rim_rows :])


def solution(mesh):
    return jax.shard_map(
        on_device,
        mesh=mesh,
        in_specs=(
            P(("req", "seq"), None),
            P(),
            P(None, "hid"),
            P(None, "hid"),
            P(),
            P(None, "hid"),
            P("hid"),
            P(None, "hid"),
            P(),
            P("hid", None),
            P(),
            P("req", "hid"),
            P("req", "hid"),
            P("hid", "req"),
            P("req", None),
            P("req", None),
        ),
        out_specs=(
            P(("req", "seq", "hid"), None),
            P(("req", "seq"), "hid", None, None),
            P(("req", "seq"), None, "hid"),
        ),
        check_vma=False,
    )
```
